512 devices in a mesh: sx: 8 (over x, core), sy: 4 (over z_lo), wa: 16 (over y, z_hi).
Axes of the slice: x: 4, y: 8, z: 8 (z_hi: 2, z_lo: 4; z = z_hi * 4 + z_lo), core: 2. Of those that a mesh axis runs over, the one named last changes fastest.
Arguments:
- queries: bfloat16 [16, 16, 16, 16, 2048], P('wa', 'sx', 'sy'), may hold values from -6 to 6
- keys_values: bfloat16 [2, 16, 16, 16, 16, 2048], P(None, 'wa', 'sx', 'sy'), may hold values from -6 to 6
- out_weight: bfloat16 [2048, 2048], P('wa'), may hold values from -0.397747564 to 0.397747564
- gain: float32 [2048], replicated, may hold values from 0.5 to 2
- read_weight: float32 [2048, 2], replicated, may hold values from -0.125 to 0.125
- adjacency: int32 [16, 16, 16, 4], P('wa', 'sx', 'sy'), may hold values from 0 to 7, all different within a row
- boundary: int32 [16, 16, 16], P('wa', 'sx', 'sy'), may hold values 0 or 1
- cotangent: float32 [16, 16, 16, 16, 2], P('wa', 'sx', 'sy'), may hold values from -6 to 6
Outputs:
- prediction: float32 [16, 16, 16, 16, 2], P('wa', 'sx', 'sy')
- grad_queries: bfloat16 [16, 16, 16, 16, 2048], P('wa', 'sx', 'sy')
- grad_keys_values: bfloat16 [2, 16, 16, 16, 16, 2048], P(None, 'wa', 'sx', 'sy')
The draws below stay inside these ranges and needn't reach their ends.
Inputs may be any that keep to these rules, and one draw needn't show every extreme that they name: `adjacency`: the 4 entries of a block differ; entry e names code e if e < 4 and e + 1 otherwise, code c being the block at offset (c // 3 - 1, c % 3 - 1).
All inputs are finite; a program needn't handle non-finite values. No bound on the sum of `boundary` on one device may be relied on, other than what follows from the above.
Results may differ from the reference program's by a relative error of at most 0.0087.
Values may be sent and summed in bfloat16 or wider, within the bound.
No kernel may reach another device: no remote copies, remote signals or barrier semaphores. Data moves between devices by JAX's collectives and lax.ppermute only.
A program may use at most 128 MiB of HBM per device.

```python
import math
import jax
import jax.numpy as jnp
from jax import lax

D = 2048
HEADS = 16
BS = 16
NBR = 4
INNER = 2048
CASES = 16
BXT = 16
BYT = 16


def draw_queries(key, part):
    full_shape = (CASES, BXT, BYT, BS, INNER)
    background = jnp.clip(jax.random.normal(jax.random.fold_in(key, 1), full_shape, jnp.float32), -6.0, 6.0)
    return background.astype(jnp.bfloat16)


def draw_keys_values(key, part):
    full_shape = (2, CASES, BXT, BYT, BS, INNER)
    background = jnp.clip(jax.random.normal(jax.random.fold_in(key, 2), full_shape, jnp.float32), -6.0, 6.0)
    return background.astype(jnp.bfloat16)


def draw_out_weight(key, part):
    column_scale = jnp.exp(jax.random.uniform(jax.random.fold_in(key, 4), (D,), jnp.float32, -1.2039728, 1.0986123))
    background = jnp.clip(jax.random.normal(jax.random.fold_in(key, 3), (INNER, D), jnp.float32), -6.0, 6.0)
    return (background * column_scale * INNER ** (-0.5)).astype(jnp.bfloat16)


def with_ends(result, key, smallest, top_value):
    longest = result.shape.index(max(result.shape))
    spots = []
    for shift in (0, 1):
        where = [jax.random.randint(jax.random.fold_in(key, axis), (), 0, length) for axis, length in enumerate(result.shape)]
        where[longest] = (where[longest] + shift) % result.shape[longest]
        spots.append(tuple(where))
    return result.at[spots[0]].set(smallest).at[spots[1]].set(top_value)


def levels(own_key, dims, shards, least, top_value):
    def one(dim, blocks):
        draws = jax.random.uniform(jax.random.fold_in(jax.random.fold_in(own_key, 6), dim), (blocks,), jnp.float32, least / len(shards), top_value / len(shards))
        return jnp.repeat(jnp.exp(draws), dims[dim] // blocks).reshape((-1,) + (1,) * (len(dims) - dim - 1))

    level = one(*shards[0])
    for cut in shards[1:]:
        level = level * one(*cut)
    return level


def choose_distinct(own_key, rows, amount, top, lift):
    sequence = jax.random.permutation(jax.random.fold_in(own_key, 1), amount)
    pull = sequence
    for power in range(3):
        pull = pull * pull // amount
    pull = pull * lift // amount
    lots = jax.random.randint(jax.random.fold_in(own_key, 2), (rows, amount), 0, 4096) + pull
    holders = jax.random.permutation(jax.random.fold_in(own_key, 3), rows)[jnp.arange(amount) % rows]
    lots = jnp.where(jnp.arange(rows)[:, None] == holders[None, :], 1 << 14, lots)
    score = lots * amount + jnp.arange(amount)
    return lax.top_k(score.astype(jnp.int32), top)[1].astype(jnp.int32)


def normal_values(stream_key, dims, spread, reach, pieces=(), kind=jnp.bfloat16):
    level = levels(stream_key, dims, pieces, -0.22, 0.18) if pieces else 1.0
    array = jax.random.normal(stream_key, dims, jnp.float32) * spread * level
    return jnp.minimum(jnp.maximum(array, -reach), reach).astype(kind)


def setup_inputs(seed: int = 0) -> dict:
    arg_keys = jax.random.split(jax.random.key(seed), 9)
    return {
        "queries": draw_queries(jax.random.fold_in(arg_keys[8], 71), 0),
        "keys_values": draw_keys_values(jax.random.fold_in(arg_keys[8], 71), 0),
        "out_weight": draw_out_weight(jax.random.fold_in(arg_keys[8], 71), 0),
        "gain": jnp.clip(jnp.exp(jax.random.uniform(arg_keys[3], (D,), jnp.float32, math.log(0.5), math.log(2.0))), 0.5, 2.0),
        "read_weight": normal_values(arg_keys[4], (D, 2), D ** -0.5, 0.125, (), jnp.float32),
        "adjacency": choose_distinct(arg_keys[5], CASES * BXT * BYT, 8, NBR, 0).reshape((CASES, BXT, BYT, NBR)),
        "boundary": with_ends((jax.random.randint(arg_keys[6], (CASES, BXT, BYT), 0, 2) < 1).astype(jnp.int32), jax.random.fold_in(arg_keys[6], 1), 0, 1),
        "cotangent": normal_values(arg_keys[7], (CASES, BXT, BYT, BS, 2), 1.0, 6.0, ((0, 16), (1, 8), (2, 4)), jnp.float32),
    }


def code_allowed(adjacency, start_row, start_col, total_rows, total_cols):
    size_x = adjacency.shape[0]
    size_y = adjacency.shape[1]
    code_values = adjacency + (adjacency >= 4).astype(jnp.int32)
    code_list = jnp.arange(9, dtype=jnp.int32)
    listed = jnp.any(code_values[:, :, :, None] == code_list, axis=2) | (code_list == 4)
    target_x = start_row + jnp.arange(size_x, dtype=jnp.int32)[:, None, None] + code_list // 3 - 1
    target_y = start_col + jnp.arange(size_y, dtype=jnp.int32)[None, :, None] + code_list % 3 - 1
    inside = (target_x >= 0) & (target_x < total_rows) & (target_y >= 0) & (target_y < total_cols)
    return listed & inside

def gather_candidates(padded, size_x, size_y):
    return jnp.stack([padded[:, row_off:row_off + size_x, col_off:col_off + size_y] for row_off in range(3) for col_off in range(3)], axis=3)

def attend_forward(queries, candidates, allowed, heads):
    size_x, size_y, block_len, inner_dim = queries.shape
    head_dim = inner_dim // heads
    scaling = head_dim ** (-0.5)
    query_heads = queries.reshape(size_x, size_y, block_len, heads, head_dim)
    key_heads = candidates[0].reshape(size_x, size_y, 9, block_len, heads, head_dim)
    value_heads = candidates[1].reshape(size_x, size_y, 9, block_len, heads, head_dim)
    scores = jnp.einsum('xyihd,xycjhd->xyhicj', query_heads.astype(jnp.float32), key_heads.astype(jnp.float32)) * scaling
    masked = jnp.where(allowed[:, :, None, None, :, None], scores, -1e+30)
    row_max = lax.optimization_barrier(jnp.max(masked, axis=(4, 5), keepdims=True))
    exponent = jnp.exp(masked - row_max)
    softmax_full = exponent / lax.optimization_barrier(jnp.sum(exponent, axis=(4, 5), keepdims=True))
    softmax_half = softmax_full.astype(jnp.bfloat16)
    attended = jnp.einsum('xyhicj,xycjhd->xyihd', softmax_half.astype(jnp.float32), value_heads.astype(jnp.float32))
    attended = attended.reshape(size_x, size_y, block_len, inner_dim).astype(jnp.bfloat16)
    return (query_heads, key_heads, value_heads, softmax_full, softmax_half, attended)

def spread_back(grad_scores, softmax_half, query_heads, grad_heads):
    size_x, size_y, block_len, heads, head_dim = query_heads.shape
    accum = jnp.zeros((2, size_x + 2, size_y + 2, block_len, heads * head_dim), jnp.float32)
    for row_off in range(3):
        for col_off in range(3):
            code = 3 * row_off + col_off
            grad_keys = jnp.einsum('xyhij,xyihd->xyjhd', grad_scores[:, :, :, :, code].astype(jnp.float32), query_heads.astype(jnp.float32))
            grad_values = jnp.einsum('xyhij,xyihd->xyjhd', softmax_half[:, :, :, :, code].astype(jnp.float32), grad_heads.astype(jnp.float32))
            piece = jnp.stack([grad_keys, grad_values]).reshape(2, size_x, size_y, block_len, heads * head_dim)
            accum = accum + jnp.pad(piece, ((0, 0), (row_off, 2 - row_off), (col_off, 2 - col_off), (0, 0), (0, 0)))
    return accum

def attend_backward(query_heads, key_heads, value_heads, softmax_full, softmax_half, grad_att):
    scaling = query_heads.shape[-1] ** (-0.5)
    grad_heads = grad_att.reshape(query_heads.shape)
    grad_probs = jnp.einsum('xyihd,xycjhd->xyhicj', grad_heads.astype(jnp.float32), value_heads.astype(jnp.float32))
    inner_sum = lax.optimization_barrier(jnp.sum(softmax_full * grad_probs, axis=(4, 5), keepdims=True))
    grad_scores = (softmax_full * (grad_probs - inner_sum) * scaling).astype(jnp.bfloat16)
    grad_queries = jnp.einsum('xyhicj,xycjhd->xyihd', grad_scores.astype(jnp.float32), key_heads.astype(jnp.float32))
    grad_queries = grad_queries.reshape(grad_att.shape).astype(jnp.bfloat16)
    accum = spread_back(grad_scores, softmax_half, query_heads, grad_heads)
    return (grad_queries, accum)

def read_out(projected, gain, read_weight, token_mask, cotangent_rows):
    mean_square = lax.optimization_barrier(jnp.mean(projected * projected, axis=1, keepdims=True))
    inv_rms = lax.rsqrt(mean_square + 1e-05)
    normed = projected * inv_rms * gain
    prediction = jnp.dot(normed, read_weight, precision=lax.Precision.HIGHEST) * token_mask
    grad_normed = jnp.dot(cotangent_rows * token_mask, read_weight.T, precision=lax.Precision.HIGHEST)
    gained_grad = grad_normed * gain
    inner_mean = lax.optimization_barrier(jnp.mean(gained_grad * projected, axis=1, keepdims=True))
    grad_proj = (inv_rms * gained_grad - projected * inv_rms ** 3 * inner_mean).astype(jnp.bfloat16)
    return (prediction, grad_proj)

def one_case(case_items, out_weight, gain, read_weight):
    queries, keys_values, adjacency, boundary, cotangent = case_items
    padded = jnp.pad(keys_values, ((0, 0), (1, 1), (1, 1), (0, 0), (0, 0)))
    candidates = gather_candidates(padded, BXT, BYT)
    allowed = code_allowed(adjacency, 0, 0, BXT, BYT)
    query_heads, key_heads, value_heads, softmax_full, softmax_half, attended = attend_forward(queries, candidates, allowed, HEADS)
    token_count = BXT * BYT * BS
    projected = jnp.dot(attended.reshape(token_count, -1), out_weight, preferred_element_type=jnp.float32)
    token_mask = jnp.broadcast_to(boundary[:, :, None], (BXT, BYT, BS)).reshape(token_count, 1).astype(jnp.float32)
    prediction, grad_proj = read_out(projected, gain, read_weight, token_mask, cotangent.reshape(token_count, 2))
    grad_att = jnp.dot(grad_proj, out_weight.T, preferred_element_type=jnp.float32).astype(jnp.bfloat16)
    grad_queries, accum = attend_backward(query_heads, key_heads, value_heads, softmax_full, softmax_half, grad_att.reshape(BXT, BYT, BS, -1))
    grad_kv = accum[:, 1:-1, 1:-1].astype(jnp.bfloat16)
    return (prediction.reshape(BXT, BYT, BS, 2), grad_queries, grad_kv)

def reference(queries, keys_values, out_weight, gain, read_weight, adjacency, boundary, cotangent):
    per_case = jnp.moveaxis(keys_values, 1, 0)

    def run_case(case_items):
        return one_case(case_items, out_weight, gain, read_weight)
    prediction, grad_queries, grad_kv = lax.map(run_case, (queries, per_case, adjacency, boundary, cotangent))
    return (prediction, grad_queries, jnp.moveaxis(grad_kv, 0, 1))
```

```python
import jax
import jax.numpy as jnp
from jax import lax
from jax.experimental import pallas as pl
from jax.experimental.pallas import tpu as pltpu
from jax.sharding import PartitionSpec as P

HS = 128
BS = 16
BX = 2
BY = 4
TOK = BX * BY * BS
GROUP = 4
VMEM_LIMIT = 60 * 1024 * 1024

LOCAL = [(x, y) for x in range(BX) for y in range(BY)]
XLOW = [(-1, y) for y in range(BY)]
XHIGH = [(BX, y) for y in range(BY)]
YLOW = [(x, -1) for x in range(BX)]
YHIGH = [(x, BY) for x in range(BX)]
CLOW = [(-1, -1), (-1, BY)]
CHIGH = [(BX, -1), (BX, BY)]
PIECES = [LOCAL, XLOW, XHIGH, YLOW, YHIGH, CLOW, CHIGH]
KEY_BLOCKS = [block for piece in PIECES for block in piece]
KEYS = len(KEY_BLOCKS) * BS


def shift(value, axis, step):
    count = lax.axis_size(axis)
    pairs = [(i, i + step) for i in range(count) if 0 <= i + step < count]
    return lax.ppermute(value, axis, pairs)


def dot(a, b, dims):
    return lax.dot_general(a, b, (dims, ((), ())), preferred_element_type=jnp.float32)


def piece_rows(refs, which, lanes):
    parts = []
    for ref in refs:
        blocks = ref[which, :, :, :, lanes]
        parts.append(blocks.reshape(-1, HS))
    return jnp.concatenate(parts, axis=0)


def allowed_mask(adj_ref, pos_ref):
    lane = lax.broadcasted_iota(jnp.int32, (1, TOK), 1)
    block = lane // BS
    bx = block // BY
    by = block % BY
    entries = []
    for e in range(4):
        vec = jnp.zeros((1, TOK), jnp.int32)
        for b in range(BX * BY):
            vec = jnp.where(block == b, adj_ref[0, b // BY, b % BY, e], vec)
        entries.append(vec)
    rows = []
    for kx, ky in KEY_BLOCKS:
        dx = kx - bx
        dy = ky - by
        near = (jnp.abs(dx) <= 1) & (jnp.abs(dy) <= 1)
        code = 3 * (dx + 1) + dy + 1
        entry = code - (code > 4).astype(jnp.int32)
        listed = code == 4
        for vec in entries:
            listed = listed | ((vec == entry) & (code != 4))
        gx = pos_ref[0] + kx
        gy = pos_ref[1] + ky
        inside = (gx >= 0) & (gx < pos_ref[2]) & (gy >= 0) & (gy < pos_ref[3])
        flag = jnp.where(near & listed, 1.0, 0.0) * jnp.where(inside, 1.0, 0.0)
        rows.append(jnp.broadcast_to(flag, (BS, TOK)))
    return jnp.concatenate(rows, axis=0)


def forward_kernel(adj_ref, pos_ref, q_ref, *rest):
    kv_refs = rest[: len(PIECES)]
    att_ref, prob_ref, mask_ref = rest[len(PIECES) :]

    @pl.when(pl.program_id(0) == 0)
    def _():
        mask_ref[...] = allowed_mask(adj_ref, pos_ref)

    for h in range(GROUP):
        lanes = slice(h * HS, (h + 1) * HS)
        query = q_ref[0, :, :, :, lanes].reshape(TOK, HS)
        keys = piece_rows(kv_refs, 0, lanes)
        values = piece_rows(kv_refs, 1, lanes)
        scores = dot(keys, query, ((1,), (1,))) * (HS**-0.5)
        masked = jnp.where(mask_ref[...] > 0.5, scores, -1e30)
        exponent = jnp.exp(masked - jnp.max(masked, axis=0, keepdims=True))
        prob = exponent / jnp.sum(exponent, axis=0, keepdims=True)
        prob_ref[h] = prob
        att = dot(prob.astype(jnp.bfloat16), values, ((0,), (0,)))
        att_ref[:, lanes] = att.astype(jnp.bfloat16)


def forward(adjacency, position, queries, pieces):
    inner = queries.shape[-1]
    width = GROUP * HS
    smem = pl.BlockSpec(memory_space=pltpu.SMEM)
    specs = [
        pl.BlockSpec(p.shape[:-1] + (width,), lambda g: (0, 0, 0, 0, g))
        for p in pieces
    ]
    return pl.pallas_call(
        forward_kernel,
        grid=(inner // width,),
        in_specs=[smem, smem, pl.BlockSpec(queries.shape[:-1] + (width,), lambda g: (0, 0, 0, 0, g))] + specs,
        out_specs=[
            pl.BlockSpec((TOK, width), lambda g: (0, g)),
            pl.BlockSpec((GROUP, KEYS, TOK), lambda g: (g, 0, 0)),
        ],
        out_shape=[
            jax.ShapeDtypeStruct((TOK, inner), jnp.bfloat16),
            jax.ShapeDtypeStruct((inner // HS, KEYS, TOK), jnp.float32),
        ],
        scratch_shapes=[pltpu.VMEM((KEYS, TOK), jnp.float32)],
        compiler_params=pltpu.CompilerParams(vmem_limit_bytes=VMEM_LIMIT),
        name="attend",
    )(adjacency, position, queries, *pieces)


def project_kernel(bound_ref, pos_ref, att_ref, own_hbm, other_hbm, gain_ref, read_ref, cot_ref, pred_ref, ga_ref, w_ref, proj_ref, gp_ref, sems):
    slabs = w_ref.shape[0]
    cols = w_ref.shape[2]
    core = pos_ref[4]
    copies = [
        pltpu.make_async_copy(own_hbm, w_ref.at[core], sems.at[0]),
        pltpu.make_async_copy(other_hbm, w_ref.at[1 - core], sems.at[1]),
    ]
    for copy in copies:
        copy.start()
    for copy in copies:
        copy.wait()
    att = att_ref[...]
    for s in range(slabs):
        proj_ref[:, s * cols : (s + 1) * cols] = dot(att, w_ref[s], ((1,), (0,)))
    inner = proj_ref.shape[1]
    for half in range(TOK // 32):
        rows = slice(half * 32, (half + 1) * 32)
        x = half * 2 // BY
        y = half * 2 % BY
        proj = proj_ref[rows, :]
        gain = gain_ref[...]
        flag = jnp.where(
            lax.broadcasted_iota(jnp.int32, (32, 1), 0) < BS, bound_ref[0, x, y], bound_ref[0, x, y + 1]
        ).astype(jnp.float32)
        cot = jnp.concatenate([cot_ref[0, x, y], cot_ref[0, x, y + 1]], axis=0) * flag
        inv_rms = lax.rsqrt(jnp.sum(proj * proj, axis=1, keepdims=True) * (1.0 / inner) + 1e-05)
        normed = proj * inv_rms * gain
        pred0 = jnp.sum(normed * read_ref[0:1, :], axis=1, keepdims=True) * flag
        pred1 = jnp.sum(normed * read_ref[1:2, :], axis=1, keepdims=True) * flag
        pred = jnp.where(lax.broadcasted_iota(jnp.int32, (32, 2), 1) == 0, pred0, pred1)
        pred_ref[0, x, y] = pred[:BS]
        pred_ref[0, x, y + 1] = pred[BS:]
        gained = (cot[:, 0:1] * read_ref[0:1, :] + cot[:, 1:2] * read_ref[1:2, :]) * gain
        inner_mean = jnp.sum(gained * proj, axis=1, keepdims=True) * (1.0 / inner)
        gp_ref[rows, :] = (inv_rms * gained - proj * (inv_rms * inv_rms * inv_rms * inner_mean)).astype(jnp.bfloat16)
    chunk = 512
    for r in range(inner // chunk):
        total = None
        for s in range(slabs):
            part = dot(gp_ref[:, s * cols : (s + 1) * cols], w_ref[s, r * chunk : (r + 1) * chunk, :], ((1,), (1,)))
            total = part if total is None else total + part
        ga_ref[:, r * chunk : (r + 1) * chunk] = total.astype(jnp.bfloat16)


def project(boundary, position, att, own_rows, other_rows, gain, read_rows, cotangent):
    vmem = pl.BlockSpec(memory_space=pltpu.VMEM)
    return pl.pallas_call(
        project_kernel,
        in_specs=[
            pl.BlockSpec(memory_space=pltpu.SMEM),
            pl.BlockSpec(memory_space=pltpu.SMEM),
            vmem,
            pl.BlockSpec(memory_space=pl.ANY),
            pl.BlockSpec(memory_space=pl.ANY),
            vmem,
            vmem,
            vmem,
        ],
        out_specs=[vmem, vmem],
        out_shape=[
            jax.ShapeDtypeStruct(cotangent.shape, jnp.float32),
            jax.ShapeDtypeStruct(att.shape, jnp.bfloat16),
        ],
        scratch_shapes=[
            pltpu.VMEM((2,) + own_rows.shape, jnp.bfloat16),
            pltpu.VMEM(att.shape, jnp.float32),
            pltpu.VMEM(att.shape, jnp.bfloat16),
            pltpu.SemaphoreType.DMA((2,)),
        ],
        compiler_params=pltpu.CompilerParams(vmem_limit_bytes=VMEM_LIMIT),
        name="project",
    )(boundary, position, att, own_rows, other_rows, gain, read_rows, cotangent)


def backward_kernel(q_ref, ga_ref, prob_ref, *rest):
    count = len(PIECES)
    kv_refs = rest[:count]
    gq_ref = rest[count]
    gkv_refs = rest[count + 1 :]
    for h in range(GROUP):
        lanes = slice(h * HS, (h + 1) * HS)
        query = q_ref[0, :, :, :, lanes].reshape(TOK, HS)
        keys = piece_rows(kv_refs, 0, lanes)
        values = piece_rows(kv_refs, 1, lanes)
        grad_att = ga_ref[:, lanes]
        prob = prob_ref[h]
        grad_prob = dot(values, grad_att, ((1,), (1,)))
        inner_sum = jnp.sum(prob * grad_prob, axis=0, keepdims=True)
        grad_scores = (prob * (grad_prob - inner_sum) * (HS**-0.5)).astype(jnp.bfloat16)
        grad_query = dot(grad_scores, keys, ((0,), (0,)))
        gq_ref[0, :, :, :, lanes] = grad_query.reshape(BX, BY, BS, HS).astype(gq_ref.dtype)
        grads = (dot(grad_scores, query, ((1,), (0,))), dot(prob.astype(jnp.bfloat16), grad_att, ((1,), (0,))))
        for which, grad in enumerate(grads):
            start = 0
            for ref in gkv_refs:
                shape = ref.shape[1:4]
                rows = shape[0] * shape[1] * shape[2]
                ref[which, :, :, :, lanes] = grad[start : start + rows].reshape(shape + (HS,)).astype(ref.dtype)
                start += rows


def backward(queries, grad_att, prob, pieces):
    inner = queries.shape[-1]
    width = GROUP * HS

    def wide(shape):
        return pl.BlockSpec(tuple(shape[:-1]) + (width,), lambda g: (0,) * (len(shape) - 1) + (g,))

    shapes = [p.shape for p in pieces]
    return pl.pallas_call(
        backward_kernel,
        grid=(inner // width,),
        in_specs=[wide(queries.shape), wide(grad_att.shape), pl.BlockSpec((GROUP, KEYS, TOK), lambda g: (g, 0, 0))]
        + [wide(s) for s in shapes],
        out_specs=[wide(queries.shape)] + [wide(s) for s in shapes],
        out_shape=[jax.ShapeDtypeStruct(queries.shape, jnp.bfloat16)]
        + [jax.ShapeDtypeStruct(s, jnp.float32 if i == 0 else jnp.bfloat16) for i, s in enumerate(shapes)],
        compiler_params=pltpu.CompilerParams(vmem_limit_bytes=VMEM_LIMIT),
        name="attend_back",
    )(queries, grad_att, prob, *pieces)


def finish_kernel(own_ref, xlow_ref, xhigh_ref, ylow_ref, yhigh_ref, out_ref):
    f32 = jnp.float32
    for which in range(2):
        for x in range(BX):
            for y in range(BY):
                total = own_ref[which, x, y]
                if x == 0:
                    total = total + xlow_ref[which, 0, y].astype(f32)
                if x == BX - 1:
                    total = total + xhigh_ref[which, 0, y].astype(f32)
                if y == 0:
                    total = total + ylow_ref[which, x, 0].astype(f32)
                if y == BY - 1:
                    total = total + yhigh_ref[which, x, 0].astype(f32)
                out_ref[which, x, y] = total.astype(out_ref.dtype)


def finish(own, xlow, xhigh, ylow, yhigh):
    inner = own.shape[-1]
    width = inner // 4

    def wide(shape):
        return pl.BlockSpec(tuple(shape[:-1]) + (width,), lambda g: (0, 0, 0, 0, g))

    args = (own, xlow, xhigh, ylow, yhigh)
    return pl.pallas_call(
        finish_kernel,
        grid=(inner // width,),
        in_specs=[wide(a.shape) for a in args],
        out_specs=wide(own.shape),
        out_shape=jax.ShapeDtypeStruct(own.shape, jnp.bfloat16),
        compiler_params=pltpu.CompilerParams(vmem_limit_bytes=VMEM_LIMIT),
        name="finish",
    )(*args)


def gather_weight(out_weight):
    inner = out_weight.shape[1]
    cols = inner // 2
    n_wa = lax.axis_size("wa")
    n_sy = lax.axis_size("sy")
    half = lax.axis_index("wa") % 2
    slab = lax.dynamic_slice_in_dim(out_weight, lax.axis_index("sx") % 2 * cols, cols, axis=1)
    mirror = [(l * n_wa + w, (n_sy - 1 - l) * n_wa + (w ^ 1)) for l in range(n_sy) for w in range(n_wa)]
    other = lax.ppermute(slab, ("sy", "wa"), mirror)
    pair = jnp.where(half == 0, jnp.stack([slab, other]), jnp.stack([other, slab]))
    groups = [list(range(h, n_wa, 2)) for h in range(2)]
    rows = lax.all_gather(pair, "wa", axis=0, axis_index_groups=groups)
    return rows.reshape(-1, cols)


def body(queries, keys_values, out_weight, gain, read_weight, adjacency, boundary, cotangent):
    size_x, size_y = queries.shape[1:3]
    kv = keys_values[:, 0]
    rows = gather_weight(out_weight)
    ylow = shift(kv[:, :, size_y - 1 :], "sy", 1)
    yhigh = shift(kv[:, :, :1], "sy", -1)
    xlow = shift(kv[:, size_x - 1 :], "sx", 1)
    xhigh = shift(kv[:, :1], "sx", -1)
    clow = shift(jnp.concatenate([ylow[:, size_x - 1 :], yhigh[:, size_x - 1 :]], axis=2), "sx", 1)
    chigh = shift(jnp.concatenate([ylow[:, :1], yhigh[:, :1]], axis=2), "sx", -1)
    pieces = (kv, xlow, xhigh, ylow, yhigh, clow, chigh)
    position = jnp.stack(
        [
            lax.axis_index("sx") * size_x,
            lax.axis_index("sy") * size_y,
            jnp.int32(size_x * lax.axis_size("sx")),
            jnp.int32(size_y * lax.axis_size("sy")),
            lax.axis_index("sx") % 2,
        ]
    ).astype(jnp.int32)
    att, prob = forward(adjacency, position, queries, pieces)
    rows, att = lax.optimization_barrier((rows, att))
    other_rows = lax.ppermute(rows, "sx", [(i, i ^ 1) for i in range(lax.axis_size("sx"))])
    prediction, grad_att = project(boundary, position, att, rows, other_rows, gain[None], read_weight.T, cotangent)
    grad_queries, own, gxlow, gxhigh, gylow, gyhigh, gclow, gchigh = backward(queries, grad_att, prob, pieces)
    to_high = shift(jnp.concatenate([gxhigh, gchigh], axis=2), "sx", 1)
    to_low = shift(jnp.concatenate([gxlow, gclow], axis=2), "sx", -1)
    f32 = jnp.float32

    def side(rim, y):
        first = rim[:, :1].astype(f32) + to_high[:, :, size_y + y : size_y + y + 1].astype(f32)
        last = rim[:, 1:].astype(f32) + to_low[:, :, size_y + y : size_y + y + 1].astype(f32)
        return jnp.concatenate([first, last], axis=1).astype(jnp.bfloat16)

    from_low = shift(side(gyhigh, 1), "sy", 1)
    from_high = shift(side(gylow, 0), "sy", -1)
    grad_kv = finish(own, to_high[:, :, :size_y], to_low[:, :, :size_y], from_low, from_high)
    return (prediction, grad_queries, grad_kv[:, None])


def solution(mesh):
    return jax.shard_map(
        body,
        mesh=mesh,
        in_specs=(
            P("wa", "sx", "sy", None, None),
            P(None, "wa", "sx", "sy", None, None),
            P("wa", None),
            P(),
            P(),
            P("wa", "sx", "sy", None),
            P("wa", "sx", "sy"),
            P("wa", "sx", "sy", None, None),
        ),
        out_specs=(
            P("wa", "sx", "sy", None, None),
            P("wa", "sx", "sy", None, None),
            P(None, "wa", "sx", "sy", None, None),
        ),
        check_vma=False,
    )
```

```python
import jax
import jax.numpy as jnp
from jax import lax
from jax.experimental import pallas as pl
from jax.experimental.pallas import tpu as pltpu
from jax.sharding import PartitionSpec as P

HS = 128
BS = 16
BX = 2
BY = 4
TOK = BX * BY * BS
GROUP = 4
VMEM_LIMIT = 60 * 1024 * 1024
SMALL_LIMIT = 24 * 1024 * 1024

LOCAL = [(x, y) for x in range(BX) for y in range(BY)]
XLOW = [(-1, y) for y in range(BY)]
XHIGH = [(BX, y) for y in range(BY)]
YLOW = [(x, -1) for x in range(BX)]
YHIGH = [(x, BY) for x in range(BX)]
CLOW = [(-1, -1), (-1, BY)]
CHIGH = [(BX, -1), (BX, BY)]
PIECES = [LOCAL, XLOW, CLOW, XHIGH, CHIGH, YLOW, YHIGH]
KEY_BLOCKS = [block for piece in PIECES for block in piece]
KEYS = len(KEY_BLOCKS) * BS


def shift(value, axis, step):
    count = lax.axis_size(axis)
    pairs = [(i, i + step) for i in range(count) if 0 <= i + step < count]
    return lax.ppermute(value, axis, pairs)


def dot(a, b, dims):
    return lax.dot_general(a, b, (dims, ((), ())), preferred_element_type=jnp.float32)


def piece_rows(refs, which, lanes):
    parts = []
    for ref in refs:
        blocks = ref[which, :, :, :, lanes]
        parts.append(blocks.reshape(-1, HS))
    return jnp.concatenate(parts, axis=0)


def allowed_mask(adj_ref, pos_ref):
    lane = lax.broadcasted_iota(jnp.int32, (1, TOK), 1)
    block = lane // BS
    bx = block // BY
    by = block % BY
    entries = []
    for e in range(4):
        vec = jnp.zeros((1, TOK), jnp.int32)
        for b in range(BX * BY):
            vec = jnp.where(block == b, adj_ref[0, b // BY, b % BY, e], vec)
        entries.append(vec)
    rows = []
    for kx, ky in KEY_BLOCKS:
        dx = kx - bx
        dy = ky - by
        near = (jnp.abs(dx) <= 1) & (jnp.abs(dy) <= 1)
        code = 3 * (dx + 1) + dy + 1
        entry = code - (code > 4).astype(jnp.int32)
        listed = code == 4
        for vec in entries:
            listed = listed | ((vec == entry) & (code != 4))
        gx = pos_ref[0] + kx
        gy = pos_ref[1] + ky
        inside = (gx >= 0) & (gx < pos_ref[2]) & (gy >= 0) & (gy < pos_ref[3])
        flag = jnp.where(near & listed, 1.0, 0.0) * jnp.where(inside, 1.0, 0.0)
        rows.append(jnp.broadcast_to(flag, (BS, TOK)))
    return jnp.concatenate(rows, axis=0)


def forward_kernel(adj_ref, pos_ref, q_ref, *rest):
    kv_refs = rest[: len(PIECES)]
    att_ref, prob_ref, mask_ref = rest[len(PIECES) :]

    @pl.when(pl.program_id(0) == 0)
    def _():
        mask_ref[...] = allowed_mask(adj_ref, pos_ref)

    for h in range(GROUP):
        lanes = slice(h * HS, (h + 1) * HS)
        query = q_ref[0, :, :, :, lanes].reshape(TOK, HS)
        keys = piece_rows(kv_refs, 0, lanes)
        values = piece_rows(kv_refs, 1, lanes)
        scores = dot(keys, query, ((1,), (1,))) * (HS**-0.5)
        masked = jnp.where(mask_ref[...] > 0.5, scores, -1e30)
        exponent = jnp.exp(masked - jnp.max(masked, axis=0, keepdims=True))
        prob = exponent / jnp.sum(exponent, axis=0, keepdims=True)
        prob_ref[h] = prob
        att = dot(prob.astype(jnp.bfloat16), values, ((0,), (0,)))
        att_ref[:, lanes] = att.astype(jnp.bfloat16)


def forward(adjacency, position, queries, pieces):
    inner = queries.shape[-1]
    width = GROUP * HS
    smem = pl.BlockSpec(memory_space=pltpu.SMEM)
    specs = [
        pl.BlockSpec(p.shape[:-1] + (width,), lambda g: (0, 0, 0, 0, g))
        for p in pieces
    ]
    return pl.pallas_call(
        forward_kernel,
        grid=(inner // width,),
        in_specs=[smem, smem, pl.BlockSpec(queries.shape[:-1] + (width,), lambda g: (0, 0, 0, 0, g))] + specs,
        out_specs=[
            pl.BlockSpec((TOK, width), lambda g: (0, g)),
            pl.BlockSpec((GROUP, KEYS, TOK), lambda g: (g, 0, 0)),
        ],
        out_shape=[
            jax.ShapeDtypeStruct((TOK, inner), jnp.bfloat16),
            jax.ShapeDtypeStruct((inner // HS, KEYS, TOK), jnp.float32),
        ],
        scratch_shapes=[pltpu.VMEM((KEYS, TOK), jnp.float32)],
        compiler_params=pltpu.CompilerParams(vmem_limit_bytes=VMEM_LIMIT),
        name="attend",
    )(adjacency, position, queries, *pieces)


def head_lanes(index):
    return pl.ds(pl.multiple_of(index * HS, HS), HS)


def far_step(k):
    return (0, 1, 7, 2)[k // 2] + 4 * (k % 2)


def project_kernel(
    bound_ref, pos_ref, att_ref, near_hbm, near_swap_hbm, far_hbm, far_swap_hbm, gain_ref, read_ref, cot_ref,
    pred_ref, ga_ref, near_ref, far_ref, own_att_ref, far_att_ref, proj_ref, gp_ref, sems,
):
    copies = [
        pltpu.make_async_copy(near_hbm, near_ref.at[0], sems.at[0]),
        pltpu.make_async_copy(near_swap_hbm, near_ref.at[1], sems.at[1]),
        pltpu.make_async_copy(far_hbm, far_ref.at[0], sems.at[2]),
        pltpu.make_async_copy(far_swap_hbm, far_ref.at[1], sems.at[3]),
    ]
    for copy in copies:
        copy.start()
    core = pos_ref[4]
    chip = pos_ref[5]
    ring = pos_ref[6]
    half = pos_ref[7]
    n_ring, _, cols = near_ref.shape[1:]
    n_chip = far_ref.shape[1]
    part = cols // n_chip

    def near_head(k):
        return head_lanes(k * 2 + half)

    def far_head(k):
        return head_lanes(lax.rem(ring + 2 * n_ring - far_step(k), n_ring) * 2 + 1 - half)

    def near_cols(side):
        return pl.ds(pl.multiple_of((core if side == 0 else 1 - core) * cols, cols), cols)

    def far_cols(side, j):
        start = (core if side == 0 else 1 - core) * cols + lax.rem(chip + n_chip - j, n_chip) * part
        return pl.ds(pl.multiple_of(start, part), part)

    for k in range(n_ring):
        own_att_ref[:, k * HS : (k + 1) * HS] = att_ref[:, near_head(k)]
        far_att_ref[:, k * HS : (k + 1) * HS] = att_ref[:, far_head(k)]
    rows = n_ring * HS
    for side in range(2):
        copies[side].wait()
        proj_ref[:, near_cols(side)] = dot(own_att_ref[...], near_ref[side].reshape(rows, cols), ((1,), (0,)))
    for side in range(2):
        copies[2 + side].wait()
        for j in range(n_chip):
            lanes = far_cols(side, j)
            proj_ref[:, lanes] += dot(far_att_ref[...], far_ref[side, j].reshape(rows, part), ((1,), (0,)))
    inner = proj_ref.shape[1]
    for pair in range(TOK // (2 * BS)):
        rows_of = slice(pair * 2 * BS, (pair + 1) * 2 * BS)
        x = pair * 2 // BY
        y = pair * 2 % BY
        proj = proj_ref[rows_of, :]
        gain = gain_ref[...]
        flag = jnp.where(
            lax.broadcasted_iota(jnp.int32, (2 * BS, 1), 0) < BS, bound_ref[0, x, y], bound_ref[0, x, y + 1]
        ).astype(jnp.float32)
        cot = jnp.concatenate([cot_ref[0, x, y], cot_ref[0, x, y + 1]], axis=0) * flag
        inv_rms = lax.rsqrt(jnp.sum(proj * proj, axis=1, keepdims=True) * (1.0 / inner) + 1e-05)
        normed = proj * inv_rms * gain
        pred0 = jnp.sum(normed * read_ref[0:1, :], axis=1, keepdims=True) * flag
        pred1 = jnp.sum(normed * read_ref[1:2, :], axis=1, keepdims=True) * flag
        pred = jnp.where(lax.broadcasted_iota(jnp.int32, (2 * BS, 2), 1) == 0, pred0, pred1)
        pred_ref[0, x, y] = pred[:BS]
        pred_ref[0, x, y + 1] = pred[BS:]
        gained = (cot[:, 0:1] * read_ref[0:1, :] + cot[:, 1:2] * read_ref[1:2, :]) * gain
        inner_mean = jnp.sum(gained * proj, axis=1, keepdims=True) * (1.0 / inner)
        gp_ref[rows_of, :] = (inv_rms * gained - proj * (inv_rms * inv_rms * inv_rms * inner_mean)).astype(jnp.bfloat16)
    near = None
    far = None
    for side in range(2):
        term = dot(gp_ref[:, near_cols(side)], near_ref[side].reshape(rows, cols), ((1,), (1,)))
        near = term if near is None else near + term
        for j in range(n_chip):
            term = dot(gp_ref[:, far_cols(side, j)], far_ref[side, j].reshape(rows, part), ((1,), (1,)))
            far = term if far is None else far + term
    near = near.astype(jnp.bfloat16)
    far = far.astype(jnp.bfloat16)
    for k in range(n_ring):
        ga_ref[:, near_head(k)] = near[:, k * HS : (k + 1) * HS]
        ga_ref[:, far_head(k)] = far[:, k * HS : (k + 1) * HS]


def project(boundary, position, att, weights, gain, read_rows, cotangent):
    vmem = pl.BlockSpec(memory_space=pltpu.VMEM)
    smem = pl.BlockSpec(memory_space=pltpu.SMEM)
    hbm = pl.BlockSpec(memory_space=pl.ANY)
    near, _, far, _ = weights
    tokens, inner = att.shape
    return pl.pallas_call(
        project_kernel,
        in_specs=[smem, smem, vmem, hbm, hbm, hbm, hbm, vmem, vmem, vmem],
        out_specs=[vmem, vmem],
        out_shape=[
            jax.ShapeDtypeStruct(cotangent.shape, jnp.float32),
            jax.ShapeDtypeStruct(att.shape, jnp.bfloat16),
        ],
        scratch_shapes=[
            pltpu.VMEM((2,) + near.shape, jnp.bfloat16),
            pltpu.VMEM((2,) + far.shape, jnp.bfloat16),
            pltpu.VMEM((tokens, inner // 2), jnp.bfloat16),
            pltpu.VMEM((tokens, inner // 2), jnp.bfloat16),
            pltpu.VMEM(att.shape, jnp.float32),
            pltpu.VMEM(att.shape, jnp.bfloat16),
            pltpu.SemaphoreType.DMA((4,)),
        ],
        compiler_params=pltpu.CompilerParams(vmem_limit_bytes=VMEM_LIMIT),
        name="project",
    )(boundary, position, att, *weights, gain, read_rows, cotangent)


def backward_kernel(q_ref, ga_ref, prob_ref, *rest):
    count = len(PIECES)
    kv_refs = rest[:count]
    gq_ref = rest[count]
    gkv_refs = rest[count + 1 :]
    for h in range(GROUP):
        lanes = slice(h * HS, (h + 1) * HS)
        query = q_ref[0, :, :, :, lanes].reshape(TOK, HS)
        keys = piece_rows(kv_refs, 0, lanes)
        values = piece_rows(kv_refs, 1, lanes)
        grad_att = ga_ref[:, lanes]
        prob = prob_ref[h]
        grad_prob = dot(values, grad_att, ((1,), (1,)))
        inner_sum = jnp.sum(prob * grad_prob, axis=0, keepdims=True)
        grad_scores = (prob * (grad_prob - inner_sum) * (HS**-0.5)).astype(jnp.bfloat16)
        grad_query = dot(grad_scores, keys, ((0,), (0,)))
        gq_ref[0, :, :, :, lanes] = grad_query.reshape(BX, BY, BS, HS).astype(gq_ref.dtype)
        grads = (dot(grad_scores, query, ((1,), (0,))), dot(prob.astype(jnp.bfloat16), grad_att, ((1,), (0,))))
        for which, grad in enumerate(grads):
            start = 0
            for ref in gkv_refs:
                shape = ref.shape[1:4]
                rows = shape[0] * shape[1] * shape[2]
                ref[which, :, :, :, lanes] = grad[start : start + rows].reshape(shape + (HS,)).astype(ref.dtype)
                start += rows


def backward(queries, grad_att, prob, pieces):
    inner = queries.shape[-1]
    width = GROUP * HS

    def wide(shape):
        return pl.BlockSpec(tuple(shape[:-1]) + (width,), lambda g: (0,) * (len(shape) - 1) + (g,))

    shapes = [p.shape for p in pieces]
    blocks, rest = shapes[0], shapes[0][3:]
    sums = [blocks, (2, 1, BY + 2) + rest, (2, 1, BY + 2) + rest, shapes[-1], shapes[-1]]
    return pl.pallas_call(
        backward_kernel,
        grid=(inner // width,),
        in_specs=[wide(queries.shape), wide(grad_att.shape), pl.BlockSpec((GROUP, KEYS, TOK), lambda g: (g, 0, 0))]
        + [wide(s) for s in shapes],
        out_specs=[wide(queries.shape)] + [wide(s) for s in sums],
        out_shape=[jax.ShapeDtypeStruct(queries.shape, jnp.bfloat16)]
        + [jax.ShapeDtypeStruct(s, jnp.float32 if i == 0 else jnp.bfloat16) for i, s in enumerate(sums)],
        compiler_params=pltpu.CompilerParams(vmem_limit_bytes=VMEM_LIMIT),
        name="attend_back",
    )(queries, grad_att, prob, *pieces)


def add_rows_kernel(own_ref, low_ref, high_ref, out_ref, edge_ref):
    f32 = jnp.float32
    for which in range(2):
        for x in range(BX):
            for y in range(BY):
                total = own_ref[which, x, y]
                if x == 0:
                    total = total + low_ref[which, 0, y].astype(f32)
                if x == BX - 1:
                    total = total + high_ref[which, 0, y].astype(f32)
                if y in (0, BY - 1):
                    edge_ref[which, x, y // (BY - 1)] = total
                else:
                    out_ref[which, x, y] = total.astype(out_ref.dtype)


def add_rows(own, low, high):
    inner = own.shape[-1]
    width = inner // 4

    def wide(shape):
        return pl.BlockSpec(tuple(shape[:-1]) + (width,), lambda g: (0, 0, 0, 0, g))

    edge = own.shape[:2] + (2,) + own.shape[3:]
    return pl.pallas_call(
        add_rows_kernel,
        grid=(inner // width,),
        in_specs=[wide(own.shape), wide(low.shape), wide(high.shape)],
        out_specs=[wide(own.shape), wide(edge)],
        out_shape=[jax.ShapeDtypeStruct(own.shape, jnp.bfloat16), jax.ShapeDtypeStruct(edge, jnp.float32)],
        compiler_params=pltpu.CompilerParams(vmem_limit_bytes=SMALL_LIMIT),
        name="add_rows",
    )(own, low, high)


def add_columns_kernel(edge_ref, low_ref, high_ref, partial_hbm, out_ref):
    del partial_hbm
    first = pl.program_id(0) == 0

    @pl.when(first)
    def _():
        out_ref[...] = (edge_ref[...] + low_ref[...].astype(jnp.float32)).astype(out_ref.dtype)

    @pl.when(jnp.logical_not(first))
    def _():
        out_ref[...] = (edge_ref[...] + high_ref[...].astype(jnp.float32)).astype(out_ref.dtype)


def add_columns(edge, low, high, partial):
    block = edge.shape[:2] + (1,) + edge.shape[3:]
    whole = pl.BlockSpec(block, lambda i: (0, 0, 0, 0, 0))
    return pl.pallas_call(
        add_columns_kernel,
        grid=(2,),
        in_specs=[
            pl.BlockSpec(block, lambda i: (0, 0, i, 0, 0)),
            whole,
            whole,
            pl.BlockSpec(memory_space=pl.ANY),
        ],
        out_specs=pl.BlockSpec(block, lambda i: (0, 0, i * (BY - 1), 0, 0)),
        out_shape=jax.ShapeDtypeStruct(partial.shape, partial.dtype),
        input_output_aliases={3: 0},
        compiler_params=pltpu.CompilerParams(vmem_limit_bytes=SMALL_LIMIT),
        name="add_columns",
    )(edge, low, high, partial)


def around(value, axis, step):
    count = lax.axis_size(axis)
    return lax.ppermute(value, axis, [(i, (i + step) % count) for i in range(count)])


def swap_cores(value):
    return lax.ppermute(value, "sx", [(i, i ^ 1) for i in range(lax.axis_size("sx"))])


def body(queries, keys_values, out_weight, gain, read_weight, adjacency, boundary, cotangent):
    size_x, size_y = queries.shape[1:3]
    inner = out_weight.shape[1]
    n_sx, n_sy, n_wa = (lax.axis_size(axis) for axis in ("sx", "sy", "wa"))
    row, column, case = (lax.axis_index(axis) for axis in ("sx", "sy", "wa"))
    core, chip, ring, half = row % 2, row // 2, case // 2, case % 2
    kv = keys_values[:, 0]
    cols = inner // 2
    part = inner // n_sx
    near_slab = lax.dynamic_slice_in_dim(out_weight, core * cols, cols, axis=1)
    far_slab = lax.dynamic_slice_in_dim(out_weight, core * cols + chip * part, part, axis=1)
    def mirrored(value, step):
        pairs = [
            (l * n_wa + w, (n_sy - 1 - l) * n_wa + (((w ^ 1) + 2 * step) % n_wa)) for l in range(n_sy) for w in range(n_wa)
        ]
        return lax.ppermute(value, ("sy", "wa"), pairs)

    far = (mirrored(far_slab, 0), mirrored(far_slab, n_wa // 4))
    groups = [list(range(h, n_wa, 2)) for h in range(2)]
    near = lax.all_gather(near_slab, "wa", axis=0, axis_index_groups=groups)
    ylow = shift(kv[:, :, size_y - 1 :], "sy", 1)
    yhigh = shift(kv[:, :, :1], "sy", -1)
    far, kv_after = lax.optimization_barrier((far, kv))
    far = jnp.stack(far)
    far_y = jnp.concatenate([far] + [around(far, "wa", 2 * k) for k in (1, -1, 2)])
    xlow = shift(kv_after[:, size_x - 1 :], "sx", 1)
    xhigh = shift(kv_after[:, :1], "sx", -1)
    clow = shift(jnp.concatenate([ylow[:, size_x - 1 :], yhigh[:, size_x - 1 :]], axis=2), "sx", 1)
    chigh = shift(jnp.concatenate([ylow[:, :1], yhigh[:, :1]], axis=2), "sx", -1)
    pieces = (kv, xlow, clow, xhigh, chigh, ylow, yhigh)
    far_x = jnp.stack([far_y] + [around(far_y, "sx", 2 * k) for k in (1, 2, -1)])
    position = jnp.stack(
        [
            row * size_x,
            column * size_y,
            jnp.int32(size_x * n_sx),
            jnp.int32(size_y * n_sy),
            core,
            chip,
            ring,
            half,
        ]
    ).astype(jnp.int32)
    att, prob = forward(adjacency, position, queries, pieces)
    near, att = lax.optimization_barrier((near, att))
    weights = (near, swap_cores(near), far_x, swap_cores(far_x))
    prediction, grad_att = project(boundary, position, att, weights, gain[None], read_weight.T, cotangent)
    grad_queries, own, gxlow, gxhigh, gylow, gyhigh = backward(queries, grad_att, prob, pieces)
    from_low = shift(gxhigh, "sx", 1)
    from_high = shift(gxlow, "sx", -1)
    f32 = jnp.float32

    def side(rim, y):
        first = rim[:, :1].astype(f32) + from_low[:, :, size_y + y : size_y + y + 1].astype(f32)
        last = rim[:, 1:].astype(f32) + from_high[:, :, size_y + y : size_y + y + 1].astype(f32)
        return jnp.concatenate([first, last], axis=1).astype(jnp.bfloat16)

    left = shift(side(gyhigh, 1), "sy", 1)
    right = shift(side(gylow, 0), "sy", -1)
    partial, edge = add_rows(own, from_low, from_high)
    grad_kv = add_columns(edge, left, right, partial)
    return (prediction, grad_queries, grad_kv[:, None])


def solution(mesh):
    return jax.shard_map(
        body,
        mesh=mesh,
        in_specs=(
            P("wa", "sx", "sy", None, None),
            P(None, "wa", "sx", "sy", None, None),
            P("wa", None),
            P(),
            P(),
            P("wa", "sx", "sy", None),
            P("wa", "sx", "sy"),
            P("wa", "sx", "sy", None, None),
        ),
        out_specs=(
            P("wa", "sx", "sy", None, None),
            P("wa", "sx", "sy", None, None),
            P(None, "wa", "sx", "sy", None, None),
        ),
        check_vma=False,
    )
```

```python
import jax
import jax.numpy as jnp
from jax import lax
from jax.experimental import pallas as pl
from jax.experimental.pallas import tpu as pltpu
from jax.sharding import PartitionSpec as P

HS = 128
BS = 16
BX = 2
BY = 4
TOK = BX * BY * BS
GROUP = 4
VMEM_LIMIT = 60 * 1024 * 1024
SMALL_LIMIT = 24 * 1024 * 1024

LOCAL = [(x, y) for x in range(BX) for y in range(BY)]
XLOW = [(-1, y) for y in range(BY)]
XHIGH = [(BX, y) for y in range(BY)]
YLOW = [(x, -1) for x in range(BX)]
YHIGH = [(x, BY) for x in range(BX)]
CLOW = [(-1, -1), (-1, BY)]
CHIGH = [(BX, -1), (BX, BY)]
PIECES = [LOCAL, XLOW, CLOW, XHIGH, CHIGH, YLOW, YHIGH]
KEY_BLOCKS = [block for piece in PIECES for block in piece]
KEYS = len(KEY_BLOCKS) * BS


def shift(value, axis, step):
    count = lax.axis_size(axis)
    pairs = [(i, i + step) for i in range(count) if 0 <= i + step < count]
    return lax.ppermute(value, axis, pairs)


def dot(a, b, dims):
    return lax.dot_general(a, b, (dims, ((), ())), preferred_element_type=jnp.float32)


def piece_rows(refs, which, lanes):
    parts = []
    for ref in refs:
        blocks = ref[which, :, :, :, lanes]
        parts.append(blocks.reshape(-1, HS))
    return jnp.concatenate(parts, axis=0)


def allowed_mask(adj_ref, pos_ref):
    lane = lax.broadcasted_iota(jnp.int32, (1, TOK), 1)
    block = lane // BS
    bx = block // BY
    by = block % BY
    entries = []
    for e in range(4):
        vec = jnp.zeros((1, TOK), jnp.int32)
        for b in range(BX * BY):
            vec = jnp.where(block == b, adj_ref[0, b // BY, b % BY, e], vec)
        entries.append(vec)
    rows = []
    for kx, ky in KEY_BLOCKS:
        dx = kx - bx
        dy = ky - by
        near = (jnp.abs(dx) <= 1) & (jnp.abs(dy) <= 1)
        code = 3 * (dx + 1) + dy + 1
        entry = code - (code > 4).astype(jnp.int32)
        listed = code == 4
        for vec in entries:
            listed = listed | ((vec == entry) & (code != 4))
        gx = pos_ref[0] + kx
        gy = pos_ref[1] + ky
        inside = (gx >= 0) & (gx < pos_ref[2]) & (gy >= 0) & (gy < pos_ref[3])
        flag = jnp.where(near & listed, 1.0, 0.0) * jnp.where(inside, 1.0, 0.0)
        rows.append(jnp.broadcast_to(flag, (BS, TOK)))
    return jnp.concatenate(rows, axis=0)


def forward_kernel(adj_ref, pos_ref, q_ref, *rest):
    kv_refs = rest[: len(PIECES)]
    att_ref, prob_ref, mask_ref = rest[len(PIECES) :]

    @pl.when(pl.program_id(0) == 0)
    def _():
        mask_ref[...] = allowed_mask(adj_ref, pos_ref)

    for h in range(GROUP):
        lanes = slice(h * HS, (h + 1) * HS)
        query = q_ref[0, :, :, :, lanes].reshape(TOK, HS)
        keys = piece_rows(kv_refs, 0, lanes)
        values = piece_rows(kv_refs, 1, lanes)
        scores = dot(keys, query, ((1,), (1,))) * (HS**-0.5)
        masked = jnp.where(mask_ref[...] > 0.5, scores, -1e30)
        exponent = jnp.exp(masked - jnp.max(masked, axis=0, keepdims=True))
        prob = exponent / jnp.sum(exponent, axis=0, keepdims=True)
        prob_ref[h] = prob
        att = dot(prob.astype(jnp.bfloat16), values, ((0,), (0,)))
        att_ref[:, lanes] = att.astype(jnp.bfloat16)


def forward(adjacency, position, queries, pieces):
    inner = queries.shape[-1]
    width = GROUP * HS
    smem = pl.BlockSpec(memory_space=pltpu.SMEM)
    specs = [
        pl.BlockSpec(p.shape[:-1] + (width,), lambda g: (0, 0, 0, 0, g))
        for p in pieces
    ]
    return pl.pallas_call(
        forward_kernel,
        grid=(inner // width,),
        in_specs=[smem, smem, pl.BlockSpec(queries.shape[:-1] + (width,), lambda g: (0, 0, 0, 0, g))] + specs,
        out_specs=[
            pl.BlockSpec((TOK, width), lambda g: (0, g)),
            pl.BlockSpec((GROUP, KEYS, TOK), lambda g: (g, 0, 0)),
        ],
        out_shape=[
            jax.ShapeDtypeStruct((TOK, inner), jnp.bfloat16),
            jax.ShapeDtypeStruct((inner // HS, KEYS, TOK), jnp.float32),
        ],
        scratch_shapes=[pltpu.VMEM((KEYS, TOK), jnp.float32)],
        compiler_params=pltpu.CompilerParams(vmem_limit_bytes=VMEM_LIMIT),
        name="attend",
    )(adjacency, position, queries, *pieces)


def head_lanes(index):
    return pl.ds(pl.multiple_of(index * HS, HS), HS)


def far_step(k):
    return (0, 1, 7, 2)[k // 2] + 4 * (k % 2)


def weight_lanes(pos_ref, n_ring, cols):
    core = pos_ref[4]
    ring = pos_ref[5]
    half = pos_ref[6]

    def near_head(k):
        return head_lanes(k * 2 + half)

    def far_head(k):
        return head_lanes(lax.rem(ring + 2 * n_ring - far_step(k), n_ring) * 2 + 1 - half)

    def side_cols(side):
        return pl.ds(pl.multiple_of((core if side == 0 else 1 - core) * cols, cols), cols)

    return near_head, far_head, side_cols


def project_near_kernel(pos_ref, att_ref, own_hbm, swap_hbm, proj_ref, w_ref, part_ref, sems):
    copies = [
        pltpu.make_async_copy(own_hbm, w_ref.at[0], sems.at[0]),
        pltpu.make_async_copy(swap_hbm, w_ref.at[1], sems.at[1]),
    ]
    for copy in copies:
        copy.start()
    n_ring, _, cols = w_ref.shape[1:]
    near_head, _, side_cols = weight_lanes(pos_ref, n_ring, cols)
    for k in range(n_ring):
        part_ref[:, k * HS : (k + 1) * HS] = att_ref[:, near_head(k)]
    for side in range(2):
        copies[side].wait()
        proj_ref[:, side_cols(side)] = dot(part_ref[...], w_ref[side].reshape(n_ring * HS, cols), ((1,), (0,)))


def project_near(position, att, own, swapped):
    vmem = pl.BlockSpec(memory_space=pltpu.VMEM)
    hbm = pl.BlockSpec(memory_space=pl.ANY)
    tokens, inner = att.shape
    return pl.pallas_call(
        project_near_kernel,
        in_specs=[pl.BlockSpec(memory_space=pltpu.SMEM), vmem, hbm, hbm],
        out_specs=vmem,
        out_shape=jax.ShapeDtypeStruct(att.shape, jnp.float32),
        scratch_shapes=[
            pltpu.VMEM((2,) + own.shape, jnp.bfloat16),
            pltpu.VMEM((tokens, inner // 2), jnp.bfloat16),
            pltpu.SemaphoreType.DMA((2,)),
        ],
        compiler_params=pltpu.CompilerParams(vmem_limit_bytes=VMEM_LIMIT),
        name="project_near",
    )(position, att, own, swapped)


def project_kernel(
    bound_ref, pos_ref, att_ref, part_ref, near_hbm, near_swap_hbm, far_hbm, far_swap_hbm, gain_ref, read_ref, cot_ref,
    pred_ref, ga_ref, near_ref, far_ref, far_att_ref, proj_ref, gp_ref, sems,
):
    far_copies = [
        pltpu.make_async_copy(far_hbm, far_ref.at[0], sems.at[0]),
        pltpu.make_async_copy(far_swap_hbm, far_ref.at[1], sems.at[1]),
    ]
    near_copies = [
        pltpu.make_async_copy(near_hbm, near_ref.at[0], sems.at[2]),
        pltpu.make_async_copy(near_swap_hbm, near_ref.at[1], sems.at[3]),
    ]
    for copy in far_copies + near_copies:
        copy.start()
    n_ring, _, cols = near_ref.shape[1:]
    near_head, far_head, side_cols = weight_lanes(pos_ref, n_ring, cols)
    for k in range(n_ring):
        far_att_ref[:, k * HS : (k + 1) * HS] = att_ref[:, far_head(k)]
    rows = n_ring * HS
    for side in range(2):
        far_copies[side].wait()
        lanes = side_cols(side)
        term = dot(far_att_ref[...], far_ref[side].reshape(rows, cols), ((1,), (0,)))
        proj_ref[:, lanes] = part_ref[:, lanes] + term
    inner = proj_ref.shape[1]
    for pair in range(TOK // (2 * BS)):
        rows_of = slice(pair * 2 * BS, (pair + 1) * 2 * BS)
        x = pair * 2 // BY
        y = pair * 2 % BY
        proj = proj_ref[rows_of, :]
        gain = gain_ref[...]
        flag = jnp.where(
            lax.broadcasted_iota(jnp.int32, (2 * BS, 1), 0) < BS, bound_ref[0, x, y], bound_ref[0, x, y + 1]
        ).astype(jnp.float32)
        cot = jnp.concatenate([cot_ref[0, x, y], cot_ref[0, x, y + 1]], axis=0) * flag
        inv_rms = lax.rsqrt(jnp.sum(proj * proj, axis=1, keepdims=True) * (1.0 / inner) + 1e-05)
        normed = proj * inv_rms * gain
        pred0 = jnp.sum(normed * read_ref[0:1, :], axis=1, keepdims=True) * flag
        pred1 = jnp.sum(normed * read_ref[1:2, :], axis=1, keepdims=True) * flag
        pred = jnp.where(lax.broadcasted_iota(jnp.int32, (2 * BS, 2), 1) == 0, pred0, pred1)
        pred_ref[0, x, y] = pred[:BS]
        pred_ref[0, x, y + 1] = pred[BS:]
        gained = (cot[:, 0:1] * read_ref[0:1, :] + cot[:, 1:2] * read_ref[1:2, :]) * gain
        inner_mean = jnp.sum(gained * proj, axis=1, keepdims=True) * (1.0 / inner)
        gp_ref[rows_of, :] = (inv_rms * gained - proj * (inv_rms * inv_rms * inv_rms * inner_mean)).astype(jnp.bfloat16)

    def grad(w_ref):
        total = None
        for side in range(2):
            term = dot(gp_ref[:, side_cols(side)], w_ref[side].reshape(rows, cols), ((1,), (1,)))
            total = term if total is None else total + term
        return total.astype(jnp.bfloat16)

    far = grad(far_ref)
    for k in range(n_ring):
        ga_ref[:, far_head(k)] = far[:, k * HS : (k + 1) * HS]
    for copy in near_copies:
        copy.wait()
    near = grad(near_ref)
    for k in range(n_ring):
        ga_ref[:, near_head(k)] = near[:, k * HS : (k + 1) * HS]


def project(boundary, position, att, part, weights, gain, read_rows, cotangent):
    vmem = pl.BlockSpec(memory_space=pltpu.VMEM)
    smem = pl.BlockSpec(memory_space=pltpu.SMEM)
    hbm = pl.BlockSpec(memory_space=pl.ANY)
    near, _, far, _ = weights
    tokens, inner = att.shape
    return pl.pallas_call(
        project_kernel,
        in_specs=[smem, smem, vmem, vmem, hbm, hbm, hbm, hbm, vmem, vmem, vmem],
        out_specs=[vmem, vmem],
        out_shape=[
            jax.ShapeDtypeStruct(cotangent.shape, jnp.float32),
            jax.ShapeDtypeStruct(att.shape, jnp.bfloat16),
        ],
        scratch_shapes=[
            pltpu.VMEM((2,) + near.shape, jnp.bfloat16),
            pltpu.VMEM((2,) + far.shape, jnp.bfloat16),
            pltpu.VMEM((tokens, inner // 2), jnp.bfloat16),
            pltpu.VMEM(att.shape, jnp.float32),
            pltpu.VMEM(att.shape, jnp.bfloat16),
            pltpu.SemaphoreType.DMA((4,)),
        ],
        compiler_params=pltpu.CompilerParams(vmem_limit_bytes=VMEM_LIMIT),
        name="project",
    )(boundary, position, att, part, *weights, gain, read_rows, cotangent)


def backward_kernel(q_ref, ga_ref, prob_ref, *rest):
    count = len(PIECES)
    kv_refs = rest[:count]
    gq_ref = rest[count]
    gkv_refs = rest[count + 1 :]
    for h in range(GROUP):
        lanes = slice(h * HS, (h + 1) * HS)
        query = q_ref[0, :, :, :, lanes].reshape(TOK, HS)
        keys = piece_rows(kv_refs, 0, lanes)
        values = piece_rows(kv_refs, 1, lanes)
        grad_att = ga_ref[:, lanes]
        prob = prob_ref[h]
        grad_prob = dot(values, grad_att, ((1,), (1,)))
        inner_sum = jnp.sum(prob * grad_prob, axis=0, keepdims=True)
        grad_scores = (prob * (grad_prob - inner_sum) * (HS**-0.5)).astype(jnp.bfloat16)
        grad_query = dot(grad_scores, keys, ((0,), (0,)))
        gq_ref[0, :, :, :, lanes] = grad_query.reshape(BX, BY, BS, HS).astype(gq_ref.dtype)
        grads = (dot(grad_scores, query, ((1,), (0,))), dot(prob.astype(jnp.bfloat16), grad_att, ((1,), (0,))))
        for which, grad in enumerate(grads):
            start = 0
            for ref in gkv_refs:
                shape = ref.shape[1:4]
                rows = shape[0] * shape[1] * shape[2]
                ref[which, :, :, :, lanes] = grad[start : start + rows].reshape(shape + (HS,)).astype(ref.dtype)
                start += rows


def backward(queries, grad_att, prob, pieces):
    inner = queries.shape[-1]
    width = GROUP * HS

    def wide(shape):
        return pl.BlockSpec(tuple(shape[:-1]) + (width,), lambda g: (0,) * (len(shape) - 1) + (g,))

    shapes = [p.shape for p in pieces]
    blocks, rest = shapes[0], shapes[0][3:]
    sums = [blocks, (2, 1, BY + 2) + rest, (2, 1, BY + 2) + rest, shapes[-1], shapes[-1]]
    return pl.pallas_call(
        backward_kernel,
        grid=(inner // width,),
        in_specs=[wide(queries.shape), wide(grad_att.shape), pl.BlockSpec((GROUP, KEYS, TOK), lambda g: (g, 0, 0))]
        + [wide(s) for s in shapes],
        out_specs=[wide(queries.shape)] + [wide(s) for s in sums],
        out_shape=[jax.ShapeDtypeStruct(queries.shape, jnp.bfloat16)]
        + [jax.ShapeDtypeStruct(s, jnp.float32 if i == 0 else jnp.bfloat16) for i, s in enumerate(sums)],
        compiler_params=pltpu.CompilerParams(vmem_limit_bytes=VMEM_LIMIT),
        name="attend_back",
    )(queries, grad_att, prob, *pieces)


def add_rows_kernel(own_ref, low_ref, high_ref, out_ref, edge_ref):
    f32 = jnp.float32
    for which in range(2):
        for x in range(BX):
            for y in range(BY):
                total = own_ref[which, x, y]
                if x == 0:
                    total = total + low_ref[which, 0, y].astype(f32)
                if x == BX - 1:
                    total = total + high_ref[which, 0, y].astype(f32)
                if y in (0, BY - 1):
                    edge_ref[which, x, y // (BY - 1)] = total
                else:
                    out_ref[which, x, y] = total.astype(out_ref.dtype)


def add_rows(own, low, high):
    inner = own.shape[-1]
    width = inner // 4

    def wide(shape):
        return pl.BlockSpec(tuple(shape[:-1]) + (width,), lambda g: (0, 0, 0, 0, g))

    edge = own.shape[:2] + (2,) + own.shape[3:]
    return pl.pallas_call(
        add_rows_kernel,
        grid=(inner // width,),
        in_specs=[wide(own.shape), wide(low.shape), wide(high.shape)],
        out_specs=[wide(own.shape), wide(edge)],
        out_shape=[jax.ShapeDtypeStruct(own.shape, jnp.bfloat16), jax.ShapeDtypeStruct(edge, jnp.float32)],
        compiler_params=pltpu.CompilerParams(vmem_limit_bytes=SMALL_LIMIT),
        name="add_rows",
    )(own, low, high)


def add_columns_kernel(edge_ref, low_ref, high_ref, partial_hbm, out_ref):
    del partial_hbm
    first = pl.program_id(0) == 0

    @pl.when(first)
    def _():
        out_ref[...] = (edge_ref[...] + low_ref[...].astype(jnp.float32)).astype(out_ref.dtype)

    @pl.when(jnp.logical_not(first))
    def _():
        out_ref[...] = (edge_ref[...] + high_ref[...].astype(jnp.float32)).astype(out_ref.dtype)


def add_columns(edge, low, high, partial):
    block = edge.shape[:2] + (1,) + edge.shape[3:]
    whole = pl.BlockSpec(block, lambda i: (0, 0, 0, 0, 0))
    return pl.pallas_call(
        add_columns_kernel,
        grid=(2,),
        in_specs=[
            pl.BlockSpec(block, lambda i: (0, 0, i, 0, 0)),
            whole,
            whole,
            pl.BlockSpec(memory_space=pl.ANY),
        ],
        out_specs=pl.BlockSpec(block, lambda i: (0, 0, i * (BY - 1), 0, 0)),
        out_shape=jax.ShapeDtypeStruct(partial.shape, partial.dtype),
        input_output_aliases={3: 0},
        compiler_params=pltpu.CompilerParams(vmem_limit_bytes=SMALL_LIMIT),
        name="add_columns",
    )(edge, low, high, partial)


def around(value, axis, step):
    count = lax.axis_size(axis)
    return lax.ppermute(value, axis, [(i, (i + step) % count) for i in range(count)])


def swap_cores(value):
    return lax.ppermute(value, "sx", [(i, i ^ 1) for i in range(lax.axis_size("sx"))])


def body(queries, keys_values, out_weight, gain, read_weight, adjacency, boundary, cotangent):
    size_x, size_y = queries.shape[1:3]
    inner = out_weight.shape[1]
    n_sx, n_sy, n_wa = (lax.axis_size(axis) for axis in ("sx", "sy", "wa"))
    row, column, case = (lax.axis_index(axis) for axis in ("sx", "sy", "wa"))
    core, ring, half = row % 2, case // 2, case % 2
    kv = keys_values[:, 0]
    cols = inner // 2
    slab = lax.dynamic_slice_in_dim(out_weight, core * cols, cols, axis=1)
    groups = [list(range(h, n_wa, 2)) for h in range(2)]
    near = lax.all_gather(slab, "wa", axis=0, axis_index_groups=groups)

    def mirrored(value, step):
        pairs = [
            (l * n_wa + w, (n_sy - 1 - l) * n_wa + (((w ^ 1) + 2 * step) % n_wa)) for l in range(n_sy) for w in range(n_wa)
        ]
        return lax.ppermute(value, ("sy", "wa"), pairs)

    far = (mirrored(slab, 0), mirrored(slab, n_wa // 4))
    ylow = shift(kv[:, :, size_y - 1 :], "sy", 1)
    yhigh = shift(kv[:, :, :1], "sy", -1)
    xlow = shift(kv[:, size_x - 1 :], "sx", 1)
    xhigh = shift(kv[:, :1], "sx", -1)
    far, xlow, xhigh, ylow, yhigh = lax.optimization_barrier((far, xlow, xhigh, ylow, yhigh))
    far = jnp.stack(far)
    far = jnp.concatenate([far] + [around(far, "wa", 2 * k) for k in (1, -1, 2)])
    clow = shift(jnp.concatenate([ylow[:, size_x - 1 :], yhigh[:, size_x - 1 :]], axis=2), "sx", 1)
    chigh = shift(jnp.concatenate([ylow[:, :1], yhigh[:, :1]], axis=2), "sx", -1)
    pieces = (kv, xlow, clow, xhigh, chigh, ylow, yhigh)
    position = jnp.stack(
        [
            row * size_x,
            column * size_y,
            jnp.int32(size_x * n_sx),
            jnp.int32(size_y * n_sy),
            core,
            ring,
            half,
        ]
    ).astype(jnp.int32)
    att, prob = forward(adjacency, position, queries, pieces)
    near, att = lax.optimization_barrier((near, att))
    near_swap = swap_cores(near)
    part = project_near(position, att, near, near_swap)
    weights = (near, near_swap, far, swap_cores(far))
    prediction, grad_att = project(boundary, position, att, part, weights, gain[None], read_weight.T, cotangent)
    grad_queries, own, gxlow, gxhigh, gylow, gyhigh = backward(queries, grad_att, prob, pieces)
    from_low = shift(gxhigh, "sx", 1)
    from_high = shift(gxlow, "sx", -1)
    f32 = jnp.float32

    def side(rim, y):
        first = rim[:, :1].astype(f32) + from_low[:, :, size_y + y : size_y + y + 1].astype(f32)
        last = rim[:, 1:].astype(f32) + from_high[:, :, size_y + y : size_y + y + 1].astype(f32)
        return jnp.concatenate([first, last], axis=1).astype(jnp.bfloat16)

    left = shift(side(gyhigh, 1), "sy", 1)
    right = shift(side(gylow, 0), "sy", -1)
    partial, edge = add_rows(own, from_low, from_high)
    grad_kv = add_columns(edge, left, right, partial)
    return (prediction, grad_queries, grad_kv[:, None])


def solution(mesh):
    return jax.shard_map(
        body,
        mesh=mesh,
        in_specs=(
            P("wa", "sx", "sy", None, None),
            P(None, "wa", "sx", "sy", None, None),
            P("wa", None),
            P(),
            P(),
            P("wa", "sx", "sy", None),
            P("wa", "sx", "sy"),
            P("wa", "sx", "sy", None, None),
        ),
        out_specs=(
            P("wa", "sx", "sy", None, None),
            P("wa", "sx", "sy", None, None),
            P(None, "wa", "sx", "sy", None, None),
        ),
        check_vma=False,
    )
```

```python
import jax
import jax.numpy as jnp
from jax import lax
from jax.experimental import pallas as pl
from jax.experimental.pallas import tpu as pltpu
from jax.sharding import PartitionSpec as P

HS = 128
BS = 16
BX = 2
BY = 4
TOK = BX * BY * BS
GROUP = 4
VMEM_LIMIT = 60 * 1024 * 1024
SMALL_LIMIT = 24 * 1024 * 1024

LOCAL = [(x, y) for x in range(BX) for y in range(BY)]
XLOW = [(-1, y) for y in range(BY)]
XHIGH = [(BX, y) for y in range(BY)]
YLOW = [(x, -1) for x in range(BX)]
YHIGH = [(x, BY) for x in range(BX)]
CLOW = [(-1, -1), (-1, BY)]
CHIGH = [(BX, -1), (BX, BY)]
PIECES = [LOCAL, XLOW, CLOW, XHIGH, CHIGH, YLOW, YHIGH]
KEY_BLOCKS = [block for piece in PIECES for block in piece]
KEYS = len(KEY_BLOCKS) * BS


def shift(value, axis, step):
    count = lax.axis_size(axis)
    pairs = [(i, i + step) for i in range(count) if 0 <= i + step < count]
    return lax.ppermute(value, axis, pairs)


def dot(a, b, dims):
    return lax.dot_general(a, b, (dims, ((), ())), preferred_element_type=jnp.float32)


def piece_rows(refs, which, lanes):
    parts = []
    for ref in refs:
        blocks = ref[which, :, :, :, lanes]
        parts.append(blocks.reshape(-1, HS))
    return jnp.concatenate(parts, axis=0)


def allowed_mask(adj_ref, pos_ref):
    lane = lax.broadcasted_iota(jnp.int32, (1, TOK), 1)
    block = lane // BS
    bx = block // BY
    by = block % BY
    entries = []
    for e in range(4):
        vec = jnp.zeros((1, TOK), jnp.int32)
        for b in range(BX * BY):
            vec = jnp.where(block == b, adj_ref[0, b // BY, b % BY, e], vec)
        entries.append(vec)
    rows = []
    for kx, ky in KEY_BLOCKS:
        dx = kx - bx
        dy = ky - by
        near = (jnp.abs(dx) <= 1) & (jnp.abs(dy) <= 1)
        code = 3 * (dx + 1) + dy + 1
        entry = code - (code > 4).astype(jnp.int32)
        listed = code == 4
        for vec in entries:
            listed = listed | ((vec == entry) & (code != 4))
        gx = pos_ref[0] + kx
        gy = pos_ref[1] + ky
        inside = (gx >= 0) & (gx < pos_ref[2]) & (gy >= 0) & (gy < pos_ref[3])
        flag = jnp.where(near & listed, 1.0, 0.0) * jnp.where(inside, 1.0, 0.0)
        rows.append(jnp.broadcast_to(flag, (BS, TOK)))
    return jnp.concatenate(rows, axis=0)


def forward_kernel(adj_ref, pos_ref, q_ref, *rest):
    kv_refs = rest[: len(PIECES)]
    att_ref, prob_ref, mask_ref = rest[len(PIECES) :]

    @pl.when(pl.program_id(0) == 0)
    def _():
        mask_ref[...] = allowed_mask(adj_ref, pos_ref)

    for h in range(GROUP):
        lanes = slice(h * HS, (h + 1) * HS)
        query = q_ref[0, :, :, :, lanes].reshape(TOK, HS)
        keys = piece_rows(kv_refs, 0, lanes)
        values = piece_rows(kv_refs, 1, lanes)
        scores = dot(keys, query, ((1,), (1,))) * (HS**-0.5)
        masked = jnp.where(mask_ref[...] > 0.5, scores, -1e30)
        exponent = jnp.exp(masked - jnp.max(masked, axis=0, keepdims=True))
        prob = exponent / jnp.sum(exponent, axis=0, keepdims=True)
        prob_ref[h] = prob
        att = dot(prob.astype(jnp.bfloat16), values, ((0,), (0,)))
        att_ref[:, lanes] = att.astype(jnp.bfloat16)


def forward(adjacency, position, queries, pieces):
    inner = queries.shape[-1]
    width = GROUP * HS
    smem = pl.BlockSpec(memory_space=pltpu.SMEM)
    specs = [
        pl.BlockSpec(p.shape[:-1] + (width,), lambda g: (0, 0, 0, 0, g))
        for p in pieces
    ]
    return pl.pallas_call(
        forward_kernel,
        grid=(inner // width,),
        in_specs=[smem, smem, pl.BlockSpec(queries.shape[:-1] + (width,), lambda g: (0, 0, 0, 0, g))] + specs,
        out_specs=[
            pl.BlockSpec((TOK, width), lambda g: (0, g)),
            pl.BlockSpec((GROUP, KEYS, TOK), lambda g: (g, 0, 0)),
        ],
        out_shape=[
            jax.ShapeDtypeStruct((TOK, inner), jnp.bfloat16),
            jax.ShapeDtypeStruct((inner // HS, KEYS, TOK), jnp.float32),
        ],
        scratch_shapes=[pltpu.VMEM((KEYS, TOK), jnp.float32)],
        compiler_params=pltpu.CompilerParams(vmem_limit_bytes=VMEM_LIMIT),
        name="attend",
    )(adjacency, position, queries, *pieces)


def side_cols(pos_ref, side, cols):
    core = pos_ref[4]
    return pl.ds(pl.multiple_of((core if side == 0 else 1 - core) * cols, cols), cols)


def project_own_kernel(att_ref, w_hbm, part_ref, w_ref, sems):
    chunks = w_ref.shape[0]
    rows = w_ref.shape[1]
    copies = [pltpu.make_async_copy(w_hbm.at[pl.ds(k * rows, rows)], w_ref.at[k], sems.at[k]) for k in range(chunks)]
    for copy in copies:
        copy.start()
    total = None
    for k in range(chunks):
        copies[k].wait()
        term = dot(att_ref[:, k * rows : (k + 1) * rows], w_ref[k], ((1,), (0,)))
        total = term if total is None else total + term
    part_ref[...] = total


def project_own(att, own):
    vmem = pl.BlockSpec(memory_space=pltpu.VMEM)
    tokens = att.shape[0]
    inner, cols = own.shape
    chunks = 2
    return pl.pallas_call(
        project_own_kernel,
        in_specs=[vmem, pl.BlockSpec(memory_space=pl.ANY)],
        out_specs=vmem,
        out_shape=jax.ShapeDtypeStruct((tokens, cols), jnp.float32),
        scratch_shapes=[
            pltpu.VMEM((chunks, inner // chunks, cols), jnp.bfloat16),
            pltpu.SemaphoreType.DMA((chunks,)),
        ],
        compiler_params=pltpu.CompilerParams(vmem_limit_bytes=VMEM_LIMIT),
        name="project_own",
    )(att, own)


def project_kernel(
    bound_ref, pos_ref, att_ref, part_ref, own_hbm, swap_hbm, gain_ref, read_ref, cot_ref,
    pred_ref, ga_ref, swap_ref, own_ref, proj_ref, gp_ref, sems,
):
    chunks, rows, cols = swap_ref.shape
    copies = [pltpu.make_async_copy(swap_hbm.at[pl.ds(k * rows, rows)], swap_ref.at[k], sems.at[k]) for k in range(chunks)]
    own_copy = pltpu.make_async_copy(own_hbm, own_ref, sems.at[chunks])
    for copy in copies:
        copy.start()
    own_copy.start()
    total = None
    for k in range(chunks):
        copies[k].wait()
        term = dot(att_ref[:, k * rows : (k + 1) * rows], swap_ref[k], ((1,), (0,)))
        total = term if total is None else total + term
    proj_ref[:, side_cols(pos_ref, 0, cols)] = part_ref[...]
    proj_ref[:, side_cols(pos_ref, 1, cols)] = total
    inner = proj_ref.shape[1]
    for pair in range(TOK // (2 * BS)):
        rows_of = slice(pair * 2 * BS, (pair + 1) * 2 * BS)
        x = pair * 2 // BY
        y = pair * 2 % BY
        proj = proj_ref[rows_of, :]
        gain = gain_ref[...]
        flag = jnp.where(
            lax.broadcasted_iota(jnp.int32, (2 * BS, 1), 0) < BS, bound_ref[0, x, y], bound_ref[0, x, y + 1]
        ).astype(jnp.float32)
        cot = jnp.concatenate([cot_ref[0, x, y], cot_ref[0, x, y + 1]], axis=0) * flag
        inv_rms = lax.rsqrt(jnp.sum(proj * proj, axis=1, keepdims=True) * (1.0 / inner) + 1e-05)
        normed = proj * inv_rms * gain
        pred0 = jnp.sum(normed * read_ref[0:1, :], axis=1, keepdims=True) * flag
        pred1 = jnp.sum(normed * read_ref[1:2, :], axis=1, keepdims=True) * flag
        pred = jnp.where(lax.broadcasted_iota(jnp.int32, (2 * BS, 2), 1) == 0, pred0, pred1)
        pred_ref[0, x, y] = pred[:BS]
        pred_ref[0, x, y + 1] = pred[BS:]
        gained = (cot[:, 0:1] * read_ref[0:1, :] + cot[:, 1:2] * read_ref[1:2, :]) * gain
        inner_mean = jnp.sum(gained * proj, axis=1, keepdims=True) * (1.0 / inner)
        gp_ref[rows_of, :] = (inv_rms * gained - proj * (inv_rms * inv_rms * inv_rms * inner_mean)).astype(jnp.bfloat16)
    gp_own = gp_ref[:, side_cols(pos_ref, 0, cols)]
    gp_swap = gp_ref[:, side_cols(pos_ref, 1, cols)]
    own_copy.wait()
    for k in range(chunks):
        lanes = slice(k * rows, (k + 1) * rows)
        total = dot(gp_swap, swap_ref[k], ((1,), (1,))) + dot(gp_own, own_ref[lanes, :], ((1,), (1,)))
        ga_ref[:, lanes] = total.astype(jnp.bfloat16)


def project(boundary, position, att, part, own, swapped, gain, read_rows, cotangent):
    vmem = pl.BlockSpec(memory_space=pltpu.VMEM)
    smem = pl.BlockSpec(memory_space=pltpu.SMEM)
    hbm = pl.BlockSpec(memory_space=pl.ANY)
    inner, cols = own.shape
    chunks = 4
    return pl.pallas_call(
        project_kernel,
        in_specs=[smem, smem, vmem, vmem, hbm, hbm, vmem, vmem, vmem],
        out_specs=[vmem, vmem],
        out_shape=[
            jax.ShapeDtypeStruct(cotangent.shape, jnp.float32),
            jax.ShapeDtypeStruct(att.shape, jnp.bfloat16),
        ],
        scratch_shapes=[
            pltpu.VMEM((chunks, inner // chunks, cols), jnp.bfloat16),
            pltpu.VMEM(own.shape, jnp.bfloat16),
            pltpu.VMEM(att.shape, jnp.float32),
            pltpu.VMEM(att.shape, jnp.bfloat16),
            pltpu.SemaphoreType.DMA((chunks + 1,)),
        ],
        compiler_params=pltpu.CompilerParams(vmem_limit_bytes=VMEM_LIMIT),
        name="project",
    )(boundary, position, att, part, own, swapped, gain, read_rows, cotangent)


def backward_kernel(q_ref, ga_ref, prob_ref, *rest):
    count = len(PIECES)
    kv_refs = rest[:count]
    gq_ref = rest[count]
    gkv_refs = rest[count + 1 :]
    for h in range(GROUP):
        lanes = slice(h * HS, (h + 1) * HS)
        query = q_ref[0, :, :, :, lanes].reshape(TOK, HS)
        keys = piece_rows(kv_refs, 0, lanes)
        values = piece_rows(kv_refs, 1, lanes)
        grad_att = ga_ref[:, lanes]
        prob = prob_ref[h]
        grad_prob = dot(values, grad_att, ((1,), (1,)))
        inner_sum = jnp.sum(prob * grad_prob, axis=0, keepdims=True)
        grad_scores = (prob * (grad_prob - inner_sum) * (HS**-0.5)).astype(jnp.bfloat16)
        grad_query = dot(grad_scores, keys, ((0,), (0,)))
        gq_ref[0, :, :, :, lanes] = grad_query.reshape(BX, BY, BS, HS).astype(gq_ref.dtype)
        grads = (dot(grad_scores, query, ((1,), (0,))), dot(prob.astype(jnp.bfloat16), grad_att, ((1,), (0,))))
        for which, grad in enumerate(grads):
            start = 0
            for ref in gkv_refs:
                shape = ref.shape[1:4]
                rows = shape[0] * shape[1] * shape[2]
                ref[which, :, :, :, lanes] = grad[start : start + rows].reshape(shape + (HS,)).astype(ref.dtype)
                start += rows


def backward(queries, grad_att, prob, pieces):
    inner = queries.shape[-1]
    width = GROUP * HS

    def wide(shape):
        return pl.BlockSpec(tuple(shape[:-1]) + (width,), lambda g: (0,) * (len(shape) - 1) + (g,))

    shapes = [p.shape for p in pieces]
    blocks, rest = shapes[0], shapes[0][3:]
    sums = [blocks, (2, 1, BY + 2) + rest, (2, 1, BY + 2) + rest, shapes[-1], shapes[-1]]
    return pl.pallas_call(
        backward_kernel,
        grid=(inner // width,),
        in_specs=[wide(queries.shape), wide(grad_att.shape), pl.BlockSpec((GROUP, KEYS, TOK), lambda g: (g, 0, 0))]
        + [wide(s) for s in shapes],
        out_specs=[wide(queries.shape)] + [wide(s) for s in sums],
        out_shape=[jax.ShapeDtypeStruct(queries.shape, jnp.bfloat16)]
        + [jax.ShapeDtypeStruct(s, jnp.float32 if i == 0 else jnp.bfloat16) for i, s in enumerate(sums)],
        compiler_params=pltpu.CompilerParams(vmem_limit_bytes=VMEM_LIMIT),
        name="attend_back",
    )(queries, grad_att, prob, *pieces)


def sides_kernel(from_low_ref, from_high_ref, low_ref, high_ref, left_ref, right_ref):
    f32 = jnp.float32
    for which in range(2):
        for y, rim, out in ((0, low_ref, left_ref), (1, high_ref, right_ref)):
            first = rim[which, 0, 0].astype(f32) + from_low_ref[which, 0, y].astype(f32)
            last = rim[which, BX - 1, 0].astype(f32) + from_high_ref[which, 0, y].astype(f32)
            out[which, 0, 0] = first.astype(out.dtype)
            out[which, BX - 1, 0] = last.astype(out.dtype)


def sides(from_low, from_high, low, high):
    corner = pl.BlockSpec(from_low.shape[:2] + (2,) + from_low.shape[3:], lambda i: (0, 0, BY // 2, 0, 0))
    rim = pl.BlockSpec(low.shape, lambda i: (0, 0, 0, 0, 0))
    shape = jax.ShapeDtypeStruct(low.shape, low.dtype)
    return pl.pallas_call(
        sides_kernel,
        grid=(1,),
        in_specs=[corner, corner, rim, rim],
        out_specs=[rim, rim],
        out_shape=[shape, shape],
        compiler_params=pltpu.CompilerParams(vmem_limit_bytes=SMALL_LIMIT),
        name="sides",
    )(from_low, from_high, low, high)


def add_rows_kernel(own_ref, low_ref, high_ref, out_ref, edge_ref):
    f32 = jnp.float32
    for which in range(2):
        for x in range(BX):
            for y in range(BY):
                total = own_ref[which, x, y]
                if x == 0:
                    total = total + low_ref[which, 0, y].astype(f32)
                if x == BX - 1:
                    total = total + high_ref[which, 0, y].astype(f32)
                if y in (0, BY - 1):
                    edge_ref[which, x, y // (BY - 1)] = total
                else:
                    out_ref[which, x, y] = total.astype(out_ref.dtype)


def add_rows(own, low, high):
    inner = own.shape[-1]
    width = inner // 4

    def wide(shape):
        return pl.BlockSpec(tuple(shape[:-1]) + (width,), lambda g: (0, 0, 0, 0, g))

    edge = own.shape[:2] + (2,) + own.shape[3:]
    return pl.pallas_call(
        add_rows_kernel,
        grid=(inner // width,),
        in_specs=[wide(own.shape), wide(low.shape), wide(high.shape)],
        out_specs=[wide(own.shape), wide(edge)],
        out_shape=[jax.ShapeDtypeStruct(own.shape, jnp.bfloat16), jax.ShapeDtypeStruct(edge, jnp.float32)],
        compiler_params=pltpu.CompilerParams(vmem_limit_bytes=SMALL_LIMIT),
        name="add_rows",
    )(own, low, high)


def add_columns_kernel(edge_ref, low_ref, high_ref, partial_hbm, out_ref):
    del partial_hbm
    first = pl.program_id(0) == 0

    @pl.when(first)
    def _():
        out_ref[...] = (edge_ref[...] + low_ref[...].astype(jnp.float32)).astype(out_ref.dtype)

    @pl.when(jnp.logical_not(first))
    def _():
        out_ref[...] = (edge_ref[...] + high_ref[...].astype(jnp.float32)).astype(out_ref.dtype)


def add_columns(edge, low, high, partial):
    block = edge.shape[:2] + (1,) + edge.shape[3:]
    whole = pl.BlockSpec(block, lambda i: (0, 0, 0, 0, 0))
    return pl.pallas_call(
        add_columns_kernel,
        grid=(2,),
        in_specs=[
            pl.BlockSpec(block, lambda i: (0, 0, i, 0, 0)),
            whole,
            whole,
            pl.BlockSpec(memory_space=pl.ANY),
        ],
        out_specs=pl.BlockSpec(block, lambda i: (0, 0, i * (BY - 1), 0, 0)),
        out_shape=jax.ShapeDtypeStruct(partial.shape, partial.dtype),
        input_output_aliases={3: 0},
        compiler_params=pltpu.CompilerParams(vmem_limit_bytes=SMALL_LIMIT),
        name="add_columns",
    )(edge, low, high, partial)


def swap_cores(value):
    return lax.ppermute(value, "sx", [(i, i ^ 1) for i in range(lax.axis_size("sx"))])


def body(queries, keys_values, out_weight, gain, read_weight, adjacency, boundary, cotangent):
    size_x, size_y = queries.shape[1:3]
    inner = out_weight.shape[1]
    n_sx, n_sy, n_wa = (lax.axis_size(axis) for axis in ("sx", "sy", "wa"))
    row, column, case = (lax.axis_index(axis) for axis in ("sx", "sy", "wa"))
    core = row % 2
    kv = keys_values[:, 0]
    cols = inner // 2
    slab = lax.dynamic_slice_in_dim(out_weight, core * cols, cols, axis=1)
    pairs = [[w, w + 1] for w in range(0, n_wa, 2)]
    rings = [list(range(h, n_wa, 2)) for h in range(2)]
    both = lax.all_gather(slab, "wa", axis=0, axis_index_groups=pairs)
    own_cols = lax.all_gather(both, "wa", axis=0, axis_index_groups=rings).reshape(-1, cols)
    ylow = shift(kv[:, :, size_y - 1 :], "sy", 1)
    yhigh = shift(kv[:, :, :1], "sy", -1)
    xlow = shift(kv[:, size_x - 1 :], "sx", 1)
    xhigh = shift(kv[:, :1], "sx", -1)
    clow = shift(jnp.concatenate([ylow[:, size_x - 1 :], yhigh[:, size_x - 1 :]], axis=2), "sx", 1)
    chigh = shift(jnp.concatenate([ylow[:, :1], yhigh[:, :1]], axis=2), "sx", -1)
    pieces = (kv, xlow, clow, xhigh, chigh, ylow, yhigh)
    position = jnp.stack(
        [
            row * size_x,
            column * size_y,
            jnp.int32(size_x * n_sx),
            jnp.int32(size_y * n_sy),
            core,
        ]
    ).astype(jnp.int32)
    att, prob = forward(adjacency, position, queries, pieces)
    own_cols, att = lax.optimization_barrier((own_cols, att))
    swapped = swap_cores(own_cols)
    part = project_own(att, own_cols)
    prediction, grad_att = project(
        boundary, position, att, part, own_cols, swapped, gain[None], read_weight.T, cotangent
    )
    grad_queries, own, gxlow, gxhigh, gylow, gyhigh = backward(queries, grad_att, prob, pieces)
    from_low = shift(gxhigh, "sx", 1)
    from_high = shift(gxlow, "sx", -1)
    to_left, to_right = sides(from_low, from_high, gylow, gyhigh)
    left = shift(to_right, "sy", 1)
    right = shift(to_left, "sy", -1)
    partial, edge = add_rows(own, from_low, from_high)
    grad_kv = add_columns(edge, left, right, partial)
    return (prediction, grad_queries, grad_kv[:, None])


def solution(mesh):
    return jax.shard_map(
        body,
        mesh=mesh,
        in_specs=(
            P("wa", "sx", "sy", None, None),
            P(None, "wa", "sx", "sy", None, None),
            P("wa", None),
            P(),
            P(),
            P("wa", "sx", "sy", None),
            P("wa", "sx", "sy"),
            P("wa", "sx", "sy", None, None),
        ),
        out_specs=(
            P("wa", "sx", "sy", None, None),
            P("wa", "sx", "sy", None, None),
            P(None, "wa", "sx", "sy", None, None),
        ),
        check_vma=False,
    )
```

```python
import jax
import jax.numpy as jnp
from jax import lax
from jax.experimental import pallas as pl
from jax.experimental.pallas import tpu as pltpu
from jax.sharding import PartitionSpec as P

HS = 128
BS = 16
BX = 2
BY = 4
TOK = BX * BY * BS
GROUP = 4
VMEM_LIMIT = 60 * 1024 * 1024
SMALL_LIMIT = 24 * 1024 * 1024

LOCAL = [(x, y) for x in range(BX) for y in range(BY)]
XLOW = [(-1, y) for y in range(BY)]
XHIGH = [(BX, y) for y in range(BY)]
YLOW = [(x, -1) for x in range(BX)]
YHIGH = [(x, BY) for x in range(BX)]
CLOW = [(-1, -1), (-1, BY)]
CHIGH = [(BX, -1), (BX, BY)]
PIECES = [LOCAL, XLOW, CLOW, XHIGH, CHIGH, YLOW, YHIGH]
KEY_BLOCKS = [block for piece in PIECES for block in piece]
KEYS = len(KEY_BLOCKS) * BS


def shift(value, axis, step):
    count = lax.axis_size(axis)
    pairs = [(i, i + step) for i in range(count) if 0 <= i + step < count]
    return lax.ppermute(value, axis, pairs)


def dot(a, b, dims):
    return lax.dot_general(a, b, (dims, ((), ())), preferred_element_type=jnp.float32)


def piece_rows(refs, which, lanes):
    parts = []
    for ref in refs:
        blocks = ref[which, :, :, :, lanes]
        parts.append(blocks.reshape(-1, HS))
    return jnp.concatenate(parts, axis=0)


def allowed_mask(adj_ref, pos_ref):
    lane = lax.broadcasted_iota(jnp.int32, (1, TOK), 1)
    block = lane // BS
    bx = block // BY
    by = block % BY
    entries = []
    for e in range(4):
        vec = jnp.zeros((1, TOK), jnp.int32)
        for b in range(BX * BY):
            vec = jnp.where(block == b, adj_ref[0, b // BY, b % BY, e], vec)
        entries.append(vec)
    rows = []
    for kx, ky in KEY_BLOCKS:
        dx = kx - bx
        dy = ky - by
        near = (jnp.abs(dx) <= 1) & (jnp.abs(dy) <= 1)
        code = 3 * (dx + 1) + dy + 1
        entry = code - (code > 4).astype(jnp.int32)
        listed = code == 4
        for vec in entries:
            listed = listed | ((vec == entry) & (code != 4))
        gx = pos_ref[0] + kx
        gy = pos_ref[1] + ky
        inside = (gx >= 0) & (gx < pos_ref[2]) & (gy >= 0) & (gy < pos_ref[3])
        flag = jnp.where(near & listed, 1.0, 0.0) * jnp.where(inside, 1.0, 0.0)
        rows.append(jnp.broadcast_to(flag, (BS, TOK)))
    return jnp.concatenate(rows, axis=0)


def forward_kernel(adj_ref, pos_ref, q_ref, *rest):
    kv_refs = rest[: len(PIECES)]
    att_ref, prob_ref, mask_ref = rest[len(PIECES) :]

    @pl.when(pl.program_id(0) == 0)
    def _():
        mask_ref[...] = allowed_mask(adj_ref, pos_ref)

    for h in range(GROUP):
        lanes = slice(h * HS, (h + 1) * HS)
        query = q_ref[0, :, :, :, lanes].reshape(TOK, HS)
        keys = piece_rows(kv_refs, 0, lanes)
        values = piece_rows(kv_refs, 1, lanes)
        scores = dot(keys, query, ((1,), (1,))) * (HS**-0.5)
        masked = jnp.where(mask_ref[...] > 0.5, scores, -1e30)
        exponent = jnp.exp(masked - jnp.max(masked, axis=0, keepdims=True))
        prob = exponent / jnp.sum(exponent, axis=0, keepdims=True)
        prob_ref[h] = prob
        att = dot(prob.astype(jnp.bfloat16), values, ((0,), (0,)))
        att_ref[:, lanes] = att.astype(jnp.bfloat16)


def forward(adjacency, position, queries, pieces):
    inner = queries.shape[-1]
    width = GROUP * HS
    smem = pl.BlockSpec(memory_space=pltpu.SMEM)
    specs = [
        pl.BlockSpec(p.shape[:-1] + (width,), lambda g: (0, 0, 0, 0, g))
        for p in pieces
    ]
    return pl.pallas_call(
        forward_kernel,
        grid=(inner // width,),
        in_specs=[smem, smem, pl.BlockSpec(queries.shape[:-1] + (width,), lambda g: (0, 0, 0, 0, g))] + specs,
        out_specs=[
            pl.BlockSpec((TOK, width), lambda g: (0, g)),
            pl.BlockSpec((GROUP, KEYS, TOK), lambda g: (g, 0, 0)),
        ],
        out_shape=[
            jax.ShapeDtypeStruct((TOK, inner), jnp.bfloat16),
            jax.ShapeDtypeStruct((inner // HS, KEYS, TOK), jnp.float32),
        ],
        scratch_shapes=[pltpu.VMEM((KEYS, TOK), jnp.float32)],
        compiler_params=pltpu.CompilerParams(vmem_limit_bytes=VMEM_LIMIT),
        name="attend",
    )(adjacency, position, queries, *pieces)


def side_cols(pos_ref, side, cols):
    core = pos_ref[4]
    return pl.ds(pl.multiple_of((core if side == 0 else 1 - core) * cols, cols), cols)


def project_own_kernel(att_ref, w_hbm, part_ref, w_ref, sems):
    chunks = w_ref.shape[0]
    rows = w_ref.shape[1]
    copies = [pltpu.make_async_copy(w_hbm.at[pl.ds(k * rows, rows)], w_ref.at[k], sems.at[k]) for k in range(chunks)]
    for copy in copies:
        copy.start()
    total = None
    for k in range(chunks):
        copies[k].wait()
        term = dot(att_ref[:, k * rows : (k + 1) * rows], w_ref[k], ((1,), (0,)))
        total = term if total is None else total + term
    part_ref[...] = total


def project_own(att, own):
    vmem = pl.BlockSpec(memory_space=pltpu.VMEM)
    tokens = att.shape[0]
    inner, cols = own.shape
    chunks = 2
    return pl.pallas_call(
        project_own_kernel,
        in_specs=[vmem, pl.BlockSpec(memory_space=pl.ANY)],
        out_specs=vmem,
        out_shape=jax.ShapeDtypeStruct((tokens, cols), jnp.float32),
        scratch_shapes=[
            pltpu.VMEM((chunks, inner // chunks, cols), jnp.bfloat16),
            pltpu.SemaphoreType.DMA((chunks,)),
        ],
        compiler_params=pltpu.CompilerParams(vmem_limit_bytes=VMEM_LIMIT),
        name="project_own",
    )(att, own)


def project_kernel(
    bound_ref, pos_ref, att_ref, part_ref, own_hbm, swap_hbm, gain_ref, read_ref, cot_ref,
    pred_ref, ga_ref, swap_ref, own_ref, proj_ref, gp_ref, sems,
):
    chunks, rows, cols = swap_ref.shape
    copies = [pltpu.make_async_copy(swap_hbm.at[pl.ds(k * rows, rows)], swap_ref.at[k], sems.at[k]) for k in range(chunks)]
    own_copy = pltpu.make_async_copy(own_hbm, own_ref, sems.at[chunks])
    for copy in copies:
        copy.start()
    own_copy.start()
    total = None
    for k in range(chunks):
        copies[k].wait()
        term = dot(att_ref[:, k * rows : (k + 1) * rows], swap_ref[k], ((1,), (0,)))
        total = term if total is None else total + term
    proj_ref[:, side_cols(pos_ref, 0, cols)] = part_ref[...]
    proj_ref[:, side_cols(pos_ref, 1, cols)] = total
    inner = proj_ref.shape[1]
    for pair in range(TOK // (2 * BS)):
        rows_of = slice(pair * 2 * BS, (pair + 1) * 2 * BS)
        x = pair * 2 // BY
        y = pair * 2 % BY
        proj = proj_ref[rows_of, :]
        gain = gain_ref[...]
        flag = jnp.where(
            lax.broadcasted_iota(jnp.int32, (2 * BS, 1), 0) < BS, bound_ref[0, x, y], bound_ref[0, x, y + 1]
        ).astype(jnp.float32)
        cot = jnp.concatenate([cot_ref[0, x, y], cot_ref[0, x, y + 1]], axis=0) * flag
        inv_rms = lax.rsqrt(jnp.sum(proj * proj, axis=1, keepdims=True) * (1.0 / inner) + 1e-05)
        normed = proj * inv_rms * gain
        pred0 = jnp.sum(normed * read_ref[0:1, :], axis=1, keepdims=True) * flag
        pred1 = jnp.sum(normed * read_ref[1:2, :], axis=1, keepdims=True) * flag
        pred = jnp.where(lax.broadcasted_iota(jnp.int32, (2 * BS, 2), 1) == 0, pred0, pred1)
        pred_ref[0, x, y] = pred[:BS]
        pred_ref[0, x, y + 1] = pred[BS:]
        gained = (cot[:, 0:1] * read_ref[0:1, :] + cot[:, 1:2] * read_ref[1:2, :]) * gain
        inner_mean = jnp.sum(gained * proj, axis=1, keepdims=True) * (1.0 / inner)
        gp_ref[rows_of, :] = (inv_rms * gained - proj * (inv_rms * inv_rms * inv_rms * inner_mean)).astype(jnp.bfloat16)
    gp_own = gp_ref[:, side_cols(pos_ref, 0, cols)]
    gp_swap = gp_ref[:, side_cols(pos_ref, 1, cols)]
    own_copy.wait()
    for k in range(chunks):
        lanes = slice(k * rows, (k + 1) * rows)
        total = dot(gp_swap, swap_ref[k], ((1,), (1,))) + dot(gp_own, own_ref[lanes, :], ((1,), (1,)))
        ga_ref[:, lanes] = total.astype(jnp.bfloat16)


def project(boundary, position, att, part, own, swapped, gain, read_rows, cotangent):
    vmem = pl.BlockSpec(memory_space=pltpu.VMEM)
    smem = pl.BlockSpec(memory_space=pltpu.SMEM)
    hbm = pl.BlockSpec(memory_space=pl.ANY)
    inner, cols = own.shape
    chunks = 4
    return pl.pallas_call(
        project_kernel,
        in_specs=[smem, smem, vmem, vmem, hbm, hbm, vmem, vmem, vmem],
        out_specs=[vmem, vmem],
        out_shape=[
            jax.ShapeDtypeStruct(cotangent.shape, jnp.float32),
            jax.ShapeDtypeStruct(att.shape, jnp.bfloat16),
        ],
        scratch_shapes=[
            pltpu.VMEM((chunks, inner // chunks, cols), jnp.bfloat16),
            pltpu.VMEM(own.shape, jnp.bfloat16),
            pltpu.VMEM(att.shape, jnp.float32),
            pltpu.VMEM(att.shape, jnp.bfloat16),
            pltpu.SemaphoreType.DMA((chunks + 1,)),
        ],
        compiler_params=pltpu.CompilerParams(vmem_limit_bytes=VMEM_LIMIT),
        name="project",
    )(boundary, position, att, part, own, swapped, gain, read_rows, cotangent)


def value_rows(refs, lanes):
    return jnp.concatenate([ref[0, :, :, :, lanes].reshape(-1, HS) for ref in refs], axis=0)


def back_rim_kernel(q_ref, ga_ref, prob_ref, *rest):
    count = len(PIECES)
    v_refs = rest[:count]
    gs_ref = rest[count]
    rim_refs = rest[count + 1 :]
    for h in range(GROUP):
        lanes = slice(h * HS, (h + 1) * HS)
        query = q_ref[0, :, :, :, lanes].reshape(TOK, HS)
        values = value_rows(v_refs, lanes)
        grad_att = ga_ref[:, lanes]
        prob = prob_ref[h]
        grad_prob = dot(values, grad_att, ((1,), (1,)))
        inner_sum = jnp.sum(prob * grad_prob, axis=0, keepdims=True)
        grad_scores = (prob * (grad_prob - inner_sum) * (HS**-0.5)).astype(jnp.bfloat16)
        gs_ref[h] = grad_scores
        half = prob[TOK:].astype(jnp.bfloat16)
        grads = (dot(grad_scores[TOK:], query, ((1,), (0,))), dot(half, grad_att, ((1,), (0,))))
        for which, grad in enumerate(grads):
            start = 0
            for ref in rim_refs:
                shape = ref.shape[1:4]
                rows = shape[0] * shape[1] * shape[2]
                ref[which, :, :, :, lanes] = grad[start : start + rows].reshape(shape + (HS,)).astype(ref.dtype)
                start += rows


def lane_block(shape, width):
    return pl.BlockSpec(tuple(shape[:-1]) + (width,), lambda g: (0,) * (len(shape) - 1) + (g,))


def half_block(shape, which, width):
    return pl.BlockSpec((1,) + tuple(shape[1:-1]) + (width,), lambda g: (which,) + (0,) * (len(shape) - 2) + (g,))


def back_rim(queries, grad_att, prob, pieces):
    inner = queries.shape[-1]
    width = GROUP * HS
    shapes = [p.shape for p in pieces]
    heads = pl.BlockSpec((GROUP, KEYS, TOK), lambda g: (g, 0, 0))
    return pl.pallas_call(
        back_rim_kernel,
        grid=(inner // width,),
        in_specs=[lane_block(queries.shape, width), lane_block(grad_att.shape, width), heads]
        + [half_block(s, 1, width) for s in shapes],
        out_specs=[heads] + [lane_block(s, width) for s in shapes[1:]],
        out_shape=[jax.ShapeDtypeStruct(prob.shape, jnp.bfloat16)]
        + [jax.ShapeDtypeStruct(s, jnp.bfloat16) for s in shapes[1:]],
        compiler_params=pltpu.CompilerParams(vmem_limit_bytes=VMEM_LIMIT),
        name="back_rim",
    )(queries, grad_att, prob, *pieces)


def back_own_kernel(q_ref, ga_ref, prob_ref, gs_ref, *rest):
    count = len(PIECES)
    k_refs = rest[:count]
    gq_ref, own_ref = rest[count:]
    for h in range(GROUP):
        lanes = slice(h * HS, (h + 1) * HS)
        query = q_ref[0, :, :, :, lanes].reshape(TOK, HS)
        grad_scores = gs_ref[h]
        grad_query = dot(grad_scores, value_rows(k_refs, lanes), ((0,), (0,)))
        gq_ref[0, :, :, :, lanes] = grad_query.reshape(BX, BY, BS, HS).astype(gq_ref.dtype)
        own_ref[0, :, :, :, lanes] = dot(grad_scores[:TOK], query, ((1,), (0,))).reshape(BX, BY, BS, HS)
        half = prob_ref[h].astype(jnp.bfloat16)
        own_ref[1, :, :, :, lanes] = dot(half, ga_ref[:, lanes], ((1,), (0,))).reshape(BX, BY, BS, HS)


def back_own(queries, grad_att, prob, grad_scores, pieces):
    inner = queries.shape[-1]
    width = GROUP * HS
    shapes = [p.shape for p in pieces]
    return pl.pallas_call(
        back_own_kernel,
        grid=(inner // width,),
        in_specs=[
            lane_block(queries.shape, width),
            lane_block(grad_att.shape, width),
            pl.BlockSpec((GROUP, TOK, TOK), lambda g: (g, 0, 0)),
            pl.BlockSpec((GROUP, KEYS, TOK), lambda g: (g, 0, 0)),
        ]
        + [half_block(s, 0, width) for s in shapes],
        out_specs=[lane_block(queries.shape, width), lane_block(shapes[0], width)],
        out_shape=[
            jax.ShapeDtypeStruct(queries.shape, jnp.bfloat16),
            jax.ShapeDtypeStruct(shapes[0], jnp.float32),
        ],
        compiler_params=pltpu.CompilerParams(vmem_limit_bytes=VMEM_LIMIT),
        name="back_own",
    )(queries, grad_att, prob, grad_scores, *pieces)


def sides_kernel(from_low_ref, from_high_ref, low_ref, high_ref, left_ref, right_ref):
    f32 = jnp.float32
    for which in range(2):
        for y, rim, out in ((0, low_ref, left_ref), (1, high_ref, right_ref)):
            first = rim[which, 0, 0].astype(f32) + from_low_ref[which, 0, y].astype(f32)
            last = rim[which, BX - 1, 0].astype(f32) + from_high_ref[which, 0, y].astype(f32)
            out[which, 0, 0] = first.astype(out.dtype)
            out[which, BX - 1, 0] = last.astype(out.dtype)


def sides(from_low, from_high, low, high):
    corner = pl.BlockSpec(from_low.shape, lambda i: (0, 0, 0, 0, 0))
    rim = pl.BlockSpec(low.shape, lambda i: (0, 0, 0, 0, 0))
    shape = jax.ShapeDtypeStruct(low.shape, low.dtype)
    return pl.pallas_call(
        sides_kernel,
        grid=(1,),
        in_specs=[corner, corner, rim, rim],
        out_specs=[rim, rim],
        out_shape=[shape, shape],
        compiler_params=pltpu.CompilerParams(vmem_limit_bytes=SMALL_LIMIT),
        name="sides",
    )(from_low, from_high, low, high)


def add_rows_kernel(own_ref, low_ref, high_ref, out_ref, edge_ref):
    f32 = jnp.float32
    for which in range(2):
        for x in range(BX):
            for y in range(BY):
                total = own_ref[which, x, y]
                if x == 0:
                    total = total + low_ref[which, 0, y].astype(f32)
                if x == BX - 1:
                    total = total + high_ref[which, 0, y].astype(f32)
                if y in (0, BY - 1):
                    edge_ref[which, x, y // (BY - 1)] = total
                else:
                    out_ref[which, x, y] = total.astype(out_ref.dtype)


def add_rows(own, low, high):
    inner = own.shape[-1]
    width = inner // 4

    def wide(shape):
        return pl.BlockSpec(tuple(shape[:-1]) + (width,), lambda g: (0, 0, 0, 0, g))

    edge = own.shape[:2] + (2,) + own.shape[3:]
    return pl.pallas_call(
        add_rows_kernel,
        grid=(inner // width,),
        in_specs=[wide(own.shape), wide(low.shape), wide(high.shape)],
        out_specs=[wide(own.shape), wide(edge)],
        out_shape=[jax.ShapeDtypeStruct(own.shape, jnp.bfloat16), jax.ShapeDtypeStruct(edge, jnp.float32)],
        compiler_params=pltpu.CompilerParams(vmem_limit_bytes=SMALL_LIMIT),
        name="add_rows",
    )(own, low, high)


def add_columns_kernel(edge_ref, low_ref, high_ref, partial_hbm, out_ref):
    del partial_hbm
    first = pl.program_id(0) == 0

    @pl.when(first)
    def _():
        out_ref[...] = (edge_ref[...] + low_ref[...].astype(jnp.float32)).astype(out_ref.dtype)

    @pl.when(jnp.logical_not(first))
    def _():
        out_ref[...] = (edge_ref[...] + high_ref[...].astype(jnp.float32)).astype(out_ref.dtype)


def add_columns(edge, low, high, partial):
    block = edge.shape[:2] + (1,) + edge.shape[3:]
    whole = pl.BlockSpec(block, lambda i: (0, 0, 0, 0, 0))
    return pl.pallas_call(
        add_columns_kernel,
        grid=(2,),
        in_specs=[
            pl.BlockSpec(block, lambda i: (0, 0, i, 0, 0)),
            whole,
            whole,
            pl.BlockSpec(memory_space=pl.ANY),
        ],
        out_specs=pl.BlockSpec(block, lambda i: (0, 0, i * (BY - 1), 0, 0)),
        out_shape=jax.ShapeDtypeStruct(partial.shape, partial.dtype),
        input_output_aliases={3: 0},
        compiler_params=pltpu.CompilerParams(vmem_limit_bytes=SMALL_LIMIT),
        name="add_columns",
    )(edge, low, high, partial)


def swap_cores(value):
    return lax.ppermute(value, "sx", [(i, i ^ 1) for i in range(lax.axis_size("sx"))])


def body(queries, keys_values, out_weight, gain, read_weight, adjacency, boundary, cotangent):
    size_x, size_y = queries.shape[1:3]
    inner = out_weight.shape[1]
    n_sx, n_sy, n_wa = (lax.axis_size(axis) for axis in ("sx", "sy", "wa"))
    row, column, case = (lax.axis_index(axis) for axis in ("sx", "sy", "wa"))
    core = row % 2
    kv = keys_values[:, 0]
    cols = inner // 2
    slab = lax.dynamic_slice_in_dim(out_weight, core * cols, cols, axis=1)
    pairs = [[w, w + 1] for w in range(0, n_wa, 2)]
    rings = [list(range(h, n_wa, 2)) for h in range(2)]
    both = lax.all_gather(slab, "wa", axis=0, axis_index_groups=pairs)
    own_cols = lax.all_gather(both, "wa", axis=0, axis_index_groups=rings).reshape(-1, cols)
    ylow = shift(kv[:, :, size_y - 1 :], "sy", 1)
    yhigh = shift(kv[:, :, :1], "sy", -1)
    xlow = shift(kv[:, size_x - 1 :], "sx", 1)
    xhigh = shift(kv[:, :1], "sx", -1)
    clow = shift(jnp.concatenate([ylow[:, size_x - 1 :], yhigh[:, size_x - 1 :]], axis=2), "sx", 1)
    chigh = shift(jnp.concatenate([ylow[:, :1], yhigh[:, :1]], axis=2), "sx", -1)
    pieces = (kv, xlow, clow, xhigh, chigh, ylow, yhigh)
    position = jnp.stack(
        [
            row * size_x,
            column * size_y,
            jnp.int32(size_x * n_sx),
            jnp.int32(size_y * n_sy),
            core,
        ]
    ).astype(jnp.int32)
    att, prob = forward(adjacency, position, queries, pieces)
    own_cols, att = lax.optimization_barrier((own_cols, att))
    swapped = swap_cores(own_cols)
    part = project_own(att, own_cols)
    prediction, grad_att = project(
        boundary, position, att, part, own_cols, swapped, gain[None], read_weight.T, cotangent
    )
    grad_scores, gxlow, gclow, gxhigh, gchigh, gylow, gyhigh = back_rim(queries, grad_att, prob, pieces)
    corner_low = shift(gchigh, "sx", 1)
    corner_high = shift(gclow, "sx", -1)
    from_low = shift(gxhigh, "sx", 1)
    from_high = shift(gxlow, "sx", -1)
    grad_queries, own = back_own(queries, grad_att, prob, grad_scores, pieces)
    to_left, to_right = sides(corner_low, corner_high, gylow, gyhigh)
    left = shift(to_right, "sy", 1)
    right = shift(to_left, "sy", -1)
    partial, edge = add_rows(own, from_low, from_high)
    grad_kv = add_columns(edge, left, right, partial)
    return (prediction, grad_queries, grad_kv[:, None])


def solution(mesh):
    return jax.shard_map(
        body,
        mesh=mesh,
        in_specs=(
            P("wa", "sx", "sy", None, None),
            P(None, "wa", "sx", "sy", None, None),
            P("wa", None),
            P(),
            P(),
            P("wa", "sx", "sy", None),
            P("wa", "sx", "sy"),
            P("wa", "sx", "sy", None, None),
        ),
        out_specs=(
            P("wa", "sx", "sy", None, None),
            P("wa", "sx", "sy", None, None),
            P(None, "wa", "sx", "sy", None, None),
        ),
        check_vma=False,
    )
```

```python
import jax
import jax.numpy as jnp
from jax import lax
from jax.experimental import pallas as pl
from jax.experimental.pallas import tpu as pltpu
from jax.sharding import PartitionSpec as P

HS = 128
BS = 16
BX = 2
BY = 4
TOK = BX * BY * BS
GROUP = 4
VMEM_LIMIT = 60 * 1024 * 1024
SMALL_LIMIT = 12 * 1024 * 1024
OWN_LIMIT = 57 * 1024 * 1024

LOCAL = [(x, y) for x in range(BX) for y in range(BY)]
XLOW = [(-1, y) for y in range(BY)]
XHIGH = [(BX, y) for y in range(BY)]
YLOW = [(x, -1) for x in range(BX)]
YHIGH = [(x, BY) for x in range(BX)]
CLOW = [(-1, -1), (-1, BY)]
CHIGH = [(BX, -1), (BX, BY)]
PIECES = [LOCAL, XLOW, CLOW, XHIGH, CHIGH, YLOW, YHIGH]
KEY_BLOCKS = [block for piece in PIECES for block in piece]
KEYS = len(KEY_BLOCKS) * BS


def shift(value, axis, step):
    count = lax.axis_size(axis)
    pairs = [(i, i + step) for i in range(count) if 0 <= i + step < count]
    return lax.ppermute(value, axis, pairs)


def dot(a, b, dims):
    return lax.dot_general(a, b, (dims, ((), ())), preferred_element_type=jnp.float32)


def piece_rows(refs, which, lanes):
    parts = []
    for ref in refs:
        blocks = ref[which, :, :, :, lanes]
        parts.append(blocks.reshape(-1, HS))
    return jnp.concatenate(parts, axis=0)


def allowed_mask(adj_ref, pos_ref):
    lane = lax.broadcasted_iota(jnp.int32, (1, TOK), 1)
    block = lane // BS
    bx = block // BY
    by = block % BY
    entries = []
    for e in range(4):
        vec = jnp.zeros((1, TOK), jnp.int32)
        for b in range(BX * BY):
            vec = jnp.where(block == b, adj_ref[0, b // BY, b % BY, e], vec)
        entries.append(vec)
    rows = []
    for kx, ky in KEY_BLOCKS:
        dx = kx - bx
        dy = ky - by
        near = (jnp.abs(dx) <= 1) & (jnp.abs(dy) <= 1)
        code = 3 * (dx + 1) + dy + 1
        entry = code - (code > 4).astype(jnp.int32)
        listed = code == 4
        for vec in entries:
            listed = listed | ((vec == entry) & (code != 4))
        gx = pos_ref[0] + kx
        gy = pos_ref[1] + ky
        inside = (gx >= 0) & (gx < pos_ref[2]) & (gy >= 0) & (gy < pos_ref[3])
        flag = jnp.where(near & listed, 1.0, 0.0) * jnp.where(inside, 1.0, 0.0)
        rows.append(jnp.broadcast_to(flag, (BS, TOK)))
    return jnp.concatenate(rows, axis=0)


def forward_kernel(adj_ref, pos_ref, q_ref, *rest):
    kv_refs = rest[: len(PIECES)]
    att_ref, prob_ref, mask_ref = rest[len(PIECES) :]

    @pl.when(pl.program_id(0) == 0)
    def _():
        mask_ref[...] = allowed_mask(adj_ref, pos_ref)

    for h in range(GROUP):
        lanes = slice(h * HS, (h + 1) * HS)
        query = q_ref[0, :, :, :, lanes].reshape(TOK, HS)
        keys = piece_rows(kv_refs, 0, lanes)
        values = piece_rows(kv_refs, 1, lanes)
        scores = dot(keys, query, ((1,), (1,))) * (HS**-0.5)
        masked = jnp.where(mask_ref[...] > 0.5, scores, -1e30)
        exponent = jnp.exp(masked - jnp.max(masked, axis=0, keepdims=True))
        prob = exponent / jnp.sum(exponent, axis=0, keepdims=True)
        prob_ref[h] = prob
        att = dot(prob.astype(jnp.bfloat16), values, ((0,), (0,)))
        att_ref[:, lanes] = att.astype(jnp.bfloat16)


def forward(adjacency, position, queries, pieces):
    inner = queries.shape[-1]
    width = GROUP * HS
    smem = pl.BlockSpec(memory_space=pltpu.SMEM)
    specs = [
        pl.BlockSpec(p.shape[:-1] + (width,), lambda g: (0, 0, 0, 0, g))
        for p in pieces
    ]
    return pl.pallas_call(
        forward_kernel,
        grid=(inner // width,),
        in_specs=[smem, smem, pl.BlockSpec(queries.shape[:-1] + (width,), lambda g: (0, 0, 0, 0, g))] + specs,
        out_specs=[
            pl.BlockSpec((TOK, width), lambda g: (0, g)),
            pl.BlockSpec((GROUP, KEYS, TOK), lambda g: (g, 0, 0)),
        ],
        out_shape=[
            jax.ShapeDtypeStruct((TOK, inner), jnp.bfloat16),
            jax.ShapeDtypeStruct((inner // HS, KEYS, TOK), jnp.float32),
        ],
        scratch_shapes=[pltpu.VMEM((KEYS, TOK), jnp.float32)],
        compiler_params=pltpu.CompilerParams(vmem_limit_bytes=VMEM_LIMIT),
        name="attend",
    )(adjacency, position, queries, *pieces)


def side_cols(pos_ref, side, cols):
    core = pos_ref[4]
    return pl.ds(pl.multiple_of((core if side == 0 else 1 - core) * cols, cols), cols)


def project_own_kernel(att_ref, w_hbm, part_ref, w_ref, sems):
    chunks = w_ref.shape[0]
    rows = w_ref.shape[1]
    copies = [pltpu.make_async_copy(w_hbm.at[pl.ds(k * rows, rows)], w_ref.at[k], sems.at[k]) for k in range(chunks)]
    for copy in copies:
        copy.start()
    total = None
    for k in range(chunks):
        copies[k].wait()
        term = dot(att_ref[:, k * rows : (k + 1) * rows], w_ref[k], ((1,), (0,)))
        total = term if total is None else total + term
    part_ref[...] = total


def project_own(att, own):
    vmem = pl.BlockSpec(memory_space=pltpu.VMEM)
    tokens = att.shape[0]
    inner, cols = own.shape
    chunks = 4
    return pl.pallas_call(
        project_own_kernel,
        in_specs=[vmem, pl.BlockSpec(memory_space=pl.ANY)],
        out_specs=vmem,
        out_shape=jax.ShapeDtypeStruct((tokens, cols), jnp.float32),
        scratch_shapes=[
            pltpu.VMEM((chunks, inner // chunks, cols), jnp.bfloat16),
            pltpu.SemaphoreType.DMA((chunks,)),
        ],
        compiler_params=pltpu.CompilerParams(vmem_limit_bytes=VMEM_LIMIT),
        name="project_own",
    )(att, own)


def project_kernel(
    bound_ref, pos_ref, att_ref, part_ref, own_hbm, swap_hbm, gain_ref, read_ref, cot_ref,
    pred_ref, ga_ref, swap_ref, own_ref, proj_ref, gp_ref, sems,
):
    chunks, rows, cols = swap_ref.shape
    copies = [pltpu.make_async_copy(swap_hbm.at[pl.ds(k * rows, rows)], swap_ref.at[k], sems.at[k]) for k in range(chunks)]
    own_copy = pltpu.make_async_copy(own_hbm, own_ref, sems.at[chunks])
    for copy in copies:
        copy.start()
    own_copy.start()
    total = None
    for k in range(chunks):
        copies[k].wait()
        term = dot(att_ref[:, k * rows : (k + 1) * rows], swap_ref[k], ((1,), (0,)))
        total = term if total is None else total + term
    proj_ref[:, side_cols(pos_ref, 0, cols)] = part_ref[...]
    proj_ref[:, side_cols(pos_ref, 1, cols)] = total
    inner = proj_ref.shape[1]
    for pair in range(TOK // (2 * BS)):
        rows_of = slice(pair * 2 * BS, (pair + 1) * 2 * BS)
        x = pair * 2 // BY
        y = pair * 2 % BY
        proj = proj_ref[rows_of, :]
        gain = gain_ref[...]
        flag = jnp.where(
            lax.broadcasted_iota(jnp.int32, (2 * BS, 1), 0) < BS, bound_ref[0, x, y], bound_ref[0, x, y + 1]
        ).astype(jnp.float32)
        cot = jnp.concatenate([cot_ref[0, x, y], cot_ref[0, x, y + 1]], axis=0) * flag
        inv_rms = lax.rsqrt(jnp.sum(proj * proj, axis=1, keepdims=True) * (1.0 / inner) + 1e-05)
        normed = proj * inv_rms * gain
        pred0 = jnp.sum(normed * read_ref[0:1, :], axis=1, keepdims=True) * flag
        pred1 = jnp.sum(normed * read_ref[1:2, :], axis=1, keepdims=True) * flag
        pred = jnp.where(lax.broadcasted_iota(jnp.int32, (2 * BS, HS), 1) == 0, pred0, pred1).T
        pred_ref[0, x, y] = pred[:2, :BS]
        pred_ref[0, x, y + 1] = pred[:2, BS:]
        gained = (cot[:, 0:1] * read_ref[0:1, :] + cot[:, 1:2] * read_ref[1:2, :]) * gain
        inner_mean = jnp.sum(gained * proj, axis=1, keepdims=True) * (1.0 / inner)
        gp_ref[rows_of, :] = (inv_rms * gained - proj * (inv_rms * inv_rms * inv_rms * inner_mean)).astype(jnp.bfloat16)
    gp_own = gp_ref[:, side_cols(pos_ref, 0, cols)]
    gp_swap = gp_ref[:, side_cols(pos_ref, 1, cols)]
    own_copy.wait()
    for k in range(chunks):
        lanes = slice(k * rows, (k + 1) * rows)
        total = dot(gp_swap, swap_ref[k], ((1,), (1,))) + dot(gp_own, own_ref[lanes, :], ((1,), (1,)))
        ga_ref[:, lanes] = total.astype(jnp.bfloat16)


def project(boundary, position, att, part, own, swapped, gain, read_rows, cotangent):
    vmem = pl.BlockSpec(memory_space=pltpu.VMEM)
    smem = pl.BlockSpec(memory_space=pltpu.SMEM)
    hbm = pl.BlockSpec(memory_space=pl.ANY)
    inner, cols = own.shape
    chunks = 4
    return pl.pallas_call(
        project_kernel,
        in_specs=[smem, smem, vmem, vmem, hbm, hbm, vmem, vmem, vmem],
        out_specs=[vmem, vmem],
        out_shape=[
            jax.ShapeDtypeStruct(cotangent.shape[:3] + (2, BS), jnp.float32),
            jax.ShapeDtypeStruct(att.shape, jnp.bfloat16),
        ],
        scratch_shapes=[
            pltpu.VMEM((chunks, inner // chunks, cols), jnp.bfloat16),
            pltpu.VMEM(own.shape, jnp.bfloat16),
            pltpu.VMEM(att.shape, jnp.float32),
            pltpu.VMEM(att.shape, jnp.bfloat16),
            pltpu.SemaphoreType.DMA((chunks + 1,)),
        ],
        compiler_params=pltpu.CompilerParams(vmem_limit_bytes=VMEM_LIMIT),
        name="project",
    )(boundary, position, att, part, own, swapped, gain, read_rows, cotangent)


def value_rows(refs, lanes):
    return jnp.concatenate([ref[0, :, :, :, lanes].reshape(-1, HS) for ref in refs], axis=0)


def back_rim_kernel(q_ref, ga_ref, prob_ref, *rest):
    count = len(PIECES)
    v_refs = rest[:count]
    gs_ref = rest[count]
    rim_refs = rest[count + 1 :]
    for h in range(GROUP):
        lanes = slice(h * HS, (h + 1) * HS)
        query = q_ref[0, :, :, :, lanes].reshape(TOK, HS)
        values = value_rows(v_refs, lanes)
        grad_att = ga_ref[:, lanes]
        prob = prob_ref[h]
        grad_prob = dot(values, grad_att, ((1,), (1,)))
        inner_sum = jnp.sum(prob * grad_prob, axis=0, keepdims=True)
        grad_scores = (prob * (grad_prob - inner_sum) * (HS**-0.5)).astype(jnp.bfloat16)
        gs_ref[h] = grad_scores
        half = prob[TOK:].astype(jnp.bfloat16)
        grads = (dot(grad_scores[TOK:], query, ((1,), (0,))), dot(half, grad_att, ((1,), (0,))))
        for which, grad in enumerate(grads):
            start = 0
            for ref in rim_refs:
                shape = ref.shape[1:4]
                rows = shape[0] * shape[1] * shape[2]
                ref[which, :, :, :, lanes] = grad[start : start + rows].reshape(shape + (HS,)).astype(ref.dtype)
                start += rows


def lane_block(shape, width):
    return pl.BlockSpec(tuple(shape[:-1]) + (width,), lambda g: (0,) * (len(shape) - 1) + (g,))


def half_block(shape, which, width):
    return pl.BlockSpec((1,) + tuple(shape[1:-1]) + (width,), lambda g: (which,) + (0,) * (len(shape) - 2) + (g,))


def back_rim(queries, grad_att, prob, pieces):
    inner = queries.shape[-1]
    width = GROUP * HS
    shapes = [p.shape for p in pieces]
    heads = pl.BlockSpec((GROUP, KEYS, TOK), lambda g: (g, 0, 0))
    return pl.pallas_call(
        back_rim_kernel,
        grid=(inner // width,),
        in_specs=[lane_block(queries.shape, width), lane_block(grad_att.shape, width), heads]
        + [half_block(s, 1, width) for s in shapes],
        out_specs=[heads] + [lane_block(s, width) for s in shapes[1:]],
        out_shape=[jax.ShapeDtypeStruct(prob.shape, jnp.bfloat16)]
        + [jax.ShapeDtypeStruct(s, jnp.bfloat16) for s in shapes[1:]],
        compiler_params=pltpu.CompilerParams(vmem_limit_bytes=VMEM_LIMIT),
        name="back_rim",
    )(queries, grad_att, prob, *pieces)


def back_own_kernel(q_ref, ga_ref, prob_ref, gs_ref, *rest):
    count = len(PIECES)
    k_refs = rest[:count]
    low_ref, high_ref, gq_ref, out_ref, edge_ref = rest[count:]
    for h in range(GROUP):
        lanes = slice(h * HS, (h + 1) * HS)
        query = q_ref[0, :, :, :, lanes].reshape(TOK, HS)
        grad_scores = gs_ref[h]
        grad_query = dot(grad_scores, value_rows(k_refs, lanes), ((0,), (0,)))
        gq_ref[0, :, :, :, lanes] = grad_query.reshape(BX, BY, BS, HS).astype(gq_ref.dtype)
        half = prob_ref[h].astype(jnp.bfloat16)
        grads = (dot(grad_scores[:TOK], query, ((1,), (0,))), dot(half, ga_ref[:, lanes], ((1,), (0,))))
        for which, grad in enumerate(grads):
            for block, (x, y) in enumerate(LOCAL):
                total = grad[block * BS : (block + 1) * BS]
                if x == 0:
                    total = total + low_ref[which, 0, y, :, lanes].astype(jnp.float32)
                if x == BX - 1:
                    total = total + high_ref[which, 0, y, :, lanes].astype(jnp.float32)
                if y in (0, BY - 1):
                    edge_ref[which, x, y // (BY - 1), :, lanes] = total
                else:
                    out_ref[which, x, y, :, lanes] = total.astype(out_ref.dtype)


def back_own(queries, grad_att, prob, grad_scores, pieces, low, high):
    inner = queries.shape[-1]
    width = GROUP * HS
    shapes = [p.shape for p in pieces]
    edge = shapes[0][:2] + (2,) + shapes[0][3:]
    return pl.pallas_call(
        back_own_kernel,
        grid=(inner // width,),
        in_specs=[
            lane_block(queries.shape, width),
            lane_block(grad_att.shape, width),
            pl.BlockSpec((GROUP, TOK, TOK), lambda g: (g, 0, 0)),
            pl.BlockSpec((GROUP, KEYS, TOK), lambda g: (g, 0, 0)),
        ]
        + [half_block(s, 0, width) for s in shapes]
        + [lane_block(low.shape, width), lane_block(high.shape, width)],
        out_specs=[lane_block(queries.shape, width), lane_block(shapes[0], width), lane_block(edge, width)],
        out_shape=[
            jax.ShapeDtypeStruct(queries.shape, jnp.bfloat16),
            jax.ShapeDtypeStruct(shapes[0], jnp.bfloat16),
            jax.ShapeDtypeStruct(edge, jnp.float32),
        ],
        compiler_params=pltpu.CompilerParams(vmem_limit_bytes=OWN_LIMIT),
        name="back_own",
    )(
        queries,
        grad_att,
        prob,
        grad_scores,
        *pieces,
        *(pltpu.with_memory_space_constraint(term, pltpu.VMEM) for term in (low, high)),
    )


def sides_kernel(from_low_ref, from_high_ref, low_hbm, high_hbm, left_ref, right_ref, rim_ref, sems):
    f32 = jnp.float32
    copies = [
        pltpu.make_async_copy(low_hbm, rim_ref.at[0], sems.at[0]),
        pltpu.make_async_copy(high_hbm, rim_ref.at[1], sems.at[1]),
    ]
    for copy in copies:
        copy.start()
    for y, out in ((0, left_ref), (1, right_ref)):
        copies[y].wait()
        for which in range(2):
            first = rim_ref[y, which, 0, 0].astype(f32) + from_low_ref[which, 0, y].astype(f32)
            last = rim_ref[y, which, BX - 1, 0].astype(f32) + from_high_ref[which, 0, y].astype(f32)
            out[which, 0, 0] = first.astype(out.dtype)
            out[which, BX - 1, 0] = last.astype(out.dtype)


def sides(from_low, from_high, low, high):
    vmem = pl.BlockSpec(memory_space=pltpu.VMEM)
    hbm = pl.BlockSpec(memory_space=pltpu.HBM)
    shape = jax.ShapeDtypeStruct(low.shape, low.dtype)
    return pl.pallas_call(
        sides_kernel,
        in_specs=[vmem, vmem, hbm, hbm],
        out_specs=[vmem, vmem],
        out_shape=[shape, shape],
        scratch_shapes=[pltpu.VMEM((2,) + low.shape, low.dtype), pltpu.SemaphoreType.DMA((2,))],
        compiler_params=pltpu.CompilerParams(vmem_limit_bytes=SMALL_LIMIT),
        name="sides",
    )(from_low, from_high, *(pltpu.with_memory_space_constraint(rim, pltpu.HBM) for rim in (low, high)))


def add_columns_kernel(low_ref, high_ref, edge_hbm, partial_hbm, out_hbm, edge_ref, sum_ref, sems):
    del partial_hbm
    loads = [pltpu.make_async_copy(edge_hbm.at[i], edge_ref.at[i], sems.at[i]) for i in range(2)]
    for load in loads:
        load.start()
    stores = []
    for which in range(2):
        loads[which].wait()
        for side, ref in enumerate((low_ref, high_ref)):
            for x in range(BX):
                total = edge_ref[which, x, side] + ref[which, x, 0].astype(jnp.float32)
                sum_ref[which, side, x] = total.astype(sum_ref.dtype)
                y = side * (BY - 1)
                index = (which * 2 + side) * BX + x
                store = pltpu.make_async_copy(
                    sum_ref.at[which, side, x], out_hbm.at[which, x, y], sems.at[2 + index]
                )
                store.start()
                stores.append(store)
    for store in stores:
        store.wait()


def add_columns(edge, low, high, partial):
    vmem = pl.BlockSpec(memory_space=pltpu.VMEM)
    hbm = pl.BlockSpec(memory_space=pltpu.HBM)
    return pl.pallas_call(
        add_columns_kernel,
        in_specs=[vmem, vmem, hbm, hbm],
        out_specs=hbm,
        out_shape=jax.ShapeDtypeStruct(partial.shape, partial.dtype),
        scratch_shapes=[
            pltpu.VMEM(edge.shape, jnp.float32),
            pltpu.VMEM((2, 2, BX) + edge.shape[3:], partial.dtype),
            pltpu.SemaphoreType.DMA((2 + 4 * BX,)),
        ],
        input_output_aliases={3: 0},
        compiler_params=pltpu.CompilerParams(vmem_limit_bytes=SMALL_LIMIT),
        name="add_columns",
    )(low, high, *(pltpu.with_memory_space_constraint(term, pltpu.HBM) for term in (edge, partial)))


def swap_cores(value):
    return lax.ppermute(value, "sx", [(i, i ^ 1) for i in range(lax.axis_size("sx"))])


def body(queries, keys_values, out_weight, gain, read_weight, adjacency, boundary, cotangent):
    size_x, size_y = queries.shape[1:3]
    inner = out_weight.shape[1]
    n_sx, n_sy, n_wa = (lax.axis_size(axis) for axis in ("sx", "sy", "wa"))
    row, column, case = (lax.axis_index(axis) for axis in ("sx", "sy", "wa"))
    core = row % 2
    kv = keys_values[:, 0]
    cols = inner // 2
    slab = lax.dynamic_slice_in_dim(out_weight, core * cols, cols, axis=1)
    pairs = [[w, w + 1] for w in range(0, n_wa, 2)]
    rings = [list(range(h, n_wa, 2)) for h in range(2)]
    both = lax.all_gather(slab, "wa", axis=0, axis_index_groups=pairs)
    own_cols = lax.all_gather(both, "wa", axis=0, axis_index_groups=rings).reshape(-1, cols)
    ylow = shift(kv[:, :, size_y - 1 :], "sy", 1)
    yhigh = shift(kv[:, :, :1], "sy", -1)
    xlow = shift(kv[:, size_x - 1 :], "sx", 1)
    xhigh = shift(kv[:, :1], "sx", -1)
    clow = shift(jnp.concatenate([ylow[:, size_x - 1 :], yhigh[:, size_x - 1 :]], axis=2), "sx", 1)
    chigh = shift(jnp.concatenate([ylow[:, :1], yhigh[:, :1]], axis=2), "sx", -1)
    pieces = (kv, xlow, clow, xhigh, chigh, ylow, yhigh)
    position = jnp.stack(
        [
            row * size_x,
            column * size_y,
            jnp.int32(size_x * n_sx),
            jnp.int32(size_y * n_sy),
            core,
        ]
    ).astype(jnp.int32)
    att, prob = forward(adjacency, position, queries, pieces)
    own_cols, att = lax.optimization_barrier((own_cols, att))
    swapped = swap_cores(own_cols)
    part = project_own(att, own_cols)
    prediction, grad_att = project(
        boundary, position, att, part, own_cols, swapped, gain[None], read_weight.T, cotangent
    )
    grad_scores, gxlow, gclow, gxhigh, gchigh, gylow, gyhigh = back_rim(queries, grad_att, prob, pieces)
    corner_low = shift(gchigh, "sx", 1)
    corner_high = shift(gclow, "sx", -1)
    from_low = shift(gxhigh, "sx", 1)
    from_high = shift(gxlow, "sx", -1)
    grad_queries, partial, edge = back_own(queries, grad_att, prob, grad_scores, pieces, from_low, from_high)
    to_left, to_right = sides(corner_low, corner_high, gylow, gyhigh)
    left = shift(to_right, "sy", 1)
    right = shift(to_left, "sy", -1)
    grad_kv = add_columns(edge, left, right, partial)
    return (jnp.swapaxes(prediction, 3, 4), grad_queries, grad_kv[:, None])


def solution(mesh):
    return jax.shard_map(
        body,
        mesh=mesh,
        in_specs=(
            P("wa", "sx", "sy", None, None),
            P(None, "wa", "sx", "sy", None, None),
            P("wa", None),
            P(),
            P(),
            P("wa", "sx", "sy", None),
            P("wa", "sx", "sy"),
            P("wa", "sx", "sy", None, None),
        ),
        out_specs=(
            P("wa", "sx", "sy", None, None),
            P("wa", "sx", "sy", None, None),
            P(None, "wa", "sx", "sy", None, None),
        ),
        check_vma=False,
    )
```

```python
import jax
import jax.numpy as jnp
from jax import lax
from jax.experimental import pallas as pl
from jax.experimental.pallas import tpu as pltpu
from jax.sharding import PartitionSpec as P

HS = 128
BS = 16
BX = 2
BY = 4
TOK = BX * BY * BS
GROUP = 4
VMEM_LIMIT = 24 * 1024 * 1024
SMALL_LIMIT = 12 * 1024 * 1024

LOCAL = [(x, y) for x in range(BX) for y in range(BY)]
XLOW = [(-1, y) for y in range(BY)]
XHIGH = [(BX, y) for y in range(BY)]
YLOW = [(x, -1) for x in range(BX)]
YHIGH = [(x, BY) for x in range(BX)]
CLOW = [(-1, -1), (-1, BY)]
CHIGH = [(BX, -1), (BX, BY)]
PIECES = [LOCAL, XLOW, CLOW, XHIGH, CHIGH, YLOW, YHIGH]
KEY_BLOCKS = [block for piece in PIECES for block in piece]
KEYS = len(KEY_BLOCKS) * BS


def shift(value, axis, step):
    count = lax.axis_size(axis)
    pairs = [(i, i + step) for i in range(count) if 0 <= i + step < count]
    return lax.ppermute(value, axis, pairs)


def in_vmem(*values):
    return tuple(pltpu.with_memory_space_constraint(value, pltpu.VMEM) for value in values)


def dot(a, b, dims):
    return lax.dot_general(a, b, (dims, ((), ())), preferred_element_type=jnp.float32)


def piece_rows(refs, which, lanes):
    parts = []
    for ref in refs:
        blocks = ref[which, :, :, :, lanes]
        parts.append(blocks.reshape(-1, HS))
    return jnp.concatenate(parts, axis=0)


def allowed_mask(adj_ref, pos_ref):
    lane = lax.broadcasted_iota(jnp.int32, (1, TOK), 1)
    block = lane // BS
    bx = block // BY
    by = block % BY
    entries = []
    for e in range(4):
        vec = jnp.zeros((1, TOK), jnp.int32)
        for b in range(BX * BY):
            vec = jnp.where(block == b, adj_ref[0, b // BY, b % BY, e], vec)
        entries.append(vec)
    rows = []
    for kx, ky in KEY_BLOCKS:
        dx = kx - bx
        dy = ky - by
        near = (jnp.abs(dx) <= 1) & (jnp.abs(dy) <= 1)
        code = 3 * (dx + 1) + dy + 1
        entry = code - (code > 4).astype(jnp.int32)
        listed = code == 4
        for vec in entries:
            listed = listed | ((vec == entry) & (code != 4))
        gx = pos_ref[0] + kx
        gy = pos_ref[1] + ky
        inside = (gx >= 0) & (gx < pos_ref[2]) & (gy >= 0) & (gy < pos_ref[3])
        flag = jnp.where(near & listed, 1.0, 0.0) * jnp.where(inside, 1.0, 0.0)
        rows.append(jnp.broadcast_to(flag, (BS, TOK)))
    return jnp.concatenate(rows, axis=0)


def forward_kernel(adj_ref, pos_ref, q_ref, *rest):
    kv_refs = rest[: len(PIECES)]
    att_ref, prob_ref, mask_ref = rest[len(PIECES) :]

    @pl.when(pl.program_id(0) == 0)
    def _():
        mask_ref[...] = allowed_mask(adj_ref, pos_ref)

    for h in range(GROUP):
        lanes = slice(h * HS, (h + 1) * HS)
        query = q_ref[0, :, :, :, lanes].reshape(TOK, HS)
        keys = piece_rows(kv_refs, 0, lanes)
        values = piece_rows(kv_refs, 1, lanes)
        scores = dot(keys, query, ((1,), (1,))) * (HS**-0.5)
        masked = jnp.where(mask_ref[...] > 0.5, scores, -1e30)
        exponent = jnp.exp(masked - jnp.max(masked, axis=0, keepdims=True))
        prob = exponent / jnp.sum(exponent, axis=0, keepdims=True)
        prob_ref[h] = prob
        att = dot(prob.astype(jnp.bfloat16), values, ((0,), (0,)))
        att_ref[:, lanes] = att.astype(jnp.bfloat16)


def forward(adjacency, position, queries, pieces):
    inner = queries.shape[-1]
    width = GROUP * HS
    smem = pl.BlockSpec(memory_space=pltpu.SMEM)
    specs = [
        pl.BlockSpec(p.shape[:-1] + (width,), lambda g: (0, 0, 0, 0, g))
        for p in pieces
    ]
    return pl.pallas_call(
        forward_kernel,
        grid=(inner // width,),
        in_specs=[smem, smem, pl.BlockSpec(queries.shape[:-1] + (width,), lambda g: (0, 0, 0, 0, g))] + specs,
        out_specs=[
            pl.BlockSpec((TOK, width), lambda g: (0, g)),
            pl.BlockSpec((GROUP, KEYS, TOK), lambda g: (g, 0, 0)),
        ],
        out_shape=[
            jax.ShapeDtypeStruct((TOK, inner), jnp.bfloat16),
            jax.ShapeDtypeStruct((inner // HS, KEYS, TOK), jnp.float32),
        ],
        scratch_shapes=[pltpu.VMEM((KEYS, TOK), jnp.float32)],
        compiler_params=pltpu.CompilerParams(vmem_limit_bytes=VMEM_LIMIT),
        name="attend",
    )(adjacency, position, queries, *pieces)


def side_cols(pos_ref, side, cols):
    core = pos_ref[4]
    return pl.ds(pl.multiple_of((core if side == 0 else 1 - core) * cols, cols), cols)


def project_own_kernel(att_ref, w_hbm, part_ref, w_ref, sems):
    chunks = 4
    rows = w_ref.shape[0] // chunks
    parts = [pl.ds(k * rows, rows) for k in range(chunks)]
    copies = [pltpu.make_async_copy(w_hbm.at[part], w_ref.at[part], sems.at[k]) for k, part in enumerate(parts)]
    for copy in copies:
        copy.start()
    total = None
    for k in range(chunks):
        copies[k].wait()
        lanes = slice(k * rows, (k + 1) * rows)
        term = dot(att_ref[:, lanes], w_ref[lanes, :], ((1,), (0,)))
        total = term if total is None else total + term
    part_ref[...] = total


def project_own(att, own):
    vmem = pl.BlockSpec(memory_space=pltpu.VMEM)
    tokens = att.shape[0]
    cols = own.shape[1]
    return pl.pallas_call(
        project_own_kernel,
        in_specs=[vmem, pl.BlockSpec(memory_space=pl.ANY)],
        out_specs=[vmem, vmem],
        out_shape=[jax.ShapeDtypeStruct((tokens, cols), jnp.float32), jax.ShapeDtypeStruct(own.shape, own.dtype)],
        scratch_shapes=[pltpu.SemaphoreType.DMA((4,))],
        compiler_params=pltpu.CompilerParams(vmem_limit_bytes=VMEM_LIMIT),
        name="project_own",
    )(att, pltpu.with_memory_space_constraint(own, pltpu.HBM))


def project_kernel(
    bound_ref, pos_ref, att_ref, part_ref, own_ref, swap_hbm, gain_ref, read_ref, cot_ref,
    pred_ref, ga_ref, swap_ref, proj_ref, gp_ref, sems,
):
    cols = swap_ref.shape[1]
    chunks = 4
    rows = swap_ref.shape[0] // chunks
    parts = [pl.ds(k * rows, rows) for k in range(chunks)]
    copies = [pltpu.make_async_copy(swap_hbm.at[part], swap_ref.at[part], sems.at[k]) for k, part in enumerate(parts)]
    for copy in copies:
        copy.start()
    total = None
    for k in range(chunks):
        copies[k].wait()
        lanes = slice(k * rows, (k + 1) * rows)
        term = dot(att_ref[:, lanes], swap_ref[lanes, :], ((1,), (0,)))
        total = term if total is None else total + term
    proj_ref[:, side_cols(pos_ref, 0, cols)] = part_ref[...]
    proj_ref[:, side_cols(pos_ref, 1, cols)] = total
    inner = proj_ref.shape[1]
    for pair in range(TOK // (2 * BS)):
        rows_of = slice(pair * 2 * BS, (pair + 1) * 2 * BS)
        x = pair * 2 // BY
        y = pair * 2 % BY
        proj = proj_ref[rows_of, :]
        gain = gain_ref[...]
        flag = jnp.where(
            lax.broadcasted_iota(jnp.int32, (2 * BS, 1), 0) < BS, bound_ref[0, x, y], bound_ref[0, x, y + 1]
        ).astype(jnp.float32)
        cot = jnp.concatenate([cot_ref[0, x, y], cot_ref[0, x, y + 1]], axis=0) * flag
        inv_rms = lax.rsqrt(jnp.sum(proj * proj, axis=1, keepdims=True) * (1.0 / inner) + 1e-05)
        normed = proj * inv_rms * gain
        pred0 = jnp.sum(normed * read_ref[0:1, :], axis=1, keepdims=True) * flag
        pred1 = jnp.sum(normed * read_ref[1:2, :], axis=1, keepdims=True) * flag
        pred = jnp.where(lax.broadcasted_iota(jnp.int32, (2 * BS, HS), 1) == 0, pred0, pred1).T
        pred_ref[0, x, y] = pred[:2, :BS]
        pred_ref[0, x, y + 1] = pred[:2, BS:]
        gained = (cot[:, 0:1] * read_ref[0:1, :] + cot[:, 1:2] * read_ref[1:2, :]) * gain
        inner_mean = jnp.sum(gained * proj, axis=1, keepdims=True) * (1.0 / inner)
        gp_ref[rows_of, :] = (inv_rms * gained - proj * (inv_rms * inv_rms * inv_rms * inner_mean)).astype(jnp.bfloat16)
    gp_own = gp_ref[:, side_cols(pos_ref, 0, cols)]
    gp_swap = gp_ref[:, side_cols(pos_ref, 1, cols)]
    for k in range(chunks):
        lanes = slice(k * rows, (k + 1) * rows)
        total = dot(gp_swap, swap_ref[lanes, :], ((1,), (1,))) + dot(gp_own, own_ref[lanes, :], ((1,), (1,)))
        ga_ref[:, lanes] = total.astype(jnp.bfloat16)


def project(boundary, position, att, part, own, swapped, gain, read_rows, cotangent):
    vmem = pl.BlockSpec(memory_space=pltpu.VMEM)
    smem = pl.BlockSpec(memory_space=pltpu.SMEM)
    return pl.pallas_call(
        project_kernel,
        in_specs=[smem, smem, vmem, vmem, vmem, pl.BlockSpec(memory_space=pl.ANY), vmem, vmem, vmem],
        out_specs=[vmem, vmem],
        out_shape=[
            jax.ShapeDtypeStruct(cotangent.shape[:3] + (2, BS), jnp.float32),
            jax.ShapeDtypeStruct(att.shape, jnp.bfloat16),
        ],
        scratch_shapes=[
            pltpu.VMEM(swapped.shape, jnp.bfloat16),
            pltpu.VMEM(att.shape, jnp.float32),
            pltpu.VMEM(att.shape, jnp.bfloat16),
            pltpu.SemaphoreType.DMA((4,)),
        ],
        compiler_params=pltpu.CompilerParams(vmem_limit_bytes=VMEM_LIMIT),
        name="project",
    )(
        boundary,
        position,
        *in_vmem(att, part, own),
        pltpu.with_memory_space_constraint(swapped, pltpu.HBM),
        gain,
        read_rows,
        cotangent,
    )


def kv_rows(refs, which, lanes):
    return jnp.concatenate([ref[which, :, :, :, lanes].reshape(-1, HS) for ref in refs], axis=0)


def back_rim_kernel(q_ref, ga_ref, prob_ref, *rest):
    count = len(PIECES)
    v_refs = rest[:count]
    gs_ref = rest[count]
    rim_refs = rest[count + 1 :]
    for h in range(prob_ref.shape[0]):
        lanes = slice(h * HS, (h + 1) * HS)
        query = q_ref[0, :, :, :, lanes].reshape(TOK, HS)
        values = kv_rows(v_refs, 1, lanes)
        grad_att = ga_ref[:, lanes]
        prob = prob_ref[h]
        grad_prob = dot(values, grad_att, ((1,), (1,)))
        inner_sum = jnp.sum(prob * grad_prob, axis=0, keepdims=True)
        grad_scores = (prob * (grad_prob - inner_sum) * (HS**-0.5)).astype(jnp.bfloat16)
        gs_ref[h] = grad_scores
        half = prob[TOK:].astype(jnp.bfloat16)
        grads = (dot(grad_scores[TOK:], query, ((1,), (0,))), dot(half, grad_att, ((1,), (0,))))
        for which, grad in enumerate(grads):
            start = 0
            for ref in rim_refs:
                shape = ref.shape[1:4]
                rows = shape[0] * shape[1] * shape[2]
                ref[which, :, :, :, lanes] = grad[start : start + rows].reshape(shape + (HS,)).astype(ref.dtype)
                start += rows


def back_rim(queries, grad_att, prob, pieces):
    vmem = pl.BlockSpec(memory_space=pltpu.VMEM)
    shapes = [p.shape for p in pieces]
    return pl.pallas_call(
        back_rim_kernel,
        in_specs=[vmem] * (3 + len(pieces)),
        out_specs=[vmem] * len(pieces),
        out_shape=[jax.ShapeDtypeStruct(prob.shape, jnp.bfloat16)]
        + [jax.ShapeDtypeStruct(s, jnp.bfloat16) for s in shapes[1:]],
        compiler_params=pltpu.CompilerParams(vmem_limit_bytes=VMEM_LIMIT),
        name="back_rim",
    )(*in_vmem(queries, grad_att, prob, *pieces))


def back_own_kernel(q_ref, ga_ref, prob_ref, gs_ref, *rest):
    count = len(PIECES)
    k_refs = rest[:count]
    low_ref, high_ref, gq_ref, out_ref, edge_ref = rest[count:]
    for h in range(prob_ref.shape[0]):
        lanes = slice(h * HS, (h + 1) * HS)
        query = q_ref[0, :, :, :, lanes].reshape(TOK, HS)
        grad_scores = gs_ref[h]
        grad_query = dot(grad_scores, kv_rows(k_refs, 0, lanes), ((0,), (0,)))
        gq_ref[0, :, :, :, lanes] = grad_query.reshape(BX, BY, BS, HS).astype(gq_ref.dtype)
        half = prob_ref[h, :TOK, :].astype(jnp.bfloat16)
        grads = (dot(grad_scores[:TOK], query, ((1,), (0,))), dot(half, ga_ref[:, lanes], ((1,), (0,))))
        for which, grad in enumerate(grads):
            for block, (x, y) in enumerate(LOCAL):
                total = grad[block * BS : (block + 1) * BS]
                if x == 0:
                    total = total + low_ref[which, 0, y, :, lanes].astype(jnp.float32)
                if x == BX - 1:
                    total = total + high_ref[which, 0, y, :, lanes].astype(jnp.float32)
                if y in (0, BY - 1):
                    edge_ref[which, x, y // (BY - 1), :, lanes] = total
                else:
                    out_ref[which, x, y, :, lanes] = total.astype(out_ref.dtype)


def back_own(queries, grad_att, prob, grad_scores, pieces, low, high):
    vmem = pl.BlockSpec(memory_space=pltpu.VMEM)
    own = pieces[0].shape
    edge = own[:2] + (2,) + own[3:]
    return pl.pallas_call(
        back_own_kernel,
        in_specs=[vmem] * (6 + len(pieces)),
        out_specs=[vmem] * 3,
        out_shape=[
            jax.ShapeDtypeStruct(queries.shape, jnp.bfloat16),
            jax.ShapeDtypeStruct(own, jnp.bfloat16),
            jax.ShapeDtypeStruct(edge, jnp.float32),
        ],
        compiler_params=pltpu.CompilerParams(vmem_limit_bytes=VMEM_LIMIT),
        name="back_own",
    )(*in_vmem(queries, grad_att, prob, grad_scores, *pieces, low, high))


def sides_kernel(from_low_ref, from_high_ref, low_ref, high_ref, left_ref, right_ref):
    f32 = jnp.float32
    for y, rim, out in ((0, low_ref, left_ref), (1, high_ref, right_ref)):
        for which in range(2):
            first = rim[which, 0, 0].astype(f32) + from_low_ref[which, 0, y].astype(f32)
            last = rim[which, BX - 1, 0].astype(f32) + from_high_ref[which, 0, y].astype(f32)
            out[which, 0, 0] = first.astype(out.dtype)
            out[which, BX - 1, 0] = last.astype(out.dtype)


def sides(from_low, from_high, low, high):
    vmem = pl.BlockSpec(memory_space=pltpu.VMEM)
    shape = jax.ShapeDtypeStruct(low.shape, low.dtype)
    return pl.pallas_call(
        sides_kernel,
        in_specs=[vmem] * 4,
        out_specs=[vmem, vmem],
        out_shape=[shape, shape],
        compiler_params=pltpu.CompilerParams(vmem_limit_bytes=SMALL_LIMIT),
        name="sides",
    )(*in_vmem(from_low, from_high, low, high))


def add_columns_kernel(low_ref, high_ref, edge_ref, partial_hbm, out_hbm, sum_ref, sems):
    del partial_hbm
    stores = []
    for which in range(2):
        for side, ref in enumerate((low_ref, high_ref)):
            for x in range(BX):
                total = edge_ref[which, x, side] + ref[which, x, 0].astype(jnp.float32)
                sum_ref[which, side, x] = total.astype(sum_ref.dtype)
                y = side * (BY - 1)
                index = (which * 2 + side) * BX + x
                store = pltpu.make_async_copy(sum_ref.at[which, side, x], out_hbm.at[which, x, y], sems.at[index])
                store.start()
                stores.append(store)
    for store in stores:
        store.wait()


def add_columns(edge, low, high, partial):
    vmem = pl.BlockSpec(memory_space=pltpu.VMEM)
    hbm = pl.BlockSpec(memory_space=pltpu.HBM)
    return pl.pallas_call(
        add_columns_kernel,
        in_specs=[vmem, vmem, vmem, hbm],
        out_specs=hbm,
        out_shape=jax.ShapeDtypeStruct(partial.shape, partial.dtype),
        scratch_shapes=[
            pltpu.VMEM((2, 2, BX) + edge.shape[3:], partial.dtype),
            pltpu.SemaphoreType.DMA((4 * BX,)),
        ],
        input_output_aliases={3: 0},
        compiler_params=pltpu.CompilerParams(vmem_limit_bytes=SMALL_LIMIT),
        name="add_columns",
    )(*in_vmem(low, high, edge), pltpu.with_memory_space_constraint(partial, pltpu.HBM))


def swap_cores(value):
    return lax.ppermute(value, "sx", [(i, i ^ 1) for i in range(lax.axis_size("sx"))])


def body(queries, keys_values, out_weight, gain, read_weight, adjacency, boundary, cotangent):
    size_x, size_y = queries.shape[1:3]
    inner = out_weight.shape[1]
    n_sx, n_sy, n_wa = (lax.axis_size(axis) for axis in ("sx", "sy", "wa"))
    row, column, case = (lax.axis_index(axis) for axis in ("sx", "sy", "wa"))
    core = row % 2
    kv = keys_values[:, 0]
    cols = inner // 2
    slab = lax.dynamic_slice_in_dim(out_weight, core * cols, cols, axis=1)
    pairs = [[w, w + 1] for w in range(0, n_wa, 2)]
    rings = [list(range(h, n_wa, 2)) for h in range(2)]
    both = lax.all_gather(slab, "wa", axis=0, axis_index_groups=pairs)
    own_cols = lax.all_gather(both, "wa", axis=0, axis_index_groups=rings).reshape(-1, cols)
    ylow = shift(kv[:, :, size_y - 1 :], "sy", 1)
    yhigh = shift(kv[:, :, :1], "sy", -1)
    xlow = shift(kv[:, size_x - 1 :], "sx", 1)
    xhigh = shift(kv[:, :1], "sx", -1)
    clow = shift(jnp.concatenate([ylow[:, size_x - 1 :], yhigh[:, size_x - 1 :]], axis=2), "sx", 1)
    chigh = shift(jnp.concatenate([ylow[:, :1], yhigh[:, :1]], axis=2), "sx", -1)
    pieces = (kv, xlow, clow, xhigh, chigh, ylow, yhigh)
    position = jnp.stack(
        [
            row * size_x,
            column * size_y,
            jnp.int32(size_x * n_sx),
            jnp.int32(size_y * n_sy),
            core,
        ]
    ).astype(jnp.int32)
    att, prob = forward(adjacency, position, queries, pieces)
    own_cols, att = lax.optimization_barrier((own_cols, att))
    swapped = swap_cores(own_cols)
    part, own_cols = project_own(att, own_cols)
    prediction, grad_att = project(
        boundary, position, att, part, own_cols, swapped, gain[None], read_weight.T, cotangent
    )
    grad_scores, gxlow, gclow, gxhigh, gchigh, gylow, gyhigh = back_rim(queries, grad_att, prob, pieces)
    corner_low = shift(gchigh, "sx", 1)
    corner_high = shift(gclow, "sx", -1)
    from_low = shift(gxhigh, "sx", 1)
    from_high = shift(gxlow, "sx", -1)
    grad_queries, partial, edge = back_own(queries, grad_att, prob, grad_scores, pieces, from_low, from_high)
    to_left, to_right = sides(corner_low, corner_high, gylow, gyhigh)
    left = shift(to_right, "sy", 1)
    right = shift(to_left, "sy", -1)
    grad_kv = add_columns(edge, left, right, partial)
    return (jnp.swapaxes(prediction, 3, 4), grad_queries, grad_kv[:, None])


def solution(mesh):
    return jax.shard_map(
        body,
        mesh=mesh,
        in_specs=(
            P("wa", "sx", "sy", None, None),
            P(None, "wa", "sx", "sy", None, None),
            P("wa", None),
            P(),
            P(),
            P("wa", "sx", "sy", None),
            P("wa", "sx", "sy"),
            P("wa", "sx", "sy", None, None),
        ),
        out_specs=(
            P("wa", "sx", "sy", None, None),
            P("wa", "sx", "sy", None, None),
            P(None, "wa", "sx", "sy", None, None),
        ),
        check_vma=False,
    )
```

```python
import jax
import jax.numpy as jnp
from jax import lax
from jax.experimental import pallas as pl
from jax.experimental.pallas import tpu as pltpu
from jax.sharding import PartitionSpec as P

HS = 128
BS = 16
BX = 2
BY = 4
TOK = BX * BY * BS
GROUP = 4
VMEM_LIMIT = 24 * 1024 * 1024
SMALL_LIMIT = 12 * 1024 * 1024

LOCAL = [(x, y) for x in range(BX) for y in range(BY)]
XLOW = [(-1, y) for y in range(BY)]
XHIGH = [(BX, y) for y in range(BY)]
YLOW = [(x, -1) for x in range(BX)]
YHIGH = [(x, BY) for x in range(BX)]
CLOW = [(-1, -1), (-1, BY)]
CHIGH = [(BX, -1), (BX, BY)]
PIECES = [LOCAL, XLOW, CLOW, XHIGH, CHIGH, YLOW, YHIGH]
KEY_BLOCKS = [block for piece in PIECES for block in piece]
KEYS = len(KEY_BLOCKS) * BS
SENT_STEPS = (0, 4, 1, 5, 7, 3, 6, 2)


def shift(value, axis, step):
    count = lax.axis_size(axis)
    pairs = [(i, i + step) for i in range(count) if 0 <= i + step < count]
    return lax.ppermute(value, axis, pairs)


def in_vmem(*values):
    return tuple(pltpu.with_memory_space_constraint(value, pltpu.VMEM) for value in values)


def dot(a, b, dims):
    return lax.dot_general(a, b, (dims, ((), ())), preferred_element_type=jnp.float32)


def piece_rows(refs, which, lanes):
    parts = []
    for ref in refs:
        blocks = ref[which, :, :, :, lanes]
        parts.append(blocks.reshape(-1, HS))
    return jnp.concatenate(parts, axis=0)


def allowed_mask(adj_ref, pos_ref):
    lane = lax.broadcasted_iota(jnp.int32, (1, TOK), 1)
    block = lane // BS
    bx = block // BY
    by = block % BY
    entries = []
    for e in range(4):
        vec = jnp.zeros((1, TOK), jnp.int32)
        for b in range(BX * BY):
            vec = jnp.where(block == b, adj_ref[0, b // BY, b % BY, e], vec)
        entries.append(vec)
    rows = []
    for kx, ky in KEY_BLOCKS:
        dx = kx - bx
        dy = ky - by
        near = (jnp.abs(dx) <= 1) & (jnp.abs(dy) <= 1)
        code = 3 * (dx + 1) + dy + 1
        entry = code - (code > 4).astype(jnp.int32)
        listed = code == 4
        for vec in entries:
            listed = listed | ((vec == entry) & (code != 4))
        gx = pos_ref[0] + kx
        gy = pos_ref[1] + ky
        inside = (gx >= 0) & (gx < pos_ref[2]) & (gy >= 0) & (gy < pos_ref[3])
        flag = jnp.where(near & listed, 1.0, 0.0) * jnp.where(inside, 1.0, 0.0)
        rows.append(jnp.broadcast_to(flag, (BS, TOK)))
    return jnp.concatenate(rows, axis=0)


def forward_kernel(adj_ref, pos_ref, q_ref, *rest):
    kv_refs = rest[: len(PIECES)]
    att_ref, prob_ref, mask_ref = rest[len(PIECES) :]

    @pl.when(pl.program_id(0) == 0)
    def _():
        mask_ref[...] = allowed_mask(adj_ref, pos_ref)

    for h in range(GROUP):
        lanes = slice(h * HS, (h + 1) * HS)
        query = q_ref[0, :, :, :, lanes].reshape(TOK, HS)
        keys = piece_rows(kv_refs, 0, lanes)
        values = piece_rows(kv_refs, 1, lanes)
        scores = dot(keys, query, ((1,), (1,))) * (HS**-0.5)
        masked = jnp.where(mask_ref[...] > 0.5, scores, -1e30)
        exponent = jnp.exp(masked - jnp.max(masked, axis=0, keepdims=True))
        prob = exponent / jnp.sum(exponent, axis=0, keepdims=True)
        prob_ref[h] = prob
        att = dot(prob.astype(jnp.bfloat16), values, ((0,), (0,)))
        att_ref[:, lanes] = att.astype(jnp.bfloat16)


def forward(adjacency, position, queries, pieces):
    inner = queries.shape[-1]
    width = GROUP * HS
    smem = pl.BlockSpec(memory_space=pltpu.SMEM)
    specs = [
        pl.BlockSpec(p.shape[:-1] + (width,), lambda g: (0, 0, 0, 0, g))
        for p in pieces
    ]
    return pl.pallas_call(
        forward_kernel,
        grid=(inner // width,),
        in_specs=[smem, smem, pl.BlockSpec(queries.shape[:-1] + (width,), lambda g: (0, 0, 0, 0, g))] + specs,
        out_specs=[
            pl.BlockSpec((TOK, width), lambda g: (0, g)),
            pl.BlockSpec((GROUP, KEYS, TOK), lambda g: (g, 0, 0)),
        ],
        out_shape=[
            jax.ShapeDtypeStruct((TOK, inner), jnp.bfloat16),
            jax.ShapeDtypeStruct((inner // HS, KEYS, TOK), jnp.float32),
        ],
        scratch_shapes=[pltpu.VMEM((KEYS, TOK), jnp.float32)],
        compiler_params=pltpu.CompilerParams(vmem_limit_bytes=VMEM_LIMIT),
        name="attend",
    )(adjacency, position, queries, *pieces)


def side_cols(pos_ref, side, cols, start=0, size=None):
    core = pos_ref[4]
    first = (core if side == 0 else 1 - core) * cols + start
    return pl.ds(pl.multiple_of(first, HS), cols - start if size is None else size)


def sent_heads(pos_ref, n_ring):
    return [
        pl.ds(pl.multiple_of((lax.rem(pos_ref[5] + 2 * n_ring - step, n_ring) * 2 + half) * HS, HS), HS)
        for step in SENT_STEPS
        for half in range(2)
    ]


def project_own_kernel(pos_ref, att_ref, w_hbm, sent_ref, part_ref, w_ref, mixed_ref, sems):
    chunks = 4
    rows = w_ref.shape[0] // chunks
    parts = [pl.ds(k * rows, rows) for k in range(chunks)]
    copies = [pltpu.make_async_copy(w_hbm.at[part], w_ref.at[part], sems.at[k]) for k, part in enumerate(parts)]
    for copy in copies:
        copy.start()
    for k, lanes in enumerate(sent_heads(pos_ref, sent_ref.shape[0])):
        mixed_ref[:, k * HS : (k + 1) * HS] = att_ref[:, lanes]
    ring_cols = w_ref.shape[1]
    inner = w_ref.shape[0]
    part_ref[:, ring_cols:] = dot(mixed_ref[...], sent_ref[...].reshape(inner, -1), ((1,), (0,)))
    total = None
    for k in range(chunks):
        copies[k].wait()
        lanes = slice(k * rows, (k + 1) * rows)
        term = dot(att_ref[:, lanes], w_ref[lanes, :], ((1,), (0,)))
        total = term if total is None else total + term
    part_ref[:, :ring_cols] = total


def project_own(position, att, own, sent):
    vmem = pl.BlockSpec(memory_space=pltpu.VMEM)
    smem = pl.BlockSpec(memory_space=pltpu.SMEM)
    tokens, inner = att.shape
    return pl.pallas_call(
        project_own_kernel,
        in_specs=[smem, vmem, pl.BlockSpec(memory_space=pl.ANY), vmem],
        out_specs=[vmem, vmem, vmem],
        out_shape=[
            jax.ShapeDtypeStruct((tokens, inner // 2), jnp.float32),
            jax.ShapeDtypeStruct(own.shape, own.dtype),
            jax.ShapeDtypeStruct(att.shape, att.dtype),
        ],
        scratch_shapes=[pltpu.SemaphoreType.DMA((4,))],
        compiler_params=pltpu.CompilerParams(vmem_limit_bytes=VMEM_LIMIT),
        name="project_own",
    )(position, att, pltpu.with_memory_space_constraint(own, pltpu.HBM), *in_vmem(sent))


def project_kernel(
    bound_ref, pos_ref, att_ref, mixed_ref, part_ref, own_ref, swap_hbm, sent_ref, sent_swap_ref, gain_ref, read_ref,
    cot_ref, pred_ref, ga_ref, swap_ref, proj_ref, gp_ref, sum_ref, sems,
):
    inner, ring_cols = swap_ref.shape
    cols = inner // 2
    chunks = 4
    rows = inner // chunks
    parts = [pl.ds(k * rows, rows) for k in range(chunks)]
    copies = [pltpu.make_async_copy(swap_hbm.at[part], swap_ref.at[part], sems.at[k]) for k, part in enumerate(parts)]
    for copy in copies:
        copy.start()
    sent = sent_ref[...].reshape(inner, cols - ring_cols)
    sent_swap = sent_swap_ref[...].reshape(inner, cols - ring_cols)
    proj_ref[:, side_cols(pos_ref, 0, cols)] = part_ref[...]
    proj_ref[:, side_cols(pos_ref, 1, cols, ring_cols)] = dot(mixed_ref[...], sent_swap, ((1,), (0,)))
    total = None
    for k in range(chunks):
        copies[k].wait()
        lanes = slice(k * rows, (k + 1) * rows)
        term = dot(att_ref[:, lanes], swap_ref[lanes, :], ((1,), (0,)))
        total = term if total is None else total + term
    proj_ref[:, side_cols(pos_ref, 1, cols, 0, ring_cols)] = total
    inner = proj_ref.shape[1]
    for pair in range(TOK // (2 * BS)):
        rows_of = slice(pair * 2 * BS, (pair + 1) * 2 * BS)
        x = pair * 2 // BY
        y = pair * 2 % BY
        proj = proj_ref[rows_of, :]
        gain = gain_ref[...]
        flag = jnp.where(
            lax.broadcasted_iota(jnp.int32, (2 * BS, 1), 0) < BS, bound_ref[0, x, y], bound_ref[0, x, y + 1]
        ).astype(jnp.float32)
        cot = jnp.concatenate([cot_ref[0, x, y], cot_ref[0, x, y + 1]], axis=0) * flag
        inv_rms = lax.rsqrt(jnp.sum(proj * proj, axis=1, keepdims=True) * (1.0 / inner) + 1e-05)
        normed = proj * inv_rms * gain
        pred0 = jnp.sum(normed * read_ref[0:1, :], axis=1, keepdims=True) * flag
        pred1 = jnp.sum(normed * read_ref[1:2, :], axis=1, keepdims=True) * flag
        pred = jnp.where(lax.broadcasted_iota(jnp.int32, (2 * BS, HS), 1) == 0, pred0, pred1).T
        pred_ref[0, x, y] = pred[:2, :BS]
        pred_ref[0, x, y + 1] = pred[:2, BS:]
        gained = (cot[:, 0:1] * read_ref[0:1, :] + cot[:, 1:2] * read_ref[1:2, :]) * gain
        inner_mean = jnp.sum(gained * proj, axis=1, keepdims=True) * (1.0 / inner)
        gp_ref[rows_of, :] = (inv_rms * gained - proj * (inv_rms * inv_rms * inv_rms * inner_mean)).astype(jnp.bfloat16)
    gp_own = gp_ref[:, side_cols(pos_ref, 0, cols)]
    gp_swap = gp_ref[:, side_cols(pos_ref, 1, cols)]
    for k in range(chunks):
        lanes = slice(k * rows, (k + 1) * rows)
        sum_ref[:, lanes] = dot(gp_swap[:, :ring_cols], swap_ref[lanes, :], ((1,), (1,))) + dot(
            gp_own[:, :ring_cols], own_ref[lanes, :], ((1,), (1,))
        )
    mixed = dot(gp_swap[:, ring_cols:], sent_swap, ((1,), (1,))) + dot(gp_own[:, ring_cols:], sent, ((1,), (1,)))
    for k, lanes in enumerate(sent_heads(pos_ref, sent_ref.shape[0])):
        ga_ref[:, lanes] = (sum_ref[:, lanes] + mixed[:, k * HS : (k + 1) * HS]).astype(jnp.bfloat16)


def project(boundary, position, att, mixed, part, own, swapped, sent, sent_swap, gain, read_rows, cotangent):
    vmem = pl.BlockSpec(memory_space=pltpu.VMEM)
    smem = pl.BlockSpec(memory_space=pltpu.SMEM)
    hbm = pl.BlockSpec(memory_space=pl.ANY)
    return pl.pallas_call(
        project_kernel,
        in_specs=[smem, smem, vmem, vmem, vmem, vmem, hbm, vmem, vmem, vmem, vmem, vmem],
        out_specs=[vmem, vmem],
        out_shape=[
            jax.ShapeDtypeStruct(cotangent.shape[:3] + (2, BS), jnp.float32),
            jax.ShapeDtypeStruct(att.shape, jnp.bfloat16),
        ],
        scratch_shapes=[
            pltpu.VMEM(swapped.shape, jnp.bfloat16),
            pltpu.VMEM(att.shape, jnp.float32),
            pltpu.VMEM(att.shape, jnp.bfloat16),
            pltpu.VMEM(att.shape, jnp.float32),
            pltpu.SemaphoreType.DMA((4,)),
        ],
        compiler_params=pltpu.CompilerParams(vmem_limit_bytes=VMEM_LIMIT),
        name="project",
    )(
        boundary,
        position,
        *in_vmem(att, mixed, part, own),
        pltpu.with_memory_space_constraint(swapped, pltpu.HBM),
        *in_vmem(sent, sent_swap),
        gain,
        read_rows,
        cotangent,
    )


def kv_rows(refs, which, lanes):
    return jnp.concatenate([ref[which, :, :, :, lanes].reshape(-1, HS) for ref in refs], axis=0)


def back_rim_kernel(q_ref, ga_ref, prob_ref, *rest):
    count = len(PIECES)
    v_refs = rest[:count]
    gs_ref = rest[count]
    rim_refs = rest[count + 1 :]
    for h in range(prob_ref.shape[0]):
        lanes = slice(h * HS, (h + 1) * HS)
        query = q_ref[0, :, :, :, lanes].reshape(TOK, HS)
        values = kv_rows(v_refs, 1, lanes)
        grad_att = ga_ref[:, lanes]
        prob = prob_ref[h]
        grad_prob = dot(values, grad_att, ((1,), (1,)))
        inner_sum = jnp.sum(prob * grad_prob, axis=0, keepdims=True)
        grad_scores = (prob * (grad_prob - inner_sum) * (HS**-0.5)).astype(jnp.bfloat16)
        gs_ref[h] = grad_scores
        half = prob[TOK:].astype(jnp.bfloat16)
        grads = (dot(grad_scores[TOK:], query, ((1,), (0,))), dot(half, grad_att, ((1,), (0,))))
        for which, grad in enumerate(grads):
            start = 0
            for ref in rim_refs:
                shape = ref.shape[1:4]
                rows = shape[0] * shape[1] * shape[2]
                ref[which, :, :, :, lanes] = grad[start : start + rows].reshape(shape + (HS,)).astype(ref.dtype)
                start += rows


def back_rim(queries, grad_att, prob, pieces):
    vmem = pl.BlockSpec(memory_space=pltpu.VMEM)
    shapes = [p.shape for p in pieces]
    return pl.pallas_call(
        back_rim_kernel,
        in_specs=[vmem] * (3 + len(pieces)),
        out_specs=[vmem] * len(pieces),
        out_shape=[jax.ShapeDtypeStruct(prob.shape, jnp.bfloat16)]
        + [jax.ShapeDtypeStruct(s, jnp.bfloat16) for s in shapes[1:]],
        compiler_params=pltpu.CompilerParams(vmem_limit_bytes=VMEM_LIMIT),
        name="back_rim",
    )(*in_vmem(queries, grad_att, prob, *pieces))


def back_own_kernel(q_ref, ga_ref, prob_ref, gs_ref, *rest):
    count = len(PIECES)
    k_refs = rest[:count]
    low_ref, high_ref, gq_ref, out_ref, edge_ref = rest[count:]
    for h in range(prob_ref.shape[0]):
        lanes = slice(h * HS, (h + 1) * HS)
        query = q_ref[0, :, :, :, lanes].reshape(TOK, HS)
        grad_scores = gs_ref[h]
        grad_query = dot(grad_scores, kv_rows(k_refs, 0, lanes), ((0,), (0,)))
        gq_ref[0, :, :, :, lanes] = grad_query.reshape(BX, BY, BS, HS).astype(gq_ref.dtype)
        half = prob_ref[h, :TOK, :].astype(jnp.bfloat16)
        grads = (dot(grad_scores[:TOK], query, ((1,), (0,))), dot(half, ga_ref[:, lanes], ((1,), (0,))))
        for which, grad in enumerate(grads):
            for block, (x, y) in enumerate(LOCAL):
                total = grad[block * BS : (block + 1) * BS]
                if x == 0:
                    total = total + low_ref[which, 0, y, :, lanes].astype(jnp.float32)
                if x == BX - 1:
                    total = total + high_ref[which, 0, y, :, lanes].astype(jnp.float32)
                if y in (0, BY - 1):
                    edge_ref[which, x, y // (BY - 1), :, lanes] = total
                else:
                    out_ref[which, x, y, :, lanes] = total.astype(out_ref.dtype)


def back_own(queries, grad_att, prob, grad_scores, pieces, low, high):
    vmem = pl.BlockSpec(memory_space=pltpu.VMEM)
    own = pieces[0].shape
    edge = own[:2] + (2,) + own[3:]
    return pl.pallas_call(
        back_own_kernel,
        in_specs=[vmem] * (6 + len(pieces)),
        out_specs=[vmem] * 3,
        out_shape=[
            jax.ShapeDtypeStruct(queries.shape, jnp.bfloat16),
            jax.ShapeDtypeStruct(own, jnp.bfloat16),
            jax.ShapeDtypeStruct(edge, jnp.float32),
        ],
        compiler_params=pltpu.CompilerParams(vmem_limit_bytes=VMEM_LIMIT),
        name="back_own",
    )(*in_vmem(queries, grad_att, prob, grad_scores, *pieces, low, high))


def sides_kernel(from_low_ref, from_high_ref, low_ref, high_ref, left_ref, right_ref):
    f32 = jnp.float32
    for y, rim, out in ((0, low_ref, left_ref), (1, high_ref, right_ref)):
        for which in range(2):
            first = rim[which, 0, 0].astype(f32) + from_low_ref[which, 0, y].astype(f32)
            last = rim[which, BX - 1, 0].astype(f32) + from_high_ref[which, 0, y].astype(f32)
            out[which, 0, 0] = first.astype(out.dtype)
            out[which, BX - 1, 0] = last.astype(out.dtype)


def sides(from_low, from_high, low, high):
    vmem = pl.BlockSpec(memory_space=pltpu.VMEM)
    shape = jax.ShapeDtypeStruct(low.shape, low.dtype)
    return pl.pallas_call(
        sides_kernel,
        in_specs=[vmem] * 4,
        out_specs=[vmem, vmem],
        out_shape=[shape, shape],
        compiler_params=pltpu.CompilerParams(vmem_limit_bytes=SMALL_LIMIT),
        name="sides",
    )(*in_vmem(from_low, from_high, low, high))


def add_columns_kernel(low_ref, high_ref, edge_ref, partial_hbm, out_hbm, sum_ref, sems):
    del partial_hbm
    stores = []
    for which in range(2):
        for side, ref in enumerate((low_ref, high_ref)):
            for x in range(BX):
                total = edge_ref[which, x, side] + ref[which, x, 0].astype(jnp.float32)
                sum_ref[which, side, x] = total.astype(sum_ref.dtype)
                y = side * (BY - 1)
                index = (which * 2 + side) * BX + x
                store = pltpu.make_async_copy(sum_ref.at[which, side, x], out_hbm.at[which, x, y], sems.at[index])
                store.start()
                stores.append(store)
    for store in stores:
        store.wait()


def add_columns(edge, low, high, partial):
    vmem = pl.BlockSpec(memory_space=pltpu.VMEM)
    hbm = pl.BlockSpec(memory_space=pltpu.HBM)
    return pl.pallas_call(
        add_columns_kernel,
        in_specs=[vmem, vmem, vmem, hbm],
        out_specs=hbm,
        out_shape=jax.ShapeDtypeStruct(partial.shape, partial.dtype),
        scratch_shapes=[
            pltpu.VMEM((2, 2, BX) + edge.shape[3:], partial.dtype),
            pltpu.SemaphoreType.DMA((4 * BX,)),
        ],
        input_output_aliases={3: 0},
        compiler_params=pltpu.CompilerParams(vmem_limit_bytes=SMALL_LIMIT),
        name="add_columns",
    )(*in_vmem(low, high, edge), pltpu.with_memory_space_constraint(partial, pltpu.HBM))


def around(value, axis, step):
    count = lax.axis_size(axis)
    return lax.ppermute(value, axis, [(i, (i + step) % count) for i in range(count)])


def swap_cores(value):
    return lax.ppermute(value, "sx", [(i, i ^ 1) for i in range(lax.axis_size("sx"))])


def body(queries, keys_values, out_weight, gain, read_weight, adjacency, boundary, cotangent):
    size_x, size_y = queries.shape[1:3]
    inner = out_weight.shape[1]
    n_sx, n_sy, n_wa = (lax.axis_size(axis) for axis in ("sx", "sy", "wa"))
    row, column, case = (lax.axis_index(axis) for axis in ("sx", "sy", "wa"))
    core = row % 2
    kv = keys_values[:, 0]
    cols = inner // 2
    slab = lax.dynamic_slice_in_dim(out_weight, core * cols, cols, axis=1)
    pairs = [[w, w + 1] for w in range(0, n_wa, 2)]
    rings = [list(range(h, n_wa, 2)) for h in range(2)]
    both = lax.all_gather(slab, "wa", axis=0, axis_index_groups=pairs)
    ring_cols = 3 * cols // 4
    own_cols = lax.all_gather(both[:, :, :ring_cols], "wa", axis=0, axis_index_groups=rings).reshape(-1, ring_cols)
    sent = both[None, :, :, ring_cols:]
    sent = jnp.concatenate([sent, around(sent, "wa", n_wa // 2)])
    ylow = shift(kv[:, :, size_y - 1 :], "sy", 1)
    yhigh = shift(kv[:, :, :1], "sy", -1)
    xlow = shift(kv[:, size_x - 1 :], "sx", 1)
    xhigh = shift(kv[:, :1], "sx", -1)
    clow = shift(jnp.concatenate([ylow[:, size_x - 1 :], yhigh[:, size_x - 1 :]], axis=2), "sx", 1)
    chigh = shift(jnp.concatenate([ylow[:, :1], yhigh[:, :1]], axis=2), "sx", -1)
    sent, xlow = lax.optimization_barrier((sent, xlow))
    sent = jnp.concatenate([sent] + [around(sent, "wa", 2 * k) for k in (1, -1, -2)])
    queries, sent = lax.optimization_barrier((queries, sent))
    sent_swap = swap_cores(sent)
    pieces = (kv, xlow, clow, xhigh, chigh, ylow, yhigh)
    position = jnp.stack(
        [
            row * size_x,
            column * size_y,
            jnp.int32(size_x * n_sx),
            jnp.int32(size_y * n_sy),
            core,
            case // 2,
        ]
    ).astype(jnp.int32)
    att, prob = forward(adjacency, position, queries, pieces)
    own_cols, att, sent_swap = lax.optimization_barrier((own_cols, att, sent_swap))
    swapped = swap_cores(own_cols)
    part, own_cols, mixed = project_own(position, att, own_cols, sent)
    prediction, grad_att = project(
        boundary,
        position,
        att,
        mixed,
        part,
        own_cols,
        swapped,
        sent,
        sent_swap,
        gain[None],
        read_weight.T,
        cotangent,
    )
    grad_scores, gxlow, gclow, gxhigh, gchigh, gylow, gyhigh = back_rim(queries, grad_att, prob, pieces)
    corner_low = shift(gchigh, "sx", 1)
    corner_high = shift(gclow, "sx", -1)
    from_low = shift(gxhigh, "sx", 1)
    from_high = shift(gxlow, "sx", -1)
    grad_queries, partial, edge = back_own(queries, grad_att, prob, grad_scores, pieces, from_low, from_high)
    to_left, to_right = sides(corner_low, corner_high, gylow, gyhigh)
    left = shift(to_right, "sy", 1)
    right = shift(to_left, "sy", -1)
    grad_kv = add_columns(edge, left, right, partial)
    return (jnp.swapaxes(prediction, 3, 4), grad_queries, grad_kv[:, None])


def solution(mesh):
    return jax.shard_map(
        body,
        mesh=mesh,
        in_specs=(
            P("wa", "sx", "sy", None, None),
            P(None, "wa", "sx", "sy", None, None),
            P("wa", None),
            P(),
            P(),
            P("wa", "sx", "sy", None),
            P("wa", "sx", "sy"),
            P("wa", "sx", "sy", None, None),
        ),
        out_specs=(
            P("wa", "sx", "sy", None, None),
            P("wa", "sx", "sy", None, None),
            P(None, "wa", "sx", "sy", None, None),
        ),
        check_vma=False,
    )
```

```python
import jax
import jax.numpy as jnp
from jax import lax
from jax.experimental import pallas as pl
from jax.experimental.pallas import tpu as pltpu
from jax.sharding import PartitionSpec as P

HS = 128
BS = 16
BX = 2
BY = 4
TOK = BX * BY * BS
GROUP = 4
VMEM_LIMIT = 24 * 1024 * 1024
SMALL_LIMIT = 12 * 1024 * 1024

LOCAL = [(x, y) for x in range(BX) for y in range(BY)]
XLOW = [(-1, y) for y in range(BY)]
XHIGH = [(BX, y) for y in range(BY)]
YLOW = [(x, -1) for x in range(BX)]
YHIGH = [(x, BY) for x in range(BX)]
CLOW = [(-1, -1), (-1, BY)]
CHIGH = [(BX, -1), (BX, BY)]
PIECES = [LOCAL, XLOW, CLOW, XHIGH, CHIGH, YLOW, YHIGH]
KEY_BLOCKS = [block for piece in PIECES for block in piece]
KEYS = len(KEY_BLOCKS) * BS


def shift(value, axis, step):
    count = lax.axis_size(axis)
    pairs = [(i, i + step) for i in range(count) if 0 <= i + step < count]
    return lax.ppermute(value, axis, pairs)


def in_vmem(*values):
    return tuple(pltpu.with_memory_space_constraint(value, pltpu.VMEM) for value in values)


def dot(a, b, dims):
    return lax.dot_general(a, b, (dims, ((), ())), preferred_element_type=jnp.float32)


def piece_rows(refs, which, lanes):
    parts = []
    for ref in refs:
        blocks = ref[which, :, :, :, lanes]
        parts.append(blocks.reshape(-1, HS))
    return jnp.concatenate(parts, axis=0)


def allowed_mask(adj_ref, pos_ref):
    lane = lax.broadcasted_iota(jnp.int32, (1, TOK), 1)
    block = lane // BS
    bx = block // BY
    by = block % BY
    entries = []
    for e in range(4):
        vec = jnp.zeros((1, TOK), jnp.int32)
        for b in range(BX * BY):
            vec = jnp.where(block == b, adj_ref[0, b // BY, b % BY, e], vec)
        entries.append(vec)
    rows = []
    for kx, ky in KEY_BLOCKS:
        dx = kx - bx
        dy = ky - by
        near = (jnp.abs(dx) <= 1) & (jnp.abs(dy) <= 1)
        code = 3 * (dx + 1) + dy + 1
        entry = code - (code > 4).astype(jnp.int32)
        listed = code == 4
        for vec in entries:
            listed = listed | ((vec == entry) & (code != 4))
        gx = pos_ref[0] + kx
        gy = pos_ref[1] + ky
        inside = (gx >= 0) & (gx < pos_ref[2]) & (gy >= 0) & (gy < pos_ref[3])
        flag = jnp.where(near & listed, 1.0, 0.0) * jnp.where(inside, 1.0, 0.0)
        rows.append(jnp.broadcast_to(flag, (BS, TOK)))
    return jnp.concatenate(rows, axis=0)


def forward_kernel(adj_ref, pos_ref, q_ref, *rest):
    kv_refs = rest[: len(PIECES)]
    att_ref, prob_ref, mask_ref = rest[len(PIECES) :]

    @pl.when(pl.program_id(0) == 0)
    def _():
        mask_ref[...] = allowed_mask(adj_ref, pos_ref)

    for h in range(GROUP):
        lanes = slice(h * HS, (h + 1) * HS)
        query = q_ref[0, :, :, :, lanes].reshape(TOK, HS)
        keys = piece_rows(kv_refs, 0, lanes)
        values = piece_rows(kv_refs, 1, lanes)
        scores = dot(keys, query, ((1,), (1,))) * (HS**-0.5)
        masked = jnp.where(mask_ref[...] > 0.5, scores, -1e30)
        exponent = jnp.exp(masked - jnp.max(masked, axis=0, keepdims=True))
        prob = exponent / jnp.sum(exponent, axis=0, keepdims=True)
        prob_ref[h] = prob
        att = dot(prob.astype(jnp.bfloat16), values, ((0,), (0,)))
        att_ref[:, lanes] = att.astype(jnp.bfloat16)


def forward(adjacency, position, queries, pieces):
    inner = queries.shape[-1]
    width = GROUP * HS
    smem = pl.BlockSpec(memory_space=pltpu.SMEM)
    specs = [
        pl.BlockSpec(p.shape[:-1] + (width,), lambda g: (0, 0, 0, 0, g))
        for p in pieces
    ]
    return pl.pallas_call(
        forward_kernel,
        grid=(inner // width,),
        in_specs=[smem, smem, pl.BlockSpec(queries.shape[:-1] + (width,), lambda g: (0, 0, 0, 0, g))] + specs,
        out_specs=[
            pl.BlockSpec((TOK, width), lambda g: (0, g)),
            pl.BlockSpec((GROUP, KEYS, TOK), lambda g: (g, 0, 0)),
        ],
        out_shape=[
            jax.ShapeDtypeStruct((TOK, inner), jnp.bfloat16),
            jax.ShapeDtypeStruct((inner // HS, KEYS, TOK), jnp.float32),
        ],
        scratch_shapes=[pltpu.VMEM((KEYS, TOK), jnp.float32)],
        compiler_params=pltpu.CompilerParams(vmem_limit_bytes=VMEM_LIMIT),
        name="attend",
    )(adjacency, position, queries, *pieces)


def side_cols(pos_ref, side, cols):
    core = pos_ref[4]
    return pl.ds(pl.multiple_of((core if side == 0 else 1 - core) * cols, cols), cols)


def project_own_kernel(att_ref, w_hbm, prob_hbm, part_ref, w_ref, prob_ref, sems):
    chunks = 4
    rows = w_ref.shape[0] // chunks
    parts = [pl.ds(k * rows, rows) for k in range(chunks)]
    copies = [pltpu.make_async_copy(w_hbm.at[part], w_ref.at[part], sems.at[k]) for k, part in enumerate(parts)]
    for copy in copies:
        copy.start()
    prob_copy = pltpu.make_async_copy(prob_hbm, prob_ref, sems.at[chunks])
    prob_copy.start()
    total = None
    for k in range(chunks):
        copies[k].wait()
        lanes = slice(k * rows, (k + 1) * rows)
        term = dot(att_ref[:, lanes], w_ref[lanes, :], ((1,), (0,)))
        total = term if total is None else total + term
    part_ref[...] = total
    prob_copy.wait()


def project_own(att, own, prob):
    vmem = pl.BlockSpec(memory_space=pltpu.VMEM)
    hbm = pl.BlockSpec(memory_space=pl.ANY)
    tokens = att.shape[0]
    cols = own.shape[1]
    return pl.pallas_call(
        project_own_kernel,
        in_specs=[vmem, hbm, hbm],
        out_specs=[vmem, vmem, vmem],
        out_shape=[
            jax.ShapeDtypeStruct((tokens, cols), jnp.float32),
            jax.ShapeDtypeStruct(own.shape, own.dtype),
            jax.ShapeDtypeStruct(prob.shape, prob.dtype),
        ],
        scratch_shapes=[pltpu.SemaphoreType.DMA((5,))],
        compiler_params=pltpu.CompilerParams(vmem_limit_bytes=VMEM_LIMIT),
        name="project_own",
    )(att, *(pltpu.with_memory_space_constraint(value, pltpu.HBM) for value in (own, prob)))


def project_kernel(
    bound_ref, pos_ref, att_ref, part_ref, own_ref, swap_hbm, gain_ref, read_ref, cot_ref,
    pred_ref, ga_ref, swap_ref, proj_ref, gp_ref, sems,
):
    cols = swap_ref.shape[1]
    chunks = 8
    rows = swap_ref.shape[0] // chunks
    parts = [pl.ds(k * rows, rows) for k in range(chunks)]
    copies = [pltpu.make_async_copy(swap_hbm.at[part], swap_ref.at[part], sems.at[k]) for k, part in enumerate(parts)]
    for copy in copies:
        copy.start()
    total = None
    for k in range(chunks):
        copies[k].wait()
        lanes = slice(k * rows, (k + 1) * rows)
        term = dot(att_ref[:, lanes], swap_ref[lanes, :], ((1,), (0,)))
        total = term if total is None else total + term
    proj_ref[:, side_cols(pos_ref, 0, cols)] = part_ref[...]
    proj_ref[:, side_cols(pos_ref, 1, cols)] = total
    inner = proj_ref.shape[1]
    for pair in range(TOK // (2 * BS)):
        rows_of = slice(pair * 2 * BS, (pair + 1) * 2 * BS)
        x = pair * 2 // BY
        y = pair * 2 % BY
        proj = proj_ref[rows_of, :]
        gain = gain_ref[...]
        flag = jnp.where(
            lax.broadcasted_iota(jnp.int32, (2 * BS, 1), 0) < BS, bound_ref[0, x, y], bound_ref[0, x, y + 1]
        ).astype(jnp.float32)
        cot = jnp.concatenate([cot_ref[0, x, y], cot_ref[0, x, y + 1]], axis=0) * flag
        inv_rms = lax.rsqrt(jnp.sum(proj * proj, axis=1, keepdims=True) * (1.0 / inner) + 1e-05)
        normed = proj * inv_rms * gain
        pred0 = jnp.sum(normed * read_ref[0:1, :], axis=1, keepdims=True) * flag
        pred1 = jnp.sum(normed * read_ref[1:2, :], axis=1, keepdims=True) * flag
        pred = jnp.where(lax.broadcasted_iota(jnp.int32, (2 * BS, HS), 1) == 0, pred0, pred1).T
        pred_ref[0, x, y] = pred[:2, :BS]
        pred_ref[0, x, y + 1] = pred[:2, BS:]
        gained = (cot[:, 0:1] * read_ref[0:1, :] + cot[:, 1:2] * read_ref[1:2, :]) * gain
        inner_mean = jnp.sum(gained * proj, axis=1, keepdims=True) * (1.0 / inner)
        gp_ref[rows_of, :] = (inv_rms * gained - proj * (inv_rms * inv_rms * inv_rms * inner_mean)).astype(jnp.bfloat16)
    gp_own = gp_ref[:, side_cols(pos_ref, 0, cols)]
    gp_swap = gp_ref[:, side_cols(pos_ref, 1, cols)]
    for k in range(chunks):
        lanes = slice(k * rows, (k + 1) * rows)
        total = dot(gp_swap, swap_ref[lanes, :], ((1,), (1,))) + dot(gp_own, own_ref[lanes, :], ((1,), (1,)))
        ga_ref[:, lanes] = total.astype(jnp.bfloat16)


def project(boundary, position, att, part, own, swapped, gain, read_rows, cotangent):
    vmem = pl.BlockSpec(memory_space=pltpu.VMEM)
    smem = pl.BlockSpec(memory_space=pltpu.SMEM)
    return pl.pallas_call(
        project_kernel,
        in_specs=[smem, smem, vmem, vmem, vmem, pl.BlockSpec(memory_space=pl.ANY), vmem, vmem, vmem],
        out_specs=[vmem, vmem],
        out_shape=[
            jax.ShapeDtypeStruct(cotangent.shape[:3] + (2, BS), jnp.float32),
            jax.ShapeDtypeStruct(att.shape, jnp.bfloat16),
        ],
        scratch_shapes=[
            pltpu.VMEM(swapped.shape, jnp.bfloat16),
            pltpu.VMEM(att.shape, jnp.float32),
            pltpu.VMEM(att.shape, jnp.bfloat16),
            pltpu.SemaphoreType.DMA((8,)),
        ],
        compiler_params=pltpu.CompilerParams(vmem_limit_bytes=VMEM_LIMIT),
        name="project",
    )(
        boundary,
        position,
        *in_vmem(att, part, own),
        pltpu.with_memory_space_constraint(swapped, pltpu.HBM),
        gain,
        read_rows,
        cotangent,
    )


def kv_rows(refs, which, lanes):
    return jnp.concatenate([ref[which, :, :, :, lanes].reshape(-1, HS) for ref in refs], axis=0)


def back_rim_kernel(q_ref, ga_ref, prob_ref, *rest):
    count = len(PIECES)
    v_refs = rest[:count]
    gs_ref = rest[count]
    rim_refs = rest[count + 1 :]
    for h in range(prob_ref.shape[0]):
        lanes = slice(h * HS, (h + 1) * HS)
        query = q_ref[0, :, :, :, lanes].reshape(TOK, HS)
        values = kv_rows(v_refs, 1, lanes)
        grad_att = ga_ref[:, lanes]
        prob = prob_ref[h]
        grad_prob = dot(values, grad_att, ((1,), (1,)))
        inner_sum = jnp.sum(prob * grad_prob, axis=0, keepdims=True)
        grad_scores = (prob * (grad_prob - inner_sum) * (HS**-0.5)).astype(jnp.bfloat16)
        gs_ref[h] = grad_scores
        half = prob[TOK:].astype(jnp.bfloat16)
        grads = (dot(grad_scores[TOK:], query, ((1,), (0,))), dot(half, grad_att, ((1,), (0,))))
        for which, grad in enumerate(grads):
            start = 0
            for ref in rim_refs:
                shape = ref.shape[1:4]
                rows = shape[0] * shape[1] * shape[2]
                ref[which, :, :, :, lanes] = grad[start : start + rows].reshape(shape + (HS,)).astype(ref.dtype)
                start += rows


def back_rim(queries, grad_att, prob, pieces):
    vmem = pl.BlockSpec(memory_space=pltpu.VMEM)
    shapes = [p.shape for p in pieces]
    return pl.pallas_call(
        back_rim_kernel,
        in_specs=[vmem] * (3 + len(pieces)),
        out_specs=[vmem] * len(pieces),
        out_shape=[jax.ShapeDtypeStruct(prob.shape, jnp.bfloat16)]
        + [jax.ShapeDtypeStruct(s, jnp.bfloat16) for s in shapes[1:]],
        compiler_params=pltpu.CompilerParams(vmem_limit_bytes=VMEM_LIMIT),
        name="back_rim",
    )(*in_vmem(queries, grad_att, prob, *pieces))


def back_own_kernel(q_ref, ga_ref, prob_ref, gs_ref, *rest):
    count = len(PIECES)
    k_refs = rest[:count]
    low_ref, high_ref, gq_ref, out_ref, edge_ref = rest[count:]
    for h in range(prob_ref.shape[0]):
        lanes = slice(h * HS, (h + 1) * HS)
        query = q_ref[0, :, :, :, lanes].reshape(TOK, HS)
        grad_scores = gs_ref[h]
        grad_query = dot(grad_scores, kv_rows(k_refs, 0, lanes), ((0,), (0,)))
        gq_ref[0, :, :, :, lanes] = grad_query.reshape(BX, BY, BS, HS).astype(gq_ref.dtype)
        half = prob_ref[h, :TOK, :].astype(jnp.bfloat16)
        grads = (dot(grad_scores[:TOK], query, ((1,), (0,))), dot(half, ga_ref[:, lanes], ((1,), (0,))))
        for which, grad in enumerate(grads):
            for block, (x, y) in enumerate(LOCAL):
                total = grad[block * BS : (block + 1) * BS]
                if x == 0:
                    total = total + low_ref[which, 0, y, :, lanes].astype(jnp.float32)
                if x == BX - 1:
                    total = total + high_ref[which, 0, y, :, lanes].astype(jnp.float32)
                if y in (0, BY - 1):
                    edge_ref[which, x, y // (BY - 1), :, lanes] = total
                else:
                    out_ref[which, x, y, :, lanes] = total.astype(out_ref.dtype)


def back_own(queries, grad_att, prob, grad_scores, pieces, low, high):
    vmem = pl.BlockSpec(memory_space=pltpu.VMEM)
    own = pieces[0].shape
    edge = own[:2] + (2,) + own[3:]
    return pl.pallas_call(
        back_own_kernel,
        in_specs=[vmem] * (6 + len(pieces)),
        out_specs=[vmem] * 3,
        out_shape=[
            jax.ShapeDtypeStruct(queries.shape, jnp.bfloat16),
            jax.ShapeDtypeStruct(own, jnp.bfloat16),
            jax.ShapeDtypeStruct(edge, jnp.float32),
        ],
        compiler_params=pltpu.CompilerParams(vmem_limit_bytes=VMEM_LIMIT),
        name="back_own",
    )(*in_vmem(queries, grad_att, prob, grad_scores, *pieces, low, high))


def sides_kernel(from_low_ref, from_high_ref, low_ref, high_ref, left_ref, right_ref):
    f32 = jnp.float32
    for y, rim, out in ((0, low_ref, left_ref), (1, high_ref, right_ref)):
        for which in range(2):
            first = rim[which, 0, 0].astype(f32) + from_low_ref[which, 0, y].astype(f32)
            last = rim[which, BX - 1, 0].astype(f32) + from_high_ref[which, 0, y].astype(f32)
            out[which, 0, 0] = first.astype(out.dtype)
            out[which, BX - 1, 0] = last.astype(out.dtype)


def sides(from_low, from_high, low, high):
    vmem = pl.BlockSpec(memory_space=pltpu.VMEM)
    shape = jax.ShapeDtypeStruct(low.shape, low.dtype)
    return pl.pallas_call(
        sides_kernel,
        in_specs=[vmem] * 4,
        out_specs=[vmem, vmem],
        out_shape=[shape, shape],
        compiler_params=pltpu.CompilerParams(vmem_limit_bytes=SMALL_LIMIT),
        name="sides",
    )(*in_vmem(from_low, from_high, low, high))


def add_columns_kernel(low_ref, high_ref, edge_ref, partial_hbm, out_hbm, sum_ref, sems):
    del partial_hbm
    stores = []
    for which in range(2):
        for side, ref in enumerate((low_ref, high_ref)):
            for x in range(BX):
                total = edge_ref[which, x, side] + ref[which, x, 0].astype(jnp.float32)
                sum_ref[which, side, x] = total.astype(sum_ref.dtype)
                y = side * (BY - 1)
                index = (which * 2 + side) * BX + x
                store = pltpu.make_async_copy(sum_ref.at[which, side, x], out_hbm.at[which, x, y], sems.at[index])
                store.start()
                stores.append(store)
    for store in stores:
        store.wait()


def add_columns(edge, low, high, partial):
    vmem = pl.BlockSpec(memory_space=pltpu.VMEM)
    hbm = pl.BlockSpec(memory_space=pltpu.HBM)
    return pl.pallas_call(
        add_columns_kernel,
        in_specs=[vmem, vmem, vmem, hbm],
        out_specs=hbm,
        out_shape=jax.ShapeDtypeStruct(partial.shape, partial.dtype),
        scratch_shapes=[
            pltpu.VMEM((2, 2, BX) + edge.shape[3:], partial.dtype),
            pltpu.SemaphoreType.DMA((4 * BX,)),
        ],
        input_output_aliases={3: 0},
        compiler_params=pltpu.CompilerParams(vmem_limit_bytes=SMALL_LIMIT),
        name="add_columns",
    )(*in_vmem(low, high, edge), pltpu.with_memory_space_constraint(partial, pltpu.HBM))


def swap_cores(value):
    return lax.ppermute(value, "sx", [(i, i ^ 1) for i in range(lax.axis_size("sx"))])


def body(queries, keys_values, out_weight, gain, read_weight, adjacency, boundary, cotangent):
    size_x, size_y = queries.shape[1:3]
    inner = out_weight.shape[1]
    n_sx, n_sy, n_wa = (lax.axis_size(axis) for axis in ("sx", "sy", "wa"))
    row, column, case = (lax.axis_index(axis) for axis in ("sx", "sy", "wa"))
    core = row % 2
    kv = keys_values[:, 0]
    cols = inner // 2
    slab = lax.dynamic_slice_in_dim(out_weight, core * cols, cols, axis=1)
    pairs = [[w, w + 1] for w in range(0, n_wa, 2)]
    rings = [list(range(h, n_wa, 2)) for h in range(2)]
    both = lax.all_gather(slab, "wa", axis=0, axis_index_groups=pairs)
    own_cols = lax.all_gather(both, "wa", axis=0, axis_index_groups=rings).reshape(-1, cols)
    ylow = shift(kv[:, :, size_y - 1 :], "sy", 1)
    yhigh = shift(kv[:, :, :1], "sy", -1)
    xlow = shift(kv[:, size_x - 1 :], "sx", 1)
    xhigh = shift(kv[:, :1], "sx", -1)
    clow = shift(jnp.concatenate([ylow[:, size_x - 1 :], yhigh[:, size_x - 1 :]], axis=2), "sx", 1)
    chigh = shift(jnp.concatenate([ylow[:, :1], yhigh[:, :1]], axis=2), "sx", -1)
    pieces = (kv, xlow, clow, xhigh, chigh, ylow, yhigh)
    position = jnp.stack(
        [
            row * size_x,
            column * size_y,
            jnp.int32(size_x * n_sx),
            jnp.int32(size_y * n_sy),
            core,
        ]
    ).astype(jnp.int32)
    att, prob = forward(adjacency, position, queries, pieces)
    own_cols, att = lax.optimization_barrier((own_cols, att))
    swapped = swap_cores(own_cols)
    part, own_cols, prob = project_own(att, own_cols, prob)
    prediction, grad_att = project(
        boundary, position, att, part, own_cols, swapped, gain[None], read_weight.T, cotangent
    )
    grad_scores, gxlow, gclow, gxhigh, gchigh, gylow, gyhigh = back_rim(queries, grad_att, prob, pieces)
    corner_low = shift(gchigh, "sx", 1)
    corner_high = shift(gclow, "sx", -1)
    from_low = shift(gxhigh, "sx", 1)
    from_high = shift(gxlow, "sx", -1)
    grad_queries, partial, edge = back_own(queries, grad_att, prob, grad_scores, pieces, from_low, from_high)
    to_left, to_right = sides(corner_low, corner_high, gylow, gyhigh)
    left = shift(to_right, "sy", 1)
    right = shift(to_left, "sy", -1)
    grad_kv = add_columns(edge, left, right, partial)
    return (jnp.swapaxes(prediction, 3, 4), grad_queries, grad_kv[:, None])


def solution(mesh):
    return jax.shard_map(
        body,
        mesh=mesh,
        in_specs=(
            P("wa", "sx", "sy", None, None),
            P(None, "wa", "sx", "sy", None, None),
            P("wa", None),
            P(),
            P(),
            P("wa", "sx", "sy", None),
            P("wa", "sx", "sy"),
            P("wa", "sx", "sy", None, None),
        ),
        out_specs=(
            P("wa", "sx", "sy", None, None),
            P("wa", "sx", "sy", None, None),
            P(None, "wa", "sx", "sy", None, None),
        ),
        check_vma=False,
    )
```

```python
import jax
import jax.numpy as jnp
from jax import lax
from jax.experimental import pallas as pl
from jax.experimental.pallas import tpu as pltpu
from jax.sharding import PartitionSpec as P

HS = 128
BS = 16
BX = 2
BY = 4
TOK = BX * BY * BS
GROUP = 4
VMEM_LIMIT = 24 * 1024 * 1024
SMALL_LIMIT = 12 * 1024 * 1024

LOCAL = [(x, y) for x in range(BX) for y in range(BY)]
XLOW = [(-1, y) for y in range(BY)]
XHIGH = [(BX, y) for y in range(BY)]
YLOW = [(x, -1) for x in range(BX)]
YHIGH = [(x, BY) for x in range(BX)]
CLOW = [(-1, -1), (-1, BY)]
CHIGH = [(BX, -1), (BX, BY)]
PIECES = [LOCAL, XLOW, CLOW, XHIGH, CHIGH, YLOW, YHIGH]
KEY_BLOCKS = [block for piece in PIECES for block in piece]
KEYS = len(KEY_BLOCKS) * BS


def shift(value, axis, step):
    count = lax.axis_size(axis)
    pairs = [(i, i + step) for i in range(count) if 0 <= i + step < count]
    return lax.ppermute(value, axis, pairs)


def in_vmem(*values):
    return tuple(pltpu.with_memory_space_constraint(value, pltpu.VMEM) for value in values)


def dot(a, b, dims):
    return lax.dot_general(a, b, (dims, ((), ())), preferred_element_type=jnp.float32)


def piece_rows(refs, which, lanes):
    parts = []
    for ref in refs:
        blocks = ref[which, :, :, :, lanes]
        parts.append(blocks.reshape(-1, HS))
    return jnp.concatenate(parts, axis=0)


def allowed_mask(adj_ref, pos_ref):
    lane = lax.broadcasted_iota(jnp.int32, (1, TOK), 1)
    block = lane // BS
    bx = block // BY
    by = block % BY
    entries = []
    for e in range(4):
        vec = jnp.zeros((1, TOK), jnp.int32)
        for b in range(BX * BY):
            vec = jnp.where(block == b, adj_ref[0, b // BY, b % BY, e], vec)
        entries.append(vec)
    rows = []
    for kx, ky in KEY_BLOCKS:
        dx = kx - bx
        dy = ky - by
        near = (jnp.abs(dx) <= 1) & (jnp.abs(dy) <= 1)
        code = 3 * (dx + 1) + dy + 1
        entry = code - (code > 4).astype(jnp.int32)
        listed = code == 4
        for vec in entries:
            listed = listed | ((vec == entry) & (code != 4))
        gx = pos_ref[0] + kx
        gy = pos_ref[1] + ky
        inside = (gx >= 0) & (gx < pos_ref[2]) & (gy >= 0) & (gy < pos_ref[3])
        flag = jnp.where(near & listed, 1.0, 0.0) * jnp.where(inside, 1.0, 0.0)
        rows.append(jnp.broadcast_to(flag, (BS, TOK)))
    return jnp.concatenate(rows, axis=0)


def forward_kernel(adj_ref, pos_ref, q_ref, *rest):
    kv_refs = rest[: len(PIECES)]
    att_ref, prob_ref, mask_ref = rest[len(PIECES) :]

    @pl.when(pl.program_id(0) == 0)
    def _():
        mask_ref[...] = allowed_mask(adj_ref, pos_ref)

    for h in range(GROUP):
        lanes = slice(h * HS, (h + 1) * HS)
        query = q_ref[0, :, :, :, lanes].reshape(TOK, HS)
        keys = piece_rows(kv_refs, 0, lanes)
        values = piece_rows(kv_refs, 1, lanes)
        scores = dot(keys, query, ((1,), (1,))) * (HS**-0.5)
        masked = jnp.where(mask_ref[...] > 0.5, scores, -1e30)
        exponent = jnp.exp(masked - jnp.max(masked, axis=0, keepdims=True))
        prob = exponent / jnp.sum(exponent, axis=0, keepdims=True)
        prob_ref[h] = prob
        att = dot(prob.astype(jnp.bfloat16), values, ((0,), (0,)))
        att_ref[:, lanes] = att.astype(jnp.bfloat16)


def forward(adjacency, position, queries, pieces):
    inner = queries.shape[-1]
    width = GROUP * HS
    smem = pl.BlockSpec(memory_space=pltpu.SMEM)
    specs = [
        pl.BlockSpec(p.shape[:-1] + (width,), lambda g: (0, 0, 0, 0, g))
        for p in pieces
    ]
    return pl.pallas_call(
        forward_kernel,
        grid=(inner // width,),
        in_specs=[smem, smem, pl.BlockSpec(queries.shape[:-1] + (width,), lambda g: (0, 0, 0, 0, g))] + specs,
        out_specs=[
            pl.BlockSpec((TOK, width), lambda g: (0, g)),
            pl.BlockSpec((GROUP, KEYS, TOK), lambda g: (g, 0, 0)),
        ],
        out_shape=[
            jax.ShapeDtypeStruct((TOK, inner), jnp.bfloat16),
            jax.ShapeDtypeStruct((inner // HS, KEYS, TOK), jnp.float32),
        ],
        scratch_shapes=[pltpu.VMEM((KEYS, TOK), jnp.float32)],
        compiler_params=pltpu.CompilerParams(vmem_limit_bytes=VMEM_LIMIT),
        name="attend",
    )(adjacency, position, queries, *pieces)


def side_cols(pos_ref, side, cols):
    core = pos_ref[4]
    return pl.ds(pl.multiple_of((core if side == 0 else 1 - core) * cols, cols), cols)


def project_own_kernel(att_ref, w_hbm, prob_hbm, part_ref, w_ref, prob_ref, sems):
    chunks = 4
    rows = w_ref.shape[0] // chunks
    parts = [pl.ds(k * rows, rows) for k in range(chunks)]
    copies = [pltpu.make_async_copy(w_hbm.at[part], w_ref.at[part], sems.at[k]) for k, part in enumerate(parts)]
    for copy in copies:
        copy.start()
    prob_copy = pltpu.make_async_copy(prob_hbm, prob_ref, sems.at[chunks])
    prob_copy.start()
    total = None
    for k in range(chunks):
        copies[k].wait()
        lanes = slice(k * rows, (k + 1) * rows)
        term = dot(att_ref[:, lanes], w_ref[lanes, :], ((1,), (0,)))
        total = term if total is None else total + term
    part_ref[...] = total
    prob_copy.wait()


def project_own(att, own, prob):
    vmem = pl.BlockSpec(memory_space=pltpu.VMEM)
    hbm = pl.BlockSpec(memory_space=pl.ANY)
    tokens = att.shape[0]
    cols = own.shape[1]
    return pl.pallas_call(
        project_own_kernel,
        in_specs=[vmem, hbm, hbm],
        out_specs=[vmem, vmem, vmem],
        out_shape=[
            jax.ShapeDtypeStruct((tokens, cols), jnp.float32),
            jax.ShapeDtypeStruct(own.shape, own.dtype),
            jax.ShapeDtypeStruct(prob.shape, prob.dtype),
        ],
        scratch_shapes=[pltpu.SemaphoreType.DMA((5,))],
        compiler_params=pltpu.CompilerParams(vmem_limit_bytes=VMEM_LIMIT),
        name="project_own",
    )(att, *(pltpu.with_memory_space_constraint(value, pltpu.HBM) for value in (own, prob)))


def project_kernel(
    bound_ref, pos_ref, att_ref, part_ref, own_ref, swap_hbm, gain_ref, read_ref, cot_ref,
    pred_ref, ga_ref, swap_ref, proj_ref, gp_ref, sems,
):
    cols = swap_ref.shape[1]
    chunks = 4
    rows = swap_ref.shape[0] // chunks
    width = cols // chunks
    parts = [pl.ds(k * width, width) for k in range(chunks)]
    copies = [
        pltpu.make_async_copy(swap_hbm.at[:, part], swap_ref.at[:, part], sems.at[k]) for k, part in enumerate(parts)
    ]
    for copy in copies:
        copy.start()
    proj_ref[:, side_cols(pos_ref, 0, cols)] = part_ref[...]
    first = pos_ref[4] * -cols + cols
    for k in range(chunks):
        copies[k].wait()
        lanes = pl.ds(pl.multiple_of(first + k * width, width), width)
        proj_ref[:, lanes] = dot(att_ref[...], swap_ref[:, k * width : (k + 1) * width], ((1,), (0,)))
    inner = proj_ref.shape[1]
    for pair in range(TOK // (2 * BS)):
        rows_of = slice(pair * 2 * BS, (pair + 1) * 2 * BS)
        x = pair * 2 // BY
        y = pair * 2 % BY
        proj = proj_ref[rows_of, :]
        gain = gain_ref[...]
        flag = jnp.where(
            lax.broadcasted_iota(jnp.int32, (2 * BS, 1), 0) < BS, bound_ref[0, x, y], bound_ref[0, x, y + 1]
        ).astype(jnp.float32)
        cot = jnp.concatenate([cot_ref[0, x, y], cot_ref[0, x, y + 1]], axis=0) * flag
        inv_rms = lax.rsqrt(jnp.sum(proj * proj, axis=1, keepdims=True) * (1.0 / inner) + 1e-05)
        normed = proj * inv_rms * gain
        pred0 = jnp.sum(normed * read_ref[0:1, :], axis=1, keepdims=True) * flag
        pred1 = jnp.sum(normed * read_ref[1:2, :], axis=1, keepdims=True) * flag
        pred = jnp.where(lax.broadcasted_iota(jnp.int32, (2 * BS, HS), 1) == 0, pred0, pred1).T
        pred_ref[0, x, y] = pred[:2, :BS]
        pred_ref[0, x, y + 1] = pred[:2, BS:]
        gained = (cot[:, 0:1] * read_ref[0:1, :] + cot[:, 1:2] * read_ref[1:2, :]) * gain
        inner_mean = jnp.sum(gained * proj, axis=1, keepdims=True) * (1.0 / inner)
        gp_ref[rows_of, :] = (inv_rms * gained - proj * (inv_rms * inv_rms * inv_rms * inner_mean)).astype(jnp.bfloat16)
    gp_own = gp_ref[:, side_cols(pos_ref, 0, cols)]
    gp_swap = gp_ref[:, side_cols(pos_ref, 1, cols)]
    for k in range(chunks):
        lanes = slice(k * rows, (k + 1) * rows)
        total = dot(gp_swap, swap_ref[lanes, :], ((1,), (1,))) + dot(gp_own, own_ref[lanes, :], ((1,), (1,)))
        ga_ref[:, lanes] = total.astype(jnp.bfloat16)


def project(boundary, position, att, part, own, swapped, gain, read_rows, cotangent):
    vmem = pl.BlockSpec(memory_space=pltpu.VMEM)
    smem = pl.BlockSpec(memory_space=pltpu.SMEM)
    return pl.pallas_call(
        project_kernel,
        in_specs=[smem, smem, vmem, vmem, vmem, pl.BlockSpec(memory_space=pl.ANY), vmem, vmem, vmem],
        out_specs=[vmem, vmem],
        out_shape=[
            jax.ShapeDtypeStruct(cotangent.shape[:3] + (2, BS), jnp.float32),
            jax.ShapeDtypeStruct(att.shape, jnp.bfloat16),
        ],
        scratch_shapes=[
            pltpu.VMEM(swapped.shape, jnp.bfloat16),
            pltpu.VMEM(att.shape, jnp.float32),
            pltpu.VMEM(att.shape, jnp.bfloat16),
            pltpu.SemaphoreType.DMA((4,)),
        ],
        compiler_params=pltpu.CompilerParams(vmem_limit_bytes=VMEM_LIMIT),
        name="project",
    )(
        boundary,
        position,
        *in_vmem(att, part, own),
        pltpu.with_memory_space_constraint(swapped, pltpu.HBM),
        gain,
        read_rows,
        cotangent,
    )


def kv_rows(refs, which, lanes):
    return jnp.concatenate([ref[which, :, :, :, lanes].reshape(-1, HS) for ref in refs], axis=0)


def back_rim_kernel(q_ref, ga_ref, prob_ref, *rest):
    count = len(PIECES)
    v_refs = rest[:count]
    gs_ref = rest[count]
    rim_refs = rest[count + 1 :]
    for h in range(prob_ref.shape[0]):
        lanes = slice(h * HS, (h + 1) * HS)
        query = q_ref[0, :, :, :, lanes].reshape(TOK, HS)
        values = kv_rows(v_refs, 1, lanes)
        grad_att = ga_ref[:, lanes]
        prob = prob_ref[h]
        grad_prob = dot(values, grad_att, ((1,), (1,)))
        inner_sum = jnp.sum(prob * grad_prob, axis=0, keepdims=True)
        grad_scores = (prob * (grad_prob - inner_sum) * (HS**-0.5)).astype(jnp.bfloat16)
        gs_ref[h] = grad_scores
        half = prob[TOK:].astype(jnp.bfloat16)
        grads = (dot(grad_scores[TOK:], query, ((1,), (0,))), dot(half, grad_att, ((1,), (0,))))
        for which, grad in enumerate(grads):
            start = 0
            for ref in rim_refs:
                shape = ref.shape[1:4]
                rows = shape[0] * shape[1] * shape[2]
                ref[which, :, :, :, lanes] = grad[start : start + rows].reshape(shape + (HS,)).astype(ref.dtype)
                start += rows


def back_rim(queries, grad_att, prob, pieces):
    vmem = pl.BlockSpec(memory_space=pltpu.VMEM)
    shapes = [p.shape for p in pieces]
    return pl.pallas_call(
        back_rim_kernel,
        in_specs=[vmem] * (3 + len(pieces)),
        out_specs=[vmem] * len(pieces),
        out_shape=[jax.ShapeDtypeStruct(prob.shape, jnp.bfloat16)]
        + [jax.ShapeDtypeStruct(s, jnp.bfloat16) for s in shapes[1:]],
        compiler_params=pltpu.CompilerParams(vmem_limit_bytes=VMEM_LIMIT),
        name="back_rim",
    )(*in_vmem(queries, grad_att, prob, *pieces))


def back_own_kernel(q_ref, ga_ref, prob_ref, gs_ref, *rest):
    count = len(PIECES)
    k_refs = rest[:count]
    low_ref, high_ref, gq_ref, out_ref, edge_ref = rest[count:]
    for h in range(prob_ref.shape[0]):
        lanes = slice(h * HS, (h + 1) * HS)
        query = q_ref[0, :, :, :, lanes].reshape(TOK, HS)
        grad_scores = gs_ref[h]
        grad_query = dot(grad_scores, kv_rows(k_refs, 0, lanes), ((0,), (0,)))
        gq_ref[0, :, :, :, lanes] = grad_query.reshape(BX, BY, BS, HS).astype(gq_ref.dtype)
        half = prob_ref[h, :TOK, :].astype(jnp.bfloat16)
        grads = (dot(grad_scores[:TOK], query, ((1,), (0,))), dot(half, ga_ref[:, lanes], ((1,), (0,))))
        for which, grad in enumerate(grads):
            for block, (x, y) in enumerate(LOCAL):
                total = grad[block * BS : (block + 1) * BS]
                if x == 0:
                    total = total + low_ref[which, 0, y, :, lanes].astype(jnp.float32)
                if x == BX - 1:
                    total = total + high_ref[which, 0, y, :, lanes].astype(jnp.float32)
                if y in (0, BY - 1):
                    edge_ref[which, x, y // (BY - 1), :, lanes] = total
                else:
                    out_ref[which, x, y, :, lanes] = total.astype(out_ref.dtype)


def back_own(queries, grad_att, prob, grad_scores, pieces, low, high):
    vmem = pl.BlockSpec(memory_space=pltpu.VMEM)
    own = pieces[0].shape
    edge = own[:2] + (2,) + own[3:]
    return pl.pallas_call(
        back_own_kernel,
        in_specs=[vmem] * (6 + len(pieces)),
        out_specs=[vmem] * 3,
        out_shape=[
            jax.ShapeDtypeStruct(queries.shape, jnp.bfloat16),
            jax.ShapeDtypeStruct(own, jnp.bfloat16),
            jax.ShapeDtypeStruct(edge, jnp.float32),
        ],
        compiler_params=pltpu.CompilerParams(vmem_limit_bytes=VMEM_LIMIT),
        name="back_own",
    )(*in_vmem(queries, grad_att, prob, grad_scores, *pieces, low, high))


def sides_kernel(from_low_ref, from_high_ref, low_ref, high_ref, left_ref, right_ref):
    f32 = jnp.float32
    for y, rim, out in ((0, low_ref, left_ref), (1, high_ref, right_ref)):
        for which in range(2):
            first = rim[which, 0, 0].astype(f32) + from_low_ref[which, 0, y].astype(f32)
            last = rim[which, BX - 1, 0].astype(f32) + from_high_ref[which, 0, y].astype(f32)
            out[which, 0, 0] = first.astype(out.dtype)
            out[which, BX - 1, 0] = last.astype(out.dtype)


def sides(from_low, from_high, low, high):
    vmem = pl.BlockSpec(memory_space=pltpu.VMEM)
    shape = jax.ShapeDtypeStruct(low.shape, low.dtype)
    return pl.pallas_call(
        sides_kernel,
        in_specs=[vmem] * 4,
        out_specs=[vmem, vmem],
        out_shape=[shape, shape],
        compiler_params=pltpu.CompilerParams(vmem_limit_bytes=SMALL_LIMIT),
        name="sides",
    )(*in_vmem(from_low, from_high, low, high))


def add_columns_kernel(low_ref, high_ref, edge_ref, partial_hbm, out_hbm, sum_ref, sems):
    del partial_hbm
    stores = []
    for which in range(2):
        for side, ref in enumerate((low_ref, high_ref)):
            for x in range(BX):
                total = edge_ref[which, x, side] + ref[which, x, 0].astype(jnp.float32)
                sum_ref[which, side, x] = total.astype(sum_ref.dtype)
                y = side * (BY - 1)
                index = (which * 2 + side) * BX + x
                store = pltpu.make_async_copy(sum_ref.at[which, side, x], out_hbm.at[which, x, y], sems.at[index])
                store.start()
                stores.append(store)
    for store in stores:
        store.wait()


def add_columns(edge, low, high, partial):
    vmem = pl.BlockSpec(memory_space=pltpu.VMEM)
    hbm = pl.BlockSpec(memory_space=pltpu.HBM)
    return pl.pallas_call(
        add_columns_kernel,
        in_specs=[vmem, vmem, vmem, hbm],
        out_specs=hbm,
        out_shape=jax.ShapeDtypeStruct(partial.shape, partial.dtype),
        scratch_shapes=[
            pltpu.VMEM((2, 2, BX) + edge.shape[3:], partial.dtype),
            pltpu.SemaphoreType.DMA((4 * BX,)),
        ],
        input_output_aliases={3: 0},
        compiler_params=pltpu.CompilerParams(vmem_limit_bytes=SMALL_LIMIT),
        name="add_columns",
    )(*in_vmem(low, high, edge), pltpu.with_memory_space_constraint(partial, pltpu.HBM))


def swap_cores(value):
    return lax.ppermute(value, "sx", [(i, i ^ 1) for i in range(lax.axis_size("sx"))])


def body(queries, keys_values, out_weight, gain, read_weight, adjacency, boundary, cotangent):
    size_x, size_y = queries.shape[1:3]
    inner = out_weight.shape[1]
    n_sx, n_sy, n_wa = (lax.axis_size(axis) for axis in ("sx", "sy", "wa"))
    row, column, case = (lax.axis_index(axis) for axis in ("sx", "sy", "wa"))
    core = row % 2
    kv = keys_values[:, 0]
    cols = inner // 2
    slab = lax.dynamic_slice_in_dim(out_weight, core * cols, cols, axis=1)
    pairs = [[w, w + 1] for w in range(0, n_wa, 2)]
    rings = [list(range(h, n_wa, 2)) for h in range(2)]
    both = lax.all_gather(slab, "wa", axis=0, axis_index_groups=pairs)
    own_cols = lax.all_gather(both, "wa", axis=0, axis_index_groups=rings).reshape(-1, cols)
    ylow = shift(kv[:, :, size_y - 1 :], "sy", 1)
    yhigh = shift(kv[:, :, :1], "sy", -1)
    xlow = shift(kv[:, size_x - 1 :], "sx", 1)
    xhigh = shift(kv[:, :1], "sx", -1)
    clow = shift(jnp.concatenate([ylow[:, size_x - 1 :], yhigh[:, size_x - 1 :]], axis=2), "sx", 1)
    chigh = shift(jnp.concatenate([ylow[:, :1], yhigh[:, :1]], axis=2), "sx", -1)
    pieces = (kv, xlow, clow, xhigh, chigh, ylow, yhigh)
    position = jnp.stack(
        [
            row * size_x,
            column * size_y,
            jnp.int32(size_x * n_sx),
            jnp.int32(size_y * n_sy),
            core,
        ]
    ).astype(jnp.int32)
    att, prob = forward(adjacency, position, queries, pieces)
    own_cols, att = lax.optimization_barrier((own_cols, att))
    swapped = swap_cores(own_cols)
    part, own_cols, prob = project_own(att, own_cols, prob)
    prediction, grad_att = project(
        boundary, position, att, part, own_cols, swapped, gain[None], read_weight.T, cotangent
    )
    grad_scores, gxlow, gclow, gxhigh, gchigh, gylow, gyhigh = back_rim(queries, grad_att, prob, pieces)
    corner_low = shift(gchigh, "sx", 1)
    corner_high = shift(gclow, "sx", -1)
    from_low = shift(gxhigh, "sx", 1)
    from_high = shift(gxlow, "sx", -1)
    grad_queries, partial, edge = back_own(queries, grad_att, prob, grad_scores, pieces, from_low, from_high)
    to_left, to_right = sides(corner_low, corner_high, gylow, gyhigh)
    left = shift(to_right, "sy", 1)
    right = shift(to_left, "sy", -1)
    grad_kv = add_columns(edge, left, right, partial)
    return (jnp.swapaxes(prediction, 3, 4), grad_queries, grad_kv[:, None])


def solution(mesh):
    return jax.shard_map(
        body,
        mesh=mesh,
        in_specs=(
            P("wa", "sx", "sy", None, None),
            P(None, "wa", "sx", "sy", None, None),
            P("wa", None),
            P(),
            P(),
            P("wa", "sx", "sy", None),
            P("wa", "sx", "sy"),
            P("wa", "sx", "sy", None, None),
        ),
        out_specs=(
            P("wa", "sx", "sy", None, None),
            P("wa", "sx", "sy", None, None),
            P(None, "wa", "sx", "sy", None, None),
        ),
        check_vma=False,
    )
```
